128 devices in a mesh: gx: 16 (over z, y), gy: 8 (over x, core).
Axes of the slice: x: 4, y: 4, z: 4, core: 2. Of those that a mesh axis runs over, the one named last changes fastest.
Arguments:
- centers: float32 [3, 262144], P(None, ('gx', 'gy')), may hold values from -6 to 6
- tilt_angle: float32 [262144], P(('gx', 'gy')), may hold values from -3.140625 to 3.140625
- turn_angle: float32 [262144], P(('gx', 'gy')), may hold values from -3.140625 to 3.140625
- radius: float32 [262144], P(('gx', 'gy')), may hold values from 0.5 to 2
- mobility_perp: float32 [262144], P(('gx', 'gy')), may hold values from 0.3 to 3
- mobility_axial: float32 [262144], P(('gx', 'gy')), may hold values from 0.2 to 2
- mobility_rot: float32 [262144], P(('gx', 'gy')), may hold values from 0.3 to 3
- external_load: float32 [6, 262144], P(None, ('gx', 'gy')), may hold values from -60 to 60
- local_first: int32 [327680], P(('gx', 'gy')), may hold values from 0 to 2047, as said below
- local_second: int32 [327680], P(('gx', 'gy')), may hold values from 0 to 2047
- arc_first: float32 [327680], P(('gx', 'gy')), may hold values from -1 to 1
- arc_second: float32 [327680], P(('gx', 'gy')), may hold values from -1 to 1
- cross_mine: int32 [128, 4, 256], P(('gx', 'gy')), may hold values from 0 to 2047
- cross_slot: int32 [128, 4, 256], P(('gx', 'gy')), may hold values from 0 to 127
- cross_arc_own: float32 [128, 4, 256], P(('gx', 'gy')), may hold values from -1 to 1
- cross_arc_other: float32 [128, 4, 256], P(('gx', 'gy')), may hold values from -1 to 1
- cross_count: int32 [128, 4], P(('gx', 'gy')), may hold values from 0 to 256, as said below
- export_rows: int32 [128, 4, 128], P(('gx', 'gy')), may hold values from 0 to 2047
Outputs:
- velocity: float32 [6, 262144], P(None, ('gx', 'gy'))
- force_local: float32 [327680], P(('gx', 'gy'))
- force_cross: float32 [128, 4, 256], P(('gx', 'gy'))
The draws below stay inside these ranges and needn't reach their ends.
Inputs may be any that keep to these rules, and one draw needn't show every extreme that they name: local_second never equals local_first of the same pair. Slots c < cross_count[k, d] are live, the others dead. A direction whose partner lies outside the mesh has count 0. In every draw some block holds 256 live pairs.
All inputs are finite; a program needn't handle non-finite values.
Results may differ from the reference program's by a relative error of at most 0.00002.
Values sent between devices are 32-bit elements; how exact they have to be, the bound alone decides.
A program may use at most 64 MiB of HBM per device.

```python
import math
import jax
import jax.numpy as jnp
from jax import lax

SEG_DEV = 2048
LOC_DEV = 2560
CAP = 256
EXP = 128
SEGS = 262144
LOCS = 327680
N_GX = 16
N_GY = 8


def pair_indices(key):
    inner = jax.random.fold_in(key, 17)
    left_key, right_key = jax.random.split(inner)
    first = jax.random.randint(left_key, (LOCS,), 0, SEG_DEV, dtype=jnp.int32)
    stride = jax.random.randint(right_key, (LOCS,), 1, SEG_DEV, dtype=jnp.int32)
    return (first, (first + stride) % SEG_DEV)


def draw_local_first(key, part):
    return pair_indices(key)[0]


def draw_local_second(key, part):
    return pair_indices(key)[1]


def draw_cross_count(key, part):
    devices = N_GX * N_GY
    count_key, pick_key = jax.random.split(jax.random.fold_in(key, 29))
    owners = jnp.arange(devices, dtype=jnp.int32)[:, None]
    slab_index = owners // N_GY
    sub_index = owners % N_GY
    heading = jnp.arange(4, dtype=jnp.int32)[None, :]
    counts = jax.random.randint(count_key, (devices, 4), CAP // 4, CAP + 1, dtype=jnp.int32)
    chosen = jax.random.randint(pick_key, (), 0, (N_GX - 1) * N_GY, dtype=jnp.int32)
    counts = jnp.where((owners == chosen) & (heading == 2), CAP, counts)
    upper = slab_index < N_GX - 1
    valid = jnp.where(heading == 0, sub_index < N_GY - 1, jnp.where(heading == 1, upper & (sub_index < N_GY - 1), jnp.where(heading == 2, upper, upper & (sub_index > 0))))
    return jnp.where(valid, counts, 0).astype(jnp.int32)


def draw_external_load(key, part):
    base_key = jax.random.fold_in(jax.random.fold_in(key, 41), 0)
    owner = (jnp.arange(SEGS, dtype=jnp.int32) // SEG_DEV).astype(jnp.float32)
    ramp = 1.0 + 2.0 * owner / max(N_GX * N_GY - 1, 1)
    values = jax.random.normal(base_key, (6, SEGS), jnp.float32)
    return values * ramp[None, :]


def place_ends(values, key, least, top_value):
    longest = values.shape.index(max(values.shape))
    spots = []
    for shift in (0, 1):
        where = [jax.random.randint(jax.random.fold_in(key, axis), (), 0, length) for axis, length in enumerate(values.shape)]
        where[longest] = (where[longest] + shift) % values.shape[longest]
        spots.append(tuple(where))
    return values.at[spots[0]].set(least).at[spots[1]].set(top_value)


def block_scale(own_key, shape, cuts, smallest, largest):
    def one(dim, blocks):
        draws = jax.random.uniform(jax.random.fold_in(jax.random.fold_in(own_key, 6), dim), (blocks,), jnp.float32, smallest / len(cuts), largest / len(cuts))
        return jnp.repeat(jnp.exp(draws), shape[dim] // blocks).reshape((-1,) + (1,) * (len(shape) - dim - 1))

    gain = one(*cuts[0])
    for cut in cuts[1:]:
        gain = gain * one(*cut)
    return gain


def noise(stream_key, dims, scale, bound, shards=(), held_as=jnp.bfloat16):
    level = block_scale(stream_key, dims, shards, -0.22, 0.18) if shards else 1.0
    values = jax.random.normal(stream_key, dims, jnp.float32) * scale * level
    return jnp.minimum(jnp.maximum(values, -bound), bound).astype(held_as)


def setup_inputs(seed: int = 0) -> dict:
    key_of = jax.random.split(jax.random.key(seed), 19)
    return {
        "centers": noise(key_of[0], (3, SEGS), 1.0, 6.0, ((1, 128),), jnp.float32),
        "tilt_angle": jnp.clip(jax.random.uniform(key_of[1], (SEGS,), jnp.float32, -3.140625, 3.140625), -3.140625, 3.140625),
        "turn_angle": jnp.clip(jax.random.uniform(key_of[2], (SEGS,), jnp.float32, -3.140625, 3.140625), -3.140625, 3.140625),
        "radius": jnp.clip(jnp.exp(math.log(2.0) - 1.3862944 * jax.random.uniform(key_of[3], (SEGS,), jnp.float32) ** block_scale(key_of[3], (SEGS,), ((0, 128),), -0.2, 0.2)), 0.5, 2.0),
        "mobility_perp": jnp.clip(jnp.exp(math.log(3.0) - 2.3025851 * jax.random.uniform(key_of[4], (SEGS,), jnp.float32) ** block_scale(key_of[4], (SEGS,), ((0, 128),), -0.2, 0.2)), 0.3, 3.0),
        "mobility_axial": jnp.clip(jnp.exp(math.log(2.0) - 2.3025851 * jax.random.uniform(key_of[5], (SEGS,), jnp.float32) ** block_scale(key_of[5], (SEGS,), ((0, 128),), -0.2, 0.2)), 0.2, 2.0),
        "mobility_rot": jnp.clip(jnp.exp(math.log(3.0) - 2.3025851 * jax.random.uniform(key_of[6], (SEGS,), jnp.float32) ** block_scale(key_of[6], (SEGS,), ((0, 128),), -0.2, 0.2)), 0.3, 3.0),
        "external_load": draw_external_load(jax.random.fold_in(key_of[18], 71), 0),
        "local_first": draw_local_first(jax.random.fold_in(key_of[18], 71), 0),
        "local_second": draw_local_second(jax.random.fold_in(key_of[18], 71), 0),
        "arc_first": jnp.clip(jax.random.uniform(key_of[10], (LOCS,), jnp.float32, -1.0, 1.0) * block_scale(key_of[10], (LOCS,), ((0, 128),), -0.4, 0.0), -1.0, 1.0),
        "arc_second": jnp.clip(jax.random.uniform(key_of[11], (LOCS,), jnp.float32, -1.0, 1.0) * block_scale(key_of[11], (LOCS,), ((0, 128),), -0.4, 0.0), -1.0, 1.0),
        "cross_mine": place_ends(jax.random.randint(key_of[12], (N_GX * N_GY, 4, CAP), 0, SEG_DEV), jax.random.fold_in(key_of[12], 1), 0, SEG_DEV - 1).astype(jnp.int32),
        "cross_slot": place_ends(jax.random.randint(key_of[13], (N_GX * N_GY, 4, CAP), 0, EXP), jax.random.fold_in(key_of[13], 1), 0, EXP - 1).astype(jnp.int32),
        "cross_arc_own": jnp.clip(jax.random.uniform(key_of[14], (N_GX * N_GY, 4, CAP), jnp.float32, -1.0, 1.0) * block_scale(key_of[14], (N_GX * N_GY, 4, CAP), ((0, 128),), -0.4, 0.0), -1.0, 1.0),
        "cross_arc_other": jnp.clip(jax.random.uniform(key_of[15], (N_GX * N_GY, 4, CAP), jnp.float32, -1.0, 1.0) * block_scale(key_of[15], (N_GX * N_GY, 4, CAP), ((0, 128),), -0.4, 0.0), -1.0, 1.0),
        "cross_count": draw_cross_count(jax.random.fold_in(key_of[18], 71), 0),
        "export_rows": place_ends(jax.random.randint(key_of[17], (N_GX * N_GY, 4, EXP), 0, SEG_DEV), jax.random.fold_in(key_of[17], 1), 0, SEG_DEV - 1).astype(jnp.int32),
    }


step_time = 0.5
floor_gap = 0.25
tiny = 1e-06

def tangent_of(polar, azimuth):
    lifted = jnp.sin(polar)
    return jnp.stack([lifted * jnp.cos(azimuth), lifted * jnp.sin(azimuth), jnp.cos(polar)])

def cross_product(left, right):
    return jnp.stack([left[1] * right[2] - left[2] * right[1], left[2] * right[0] - left[0] * right[2], left[0] * right[1] - left[1] * right[0]])

def pair_terms(geo_first, geo_second, arc_one, arc_two, live_mask):
    lever_first = arc_one * tangent_of(geo_first[3], geo_first[4])
    lever_second = arc_two * tangent_of(geo_second[3], geo_second[4])
    apart = geo_first[:3] + lever_first - geo_second[:3] - lever_second
    spacing = jnp.sqrt(lax.optimization_barrier(jnp.sum(apart * apart, axis=0)))
    normal = apart / jnp.maximum(spacing, floor_gap) * live_mask
    jacobian = jnp.concatenate([normal, cross_product(lever_first, normal), cross_product(lever_second, normal)], axis=0)
    clearance = (spacing - geo_first[5] - geo_second[5]) * live_mask
    return (jacobian, clearance)

def rate_of(jacobian, moving_first, moving_second):
    return lax.optimization_barrier(jnp.sum(jacobian[:3] * (moving_first[:3] - moving_second[:3]), axis=0)) + lax.optimization_barrier(jnp.sum(jacobian[3:6] * moving_first[3:], axis=0)) - lax.optimization_barrier(jnp.sum(jacobian[6:] * moving_second[3:], axis=0))

def push_terms(jacobian, amount):
    return (amount * jacobian[:6], -amount * jnp.concatenate([jacobian[:3], jacobian[6:]], axis=0))

def apply_mobility(applied, tangent, perp, axial, rotary):
    force = applied[:3]
    along = lax.optimization_barrier(jnp.sum(tangent * force, axis=0))
    return jnp.concatenate([perp * force + axial * along * tangent, rotary * applied[3:]], axis=0)

def reference(centers, tilt_angle, turn_angle, radius, mobility_perp, mobility_axial, mobility_rot, external_load, local_first, local_second, arc_first, arc_second, cross_mine, cross_slot, cross_arc_own, cross_arc_other, cross_count, export_rows):
    devices = N_GX * N_GY
    owners = jnp.arange(devices, dtype=jnp.int32)
    slab_index = owners // N_GY
    sub_index = owners % N_GY
    step_slab = jnp.array([0, 1, 1, 1], dtype=jnp.int32)
    step_sub = jnp.array([1, 1, 0, -1], dtype=jnp.int32)
    partner = jnp.clip(slab_index[:, None] + step_slab[None, :], 0, N_GX - 1) * N_GY + jnp.clip(sub_index[:, None] + step_sub[None, :], 0, N_GY - 1)
    partner = partner.astype(jnp.int32)
    headings = jnp.arange(4, dtype=jnp.int32)
    remote_rows = export_rows[partner[:, :, None], headings[None, :, None], cross_slot]
    local_base = jnp.arange(LOCS, dtype=jnp.int32) // LOC_DEV * SEG_DEV
    first_all = jnp.concatenate([local_base + local_first, ((owners * SEG_DEV)[:, None, None] + cross_mine).reshape(-1)]).astype(jnp.int32)
    second_all = jnp.concatenate([local_base + local_second, (partner[:, :, None] * SEG_DEV + remote_rows).reshape(-1)]).astype(jnp.int32)
    live_cross = (jnp.arange(CAP, dtype=jnp.int32)[None, None, :] < cross_count[:, :, None]).astype(jnp.float32).reshape(-1)
    live_mask = jnp.concatenate([jnp.ones((LOCS,), jnp.float32), live_cross])
    arc_one = jnp.concatenate([arc_first, cross_arc_own.reshape(-1)])
    arc_two = jnp.concatenate([arc_second, cross_arc_other.reshape(-1)])
    geometry = jnp.concatenate([centers, tilt_angle[None], turn_angle[None], radius[None]], axis=0)
    tangent = tangent_of(tilt_angle, turn_angle)
    jacobian, clearance = pair_terms(geometry[:, first_all], geometry[:, second_all], arc_one, arc_two, live_mask)

    def spread(amount):
        push_first, push_second = push_terms(jacobian, amount)
        loads = jnp.zeros((6, SEGS), jnp.float32)
        return loads.at[:, first_all].add(push_first).at[:, second_all].add(push_second)

    def rates(moving):
        return rate_of(jacobian, moving[:, first_all], moving[:, second_all])

    def mobile(applied):
        return apply_mobility(applied, tangent, mobility_perp, mobility_axial, mobility_rot)
    drift = mobile(external_load)
    slope_first = clearance / step_time + rates(drift)
    curved = rates(mobile(spread(slope_first)))
    step_first = jnp.sum(slope_first * slope_first) / (jnp.sum(slope_first * curved) + tiny)
    thrust = jnp.maximum(0.0, -step_first * slope_first)
    moving_one = drift + mobile(spread(thrust))
    slope_second = clearance / step_time + rates(moving_one)
    step_second = jnp.sum(thrust * thrust) / (jnp.sum(thrust * (slope_second - slope_first)) + tiny)
    force = jnp.maximum(0.0, thrust - step_second * slope_second)
    velocity = drift + mobile(spread(force))
    return (velocity, force[:LOCS], force[LOCS:].reshape(devices, 4, CAP))
```

```python
import functools

import jax
import jax.numpy as jnp
from jax import lax
from jax.experimental import pallas as pl
from jax.experimental.pallas import tpu as pltpu
from jax.sharding import PartitionSpec as P


F32 = jnp.float32
I32 = jnp.int32
STEP_TIME = 0.5
FLOOR_GAP = 0.25
TINY = 1e-06
PARTS = 2
OFFSETS = ((0, 1), (1, 1), (1, 0), (1, -1))
MESH = pl.DeviceIdType.MESH
LOCAL_STARTS = (0, 8, 12)
CHUNKS = (
    [(0, s) for s in range(8)]
    + [(1, s) for s in range(8)]
    + [(2, s) for s in range(4, 8)]
    + [(3, s) for s in range(8)]
    + [(4, s) for s in range(8)]
    + [(5, s) for s in range(4, 8)]
    + [(6, s) for s in range(8)]
    + [(7, s) for s in range(8)]
)
LOCAL_CHUNKS = 40


def cross3(a, b):
    return [a[1] * b[2] - a[2] * b[1], a[2] * b[0] - a[0] * b[2], a[0] * b[1] - a[1] * b[0]]


def dot3(a, b):
    return a[0] * b[0] + a[1] * b[1] + a[2] * b[2]


def lanes_of(table, index):
    return jnp.take_along_axis(table, index, axis=1, mode="promise_in_bounds")


def kernel(
    n_gx,
    n_gy,
    h_cent,
    h_tilt,
    h_turn,
    h_rad,
    h_perp,
    h_axial,
    h_rot,
    h_load,
    h_lf,
    h_ls,
    h_a1,
    h_a2,
    h_mine,
    h_slot,
    h_own,
    h_oth,
    h_count,
    h_exp,
    o_vel,
    o_fl,
    o_fc,
    v_cent,
    v_tilt,
    v_turn,
    v_rad,
    v_perp,
    v_axial,
    v_rot,
    v_load,
    v_lf,
    v_ls,
    v_a1,
    v_a2,
    v_mine,
    v_slot,
    v_own,
    v_oth,
    s_count,
    v_exp,
    w_vel,
    w_fl,
    w_fc,
    t_seg,
    t_move,
    x_seg,
    pk,
    pk_int,
    key_hi,
    key_lo,
    push,
    a_mat,
    o_mat,
    send_s,
    recv_s,
    send_d,
    recv_d,
    send_e,
    recv_e,
    send_f,
    recv_f,
    send_g,
    recv_g,
    sum_a,
    got_a,
    sum_b,
    got_b,
    in_sem,
    out_sem,
    ex_send,
    ex_recv,
    a_send,
    a_recv,
    b_send,
    b_recv,
):
    gx = lax.axis_index("gx")
    gy = lax.axis_index("gy")

    def place(dx, dy):
        return (lax.rem(gx + (dx + n_gx), n_gx), lax.rem(gy + (dy + n_gy), n_gy))

    known = []
    for dx, dy in OFFSETS:
        known += [(dx % n_gx, dy % n_gy), (-dx % n_gx, -dy % n_gy)]
    known += [(0, o) for o in range(1, n_gy)] + [(o, 0) for o in range(1, n_gx)]
    known = list(dict.fromkeys(known))
    barrier = pltpu.get_barrier_semaphore()
    for dx, dy in known:
        pl.semaphore_signal(barrier, inc=1, device_id=place(dx, dy), device_id_type=MESH)

    sources = (h_cent, h_tilt, h_turn, h_rad, h_perp, h_axial, h_rot, h_load, h_lf, h_ls, h_a1, h_a2, h_mine, h_slot, h_own, h_oth, h_count, h_exp)
    targets = (v_cent, v_tilt, v_turn, v_rad, v_perp, v_axial, v_rot, v_load, v_lf, v_ls, v_a1, v_a2, v_mine, v_slot, v_own, v_oth, s_count, v_exp)
    loads_in = {}
    for i in (1, 2, 7, 4, 5, 6, 13, 15, 16, 17, 12, 14, 0, 3, 8, 9, 10, 11):
        loads_in[i] = pltpu.make_async_copy(sources[i], targets[i], in_sem.at[i])
        loads_in[i].start()

    def need(*which):
        for i in which:
            loads_in[i].wait()

    row8 = lax.broadcasted_iota(I32, (8, 128), 0)
    lane8 = lax.broadcasted_iota(I32, (8, 128), 1)
    heading8 = row8 // 2
    zero8 = jnp.zeros((8, 128), F32)

    def spread_rows(ref, row):
        return jnp.broadcast_to(ref[row : row + 1, :], (8, 128))

    need(1, 2)
    lifted = jnp.sin(v_tilt[...])
    tangent = [lifted * jnp.cos(v_turn[...]), lifted * jnp.sin(v_turn[...]), jnp.cos(v_tilt[...])]
    need(7, 4, 5, 6)
    for c in range(6):
        for r in range(16):
            x_seg[c, r : r + 1, :] = v_load[c : c + 1, r * 128 : (r + 1) * 128]

    def mobile(applied):
        along = dot3(tangent, applied)
        pulled = v_axial[...] * along
        return [v_perp[...] * applied[c] + pulled * tangent[c] for c in range(3)] + [
            v_rot[...] * applied[3 + c] for c in range(3)
        ]

    drift = mobile([x_seg[c] for c in range(6)])
    for c in range(3):
        t_seg[c] = tangent[c]
    for c in range(6):
        t_seg[3 + c] = drift[c]

    def unpacked(ref, into, field):
        for d in range(4):
            for h in range(2):
                into[field, 2 * d + h : 2 * d + h + 1, :] = ref[d : d + 1, h * 128 : (h + 1) * 128]
        return into[field]

    need(13, 15, 16)
    for d in range(4):
        for h in range(2):
            piece = slice(h * 128, (h + 1) * 128)
            send_s[d, h : h + 1, :] = v_slot[d : d + 1, piece].astype(F32)
            send_s[d, 2 + h : 3 + h, :] = v_oth[d : d + 1, piece]
    live_own = zero8
    for d in range(4):
        bound = s_count[0, d]
        live_own = jnp.where(
            (heading8 == d) & ((row8 - 2 * d) * 128 + lane8 < bound), 1.0, live_own
        )
    for d in range(4):
        send_s[d, 4:6, :] = live_own[2 * d : 2 * d + 2]

    pl.semaphore_wait(barrier, len(known))

    sent = []

    def remote(src, dst, step, d, to):
        copy = pltpu.make_async_remote_copy(
            src_ref=src,
            dst_ref=dst,
            send_sem=ex_send.at[step, d],
            recv_sem=ex_recv.at[step, d],
            device_id=to,
            device_id_type=MESH,
        )
        copy.start()
        sent.append(copy)
        return copy

    partner = [place(dx, dy) for dx, dy in OFFSETS]
    owner = [place(-dx, -dy) for dx, dy in OFFSETS]
    copies_s = [remote(send_s.at[d], recv_s.at[d], 0, d, partner[d]) for d in range(4)]

    need(0, 3)

    def table_row(c, r):
        if c < 3:
            return jnp.broadcast_to(v_cent[c : c + 1, r * 128 : (r + 1) * 128], (8, 128))
        if c == 3:
            return spread_rows(v_rad, r)
        return jnp.broadcast_to(t_seg[c - 4, r : r + 1, :], (8, 128))

    def move_row(c, r):
        return jnp.broadcast_to(t_move[c, r : r + 1, :], (8, 128))

    def picked(index, row_of, count):
        block = index >> 7
        lane = index & 127
        out = [None] * count
        for r in range(16):
            here = block == r
            for c in range(count):
                taken = lanes_of(row_of(c, r), lane)
                out[c] = taken if r == 0 else jnp.where(here, taken, out[c])
        return out

    def endpoint(values, arc):
        lever = [arc * values[4 + c] for c in range(3)]
        place_of = [values[c] + lever[c] for c in range(3)]
        turned = cross3(values[10:13], lever)
        moving = [values[7 + c] + turned[c] for c in range(3)]
        return dict(lever=lever, at=place_of, radius=values[3], moving=moving)

    need(17)
    exports = v_exp[...]
    offered = picked(jnp.concatenate([exports, exports], axis=0), table_row, 13)
    for d in range(4):
        for c in range(13):
            send_e[d, c : c + 1, :] = offered[c][d : d + 1]
    copies_e = [remote(send_e.at[d], recv_e.at[d], 1, d, owner[d]) for d in range(4)]

    need(12, 14)
    index = [None] * 8
    index[6] = unpacked(v_mine, pk_int, 0)
    arc_own = unpacked(v_own, pk, 1)
    own = endpoint(picked(index[6], table_row, 13), arc_own)
    for i, value in enumerate(own["at"] + [own["radius"]] + own["moving"]):
        for d in range(4):
            send_d[d, 2 * i : 2 * i + 2, :] = value[2 * d : 2 * d + 2]
    copies_d = [remote(send_d.at[d], recv_d.at[d], 2, d, partner[d]) for d in range(4)]

    def pair(one, two, live):
        apart = [one["at"][c] - two["at"][c] for c in range(3)]
        spacing = jnp.sqrt(dot3(apart, apart))
        scale = 1.0 / jnp.maximum(spacing, FLOOR_GAP)
        if live is not None:
            scale = scale * live
        normal = [a * scale for a in apart]
        clearance = spacing - one["radius"] - two["radius"]
        if live is not None:
            clearance = clearance * live
        rate = dot3(normal, [one["moving"][c] - two["moving"][c] for c in range(3)])
        slope = clearance * (1.0 / STEP_TIME) + rate
        return dict(normal=normal, slope=slope, down=jnp.maximum(0.0, -slope))

    def split(value):
        pieces = []
        for _ in range(PARTS):
            piece = value.astype(jnp.bfloat16).astype(F32)
            pieces.append(piece)
            value = value - piece
        return pieces

    def set_keys(e):
        key_hi[e] = (index[e] >> 7) & 7
        key_lo[e] = ((index[e] >> 10) << 7) | (index[e] & 127)

    def set_push(e, first, normal, arm, amounts):
        sign = 1.0 if first else -1.0
        for i, amount in enumerate(amounts):
            scaled = amount * sign
            for c in range(6):
                value = scaled * (normal[c] if c < 3 else arm[c - 3])
                for p, piece in enumerate(split(value)):
                    push[p * 6 * len(amounts) + i * 6 + c, e] = piece

    def set_columns(chunks, start):
        low = lax.broadcasted_iota(I32, (256, 128), 0)
        for n, (e, s) in enumerate(chunks):
            at = (start + n) * 128
            key = jnp.broadcast_to(key_lo[e, s : s + 1, :], (256, 128))
            o_mat[:, at : at + 128] = jnp.where(low == key, 1.0, 0.0).astype(jnp.bfloat16)

    def set_rows(chunks, start, count):
        for n, (e, s) in enumerate(chunks):
            at = (start + n) * 128
            here = row8 == jnp.broadcast_to(key_hi[e, s : s + 1, :], (8, 128))
            for k in range(0, count, 2):
                two = [
                    jnp.where(here, jnp.broadcast_to(push[k + j, e, s : s + 1, :], (8, 128)), 0.0)
                    for j in range(2)
                ]
                a_mat[k * 8 : k * 8 + 16, at : at + 128] = jnp.concatenate(two, axis=0).astype(jnp.bfloat16)

    def summed(start, chunks, count):
        cols = slice(start * 128, (start + chunks) * 128)
        return lax.dot_general(
            a_mat[0 : count * 8, cols],
            o_mat[:, cols],
            (((1,), (1,)), ((), ())),
            preferred_element_type=F32,
        )

    def loads_of(total, groups):
        out = []
        for i in range(groups * 6):
            value = None
            for p in reversed(range(PARTS)):
                at = (p * 6 * groups + i) * 8
                piece = jnp.concatenate(
                    [total[at : at + 8, 0:128], total[at : at + 8, 128:256]], axis=0
                )
                value = piece if value is None else value + piece
            out.append(value)
        return out

    need(8, 9, 10, 11)
    pairs = [None] * 5
    ends = [None] * 8
    for b, start in enumerate(LOCAL_STARTS):
        index[b] = v_lf[start : start + 8, :]
        index[3 + b] = v_ls[start : start + 8, :]
        ends[b] = endpoint(picked(index[b], table_row, 13), v_a1[start : start + 8, :])
        ends[3 + b] = endpoint(picked(index[3 + b], table_row, 13), v_a2[start : start + 8, :])
        pairs[b] = pair(ends[b], ends[3 + b], None)
    ends[6] = own

    def set_ends(b, one, two, amounts):
        if one is not None:
            set_push(one, True, pairs[b]["normal"], cross3(ends[one]["lever"], pairs[b]["normal"]), amounts)
        if two is not None:
            set_push(two, False, pairs[b]["normal"], cross3(ends[two]["lever"], pairs[b]["normal"]), amounts)

    wide = 12 * PARTS
    narrow = 6 * PARTS
    for b in range(3):
        set_keys(b)
        set_keys(3 + b)
        set_ends(b, b, 3 + b, (pairs[b]["slope"], pairs[b]["down"]))
    set_keys(6)
    set_columns(CHUNKS[:48], 0)
    set_rows(CHUNKS[:LOCAL_CHUNKS], 0, wide)
    total = summed(0, LOCAL_CHUNKS, wide)

    for copy in copies_s:
        copy.wait_recv()

    def repacked(ref, field, slot):
        for d in range(4):
            pk[slot, 2 * d : 2 * d + 2, :] = ref[d, 2 * field : 2 * field + 2, :]
        return pk[slot]

    def by_heading(row_of):
        out = row_of(0)
        for d in range(1, 4):
            out = jnp.where(heading8 == d, row_of(d), out)
        return out

    slot_in = repacked(recv_s, 0, 2).astype(I32)
    arc_in = repacked(recv_s, 1, 3)
    live_in = repacked(recv_s, 2, 4)
    index[7] = lanes_of(by_heading(lambda d: spread_rows(v_exp, d)), slot_in)
    ends[7] = endpoint(picked(index[7], table_row, 13), arc_in)
    set_keys(7)
    set_columns(CHUNKS[48:], 48)

    slot_own = unpacked(v_slot, pk_int, 1)
    arc_oth = unpacked(v_oth, pk, 6)
    for copy in copies_e:
        copy.wait_recv()
    far = [
        lanes_of(
            by_heading(lambda d, c=c: jnp.broadcast_to(recv_e[d, c : c + 1, :], (8, 128))), slot_own
        )
        for c in range(13)
    ]
    pairs[3] = pair(own, endpoint(far, arc_oth), live_own)
    set_ends(3, 6, None, (pairs[3]["slope"], pairs[3]["down"]))
    for copy in copies_d:
        copy.wait_recv()
    near = [repacked(recv_d, i, 7 + i) for i in range(7)]
    pairs[4] = pair(dict(at=near[0:3], radius=near[3], moving=near[4:7]), ends[7], live_in)
    set_ends(4, None, 7, (pairs[4]["slope"], pairs[4]["down"]))

    set_rows(CHUNKS[LOCAL_CHUNKS:], LOCAL_CHUNKS, wide)
    total = total + summed(LOCAL_CHUNKS, len(CHUNKS) - LOCAL_CHUNKS, wide)
    both = loads_of(total, 2)
    moved_all = mobile(both[0:6])
    moved_down = mobile(both[6:12])
    for c in range(6):
        t_move[c] = moved_down[c]

    def folded(value):
        return jnp.sum(value, axis=0, keepdims=True)

    def halved(row):
        row = row + pltpu.roll(row, 64, 1)
        return row + pltpu.roll(row, 32, 1)

    def counted(name):
        value = pairs[0][name] * pairs[0][name] + pairs[1][name] * pairs[1][name]
        last = pairs[2][name] * pairs[2][name]
        return value + jnp.where(row8 >= 4, last, 0.0) + pairs[3][name] * pairs[3][name]

    def power(one, two):
        value = one[0] * two[0]
        for c in range(1, 6):
            value = value + one[c] * two[c]
        return value

    rows = [
        halved(folded(v))
        for v in (counted("slope"), power(both[0:6], moved_all), counted("down"), power(both[6:12], moved_down))
    ]
    quarter = lax.broadcasted_iota(I32, (1, 128), 1) // 32
    mine = rows[0]
    for i in range(1, 4):
        mine = jnp.where(quarter == i, rows[i], mine)
    sum_a[...] = mine

    def ring(src, dst, send, recv, o, to):
        copy = pltpu.make_async_remote_copy(
            src_ref=src,
            dst_ref=dst.at[o - 1],
            send_sem=send.at[o - 1],
            recv_sem=recv.at[o - 1],
            device_id=to,
            device_id_type=MESH,
        )
        copy.start()
        sent.append(copy)
        return copy

    copies_a = [ring(sum_a, got_a, a_send, a_recv, o, place(0, o)) for o in range(1, n_gy)]

    def contact(e):
        values = picked(index[e], move_row, 6)
        turned = cross3(values[3:6], ends[e]["lever"])
        return [values[c] + turned[c] for c in range(3)]

    moved_own = contact(6)
    for c in range(3):
        for d in range(4):
            send_f[d, 2 * c : 2 * c + 2, :] = moved_own[c][2 * d : 2 * d + 2]
    copies_f = [remote(send_f.at[d], recv_f.at[d], 3, d, partner[d]) for d in range(4)]
    moved_in = contact(7)
    for c in range(3):
        for d in range(4):
            send_g[d, 2 * c : 2 * c + 2, :] = moved_in[c][2 * d : 2 * d + 2]
    copies_g = [remote(send_g.at[d], recv_g.at[d], 4, d, owner[d]) for d in range(4)]

    for copy in copies_a:
        copy.wait_recv()
    mine = sum_a[...]
    for o in range(1, n_gy):
        mine = mine + got_a[o - 1]
    sum_b[...] = mine
    copies_b = [ring(sum_b, got_b, b_send, b_recv, o, place(o, 0)) for o in range(1, n_gx)]

    def curve(b, one, two):
        return dot3(pairs[b]["normal"], [one[c] - two[c] for c in range(3)])

    curved = [None] * 5
    for b in range(3):
        curved[b] = curve(b, contact(b), contact(3 + b))
    for copy in copies_f + copies_g:
        copy.wait_recv()
    curved[3] = curve(3, moved_own, [repacked(recv_g, c, c) for c in range(3)])
    curved[4] = curve(4, [repacked(recv_f, c, 3 + c) for c in range(3)], moved_in)

    for copy in copies_b:
        copy.wait_recv()
    mine = sum_b[...]
    for o in range(1, n_gx):
        mine = mine + got_b[o - 1]
    sums = [
        jnp.sum(jnp.where(quarter == i, mine, 0.0), axis=1, keepdims=True) for i in range(4)
    ]
    step_first = sums[0] / (sums[1] + TINY)
    square = step_first * step_first
    step_second = (square * sums[2]) / (square * sums[3] + TINY)
    step_first = jnp.broadcast_to(step_first, (8, 128))
    step_second = jnp.broadcast_to(step_second, (8, 128))

    force = []
    for b in range(5):
        thrust = step_first * pairs[b]["down"]
        slope = pairs[b]["slope"] + step_first * curved[b]
        force.append(jnp.maximum(0.0, thrust - step_second * slope))
    for b, start in enumerate(LOCAL_STARTS):
        w_fl[start : start + 8, :] = force[b]
    for d in range(4):
        for h in range(2):
            w_fc[d : d + 1, h * 128 : (h + 1) * 128] = force[3][2 * d + h : 2 * d + h + 1]
    out_fl = pltpu.make_async_copy(w_fl, o_fl, out_sem.at[0])
    out_fl.start()
    out_fc = pltpu.make_async_copy(w_fc, o_fc, out_sem.at[1])
    out_fc.start()
    for b in range(3):
        set_ends(b, b, 3 + b, (force[b],))
    set_ends(3, 6, None, (force[3],))
    set_ends(4, None, 7, (force[4],))
    set_rows(CHUNKS, 0, narrow)
    moved = mobile(loads_of(summed(0, len(CHUNKS), narrow), 1))
    for c in range(6):
        velocity = t_seg[3 + c] + moved[c]
        for r in range(16):
            w_vel[c : c + 1, r * 128 : (r + 1) * 128] = velocity[r : r + 1]
    out_vel = pltpu.make_async_copy(w_vel, o_vel, out_sem.at[2])
    out_vel.start()
    for copy in sent:
        copy.wait_send()
    out_fl.wait()
    out_fc.wait()
    out_vel.wait()


def on_device(n_gx, n_gy, cent, tilt, turn, rad, perp, axial, rot, load, lf, ls, a1, a2, mine, slot, own, oth, count, exports):
    segs = [v.reshape(16, 128) for v in (tilt, turn, rad, perp, axial, rot)]
    local = [v.reshape(20, 128) for v in (lf, ls, a1, a2)]
    cross = [v.reshape(4, 256) for v in (mine, slot, own, oth)]
    operands = [cent, *segs, load, *local, *cross, count, exports.reshape(4, 128)]
    anyspace = pl.BlockSpec(memory_space=pl.ANY)

    def held(v):
        return pltpu.VMEM(v.shape, v.dtype)

    inputs = [held(v) for v in operands]
    inputs[16] = pltpu.SMEM(count.shape, count.dtype)
    dma = pltpu.SemaphoreType.DMA
    scratch = inputs + [
        pltpu.VMEM((6, 2048), F32),
        pltpu.VMEM((20, 128), F32),
        pltpu.VMEM((4, 256), F32),
        pltpu.VMEM((9, 16, 128), F32),
        pltpu.VMEM((6, 16, 128), F32),
        pltpu.VMEM((6, 16, 128), F32),
        pltpu.VMEM((14, 8, 128), F32),
        pltpu.VMEM((2, 8, 128), I32),
        pltpu.VMEM((8, 8, 128), I32),
        pltpu.VMEM((8, 8, 128), I32),
        pltpu.VMEM((12 * PARTS, 8, 8, 128), F32),
        pltpu.VMEM((96 * PARTS, 128 * len(CHUNKS)), jnp.bfloat16),
        pltpu.VMEM((256, 128 * len(CHUNKS)), jnp.bfloat16),
        pltpu.VMEM((4, 8, 128), F32),
        pltpu.VMEM((4, 8, 128), F32),
        pltpu.VMEM((4, 16, 128), F32),
        pltpu.VMEM((4, 16, 128), F32),
        pltpu.VMEM((4, 16, 128), F32),
        pltpu.VMEM((4, 16, 128), F32),
        pltpu.VMEM((4, 8, 128), F32),
        pltpu.VMEM((4, 8, 128), F32),
        pltpu.VMEM((4, 8, 128), F32),
        pltpu.VMEM((4, 8, 128), F32),
        pltpu.VMEM((1, 128), F32),
        pltpu.VMEM((n_gy - 1, 1, 128), F32),
        pltpu.VMEM((1, 128), F32),
        pltpu.VMEM((n_gx - 1, 1, 128), F32),
        dma((18,)),
        dma((3,)),
        dma((5, 4)),
        dma((5, 4)),
        dma((n_gy - 1,)),
        dma((n_gy - 1,)),
        dma((n_gx - 1,)),
        dma((n_gx - 1,)),
    ]
    velocity, force_local, force_cross = pl.pallas_call(
        functools.partial(kernel, n_gx, n_gy),
        out_shape=(
            jax.ShapeDtypeStruct((6, 2048), F32),
            jax.ShapeDtypeStruct((20, 128), F32),
            jax.ShapeDtypeStruct((4, 256), F32),
        ),
        in_specs=[anyspace] * 18,
        out_specs=(anyspace,) * 3,
        scratch_shapes=scratch,
        compiler_params=pltpu.CompilerParams(
            collective_id=0, has_side_effects=True, vmem_limit_bytes=48 * 1024 * 1024
        ),
    )(*operands)
    return velocity, force_local.reshape(2560), force_cross.reshape(1, 4, 256)


def solution(mesh):
    both = ("gx", "gy")
    flat = P(both)
    wide = P(None, both)
    cube = P(both, None, None)
    return jax.shard_map(
        functools.partial(on_device, mesh.shape["gx"], mesh.shape["gy"]),
        mesh=mesh,
        in_specs=(wide, *[flat] * 6, wide, *[flat] * 4, *[cube] * 4, P(both, None), cube),
        out_specs=(wide, flat, cube),
        check_vma=False,
    )
```

```python
import functools

import jax
import jax.numpy as jnp
from jax import lax
from jax.experimental import pallas as pl
from jax.experimental.pallas import tpu as pltpu
from jax.sharding import PartitionSpec as P


F32 = jnp.float32
I32 = jnp.int32
STEP_TIME = 0.5
FLOOR_GAP = 0.25
TINY = 1e-06
PARTS = 2
OFFSETS = ((0, 1), (1, 1), (1, 0), (1, -1))
MESH = pl.DeviceIdType.MESH
LOCAL_STARTS = (0, 8, 12)
CHUNKS = (
    [(0, s) for s in range(8)]
    + [(1, s) for s in range(8)]
    + [(2, s) for s in range(4, 8)]
    + [(3, s) for s in range(8)]
    + [(4, s) for s in range(8)]
    + [(5, s) for s in range(4, 8)]
    + [(6, s) for s in range(8)]
    + [(7, s) for s in range(8)]
)
LOCAL_CHUNKS = 40


def cross3(a, b):
    return [a[1] * b[2] - a[2] * b[1], a[2] * b[0] - a[0] * b[2], a[0] * b[1] - a[1] * b[0]]


def dot3(a, b):
    return a[0] * b[0] + a[1] * b[1] + a[2] * b[2]


def lanes_of(table, index):
    return jnp.take_along_axis(table, index, axis=1, mode="promise_in_bounds")


def kernel(
    n_gx,
    n_gy,
    h_cent,
    h_tilt,
    h_turn,
    h_rad,
    h_perp,
    h_axial,
    h_rot,
    h_load,
    h_lf,
    h_ls,
    h_a1,
    h_a2,
    h_mine,
    h_slot,
    h_own,
    h_oth,
    h_count,
    h_exp,
    o_vel,
    o_fl,
    o_fc,
    v_cent,
    v_tilt,
    v_turn,
    v_rad,
    v_perp,
    v_axial,
    v_rot,
    v_load,
    v_lf,
    v_ls,
    v_a1,
    v_a2,
    v_mine,
    v_slot,
    v_own,
    v_oth,
    s_count,
    v_exp,
    w_vel,
    w_fl,
    w_fc,
    t_seg,
    t_move,
    x_seg,
    pk,
    pk_int,
    key_hi,
    key_lo,
    push,
    a_mat,
    o_mat,
    send_s,
    recv_s,
    send_d,
    recv_d,
    send_e,
    recv_e,
    send_f,
    recv_f,
    send_g,
    recv_g,
    sum_a,
    got_a,
    sum_b,
    got_b,
    in_sem,
    out_sem,
    ex_send,
    ex_recv,
    a_send,
    a_recv,
    b_send,
    b_recv,
):
    gx = lax.axis_index("gx")
    gy = lax.axis_index("gy")

    def place(dx, dy):
        return (lax.rem(gx + (dx + n_gx), n_gx), lax.rem(gy + (dy + n_gy), n_gy))

    known = []
    for dx, dy in OFFSETS:
        known += [(dx % n_gx, dy % n_gy), (-dx % n_gx, -dy % n_gy)]
    known += [(0, o) for o in range(1, n_gy)] + [(o, 0) for o in range(1, n_gx)]
    known = list(dict.fromkeys(known))
    barrier = pltpu.get_barrier_semaphore()
    for dx, dy in known:
        pl.semaphore_signal(barrier, inc=1, device_id=place(dx, dy), device_id_type=MESH)

    sources = (h_cent, h_tilt, h_turn, h_rad, h_perp, h_axial, h_rot, h_load, h_lf, h_ls, h_a1, h_a2, h_mine, h_slot, h_own, h_oth, h_count, h_exp)
    targets = (v_cent, v_tilt, v_turn, v_rad, v_perp, v_axial, v_rot, v_load, v_lf, v_ls, v_a1, v_a2, v_mine, v_slot, v_own, v_oth, s_count, v_exp)
    loads_in = {}
    for i in (1, 2, 7, 4, 5, 6, 13, 15, 16, 17, 12, 14, 0, 3, 8, 9, 10, 11):
        loads_in[i] = pltpu.make_async_copy(sources[i], targets[i], in_sem.at[i])
        loads_in[i].start()

    def need(*which):
        for i in which:
            loads_in[i].wait()

    row8 = lax.broadcasted_iota(I32, (8, 128), 0)
    lane8 = lax.broadcasted_iota(I32, (8, 128), 1)
    heading8 = row8 // 2
    zero8 = jnp.zeros((8, 128), F32)

    def spread_rows(ref, row):
        return jnp.broadcast_to(ref[row : row + 1, :], (8, 128))

    need(1, 2)
    lifted = jnp.sin(v_tilt[...])
    tangent = [lifted * jnp.cos(v_turn[...]), lifted * jnp.sin(v_turn[...]), jnp.cos(v_tilt[...])]
    need(7, 4, 5, 6)
    for c in range(6):
        for r in range(16):
            x_seg[c, r : r + 1, :] = v_load[c : c + 1, r * 128 : (r + 1) * 128]

    def mobile(applied):
        along = dot3(tangent, applied)
        pulled = v_axial[...] * along
        return [v_perp[...] * applied[c] + pulled * tangent[c] for c in range(3)] + [
            v_rot[...] * applied[3 + c] for c in range(3)
        ]

    drift = mobile([x_seg[c] for c in range(6)])
    for c in range(3):
        t_seg[c] = tangent[c]
    for c in range(6):
        t_seg[3 + c] = drift[c]

    def unpacked(ref, into, field):
        for d in range(4):
            for h in range(2):
                into[field, 2 * d + h : 2 * d + h + 1, :] = ref[d : d + 1, h * 128 : (h + 1) * 128]
        return into[field]

    need(13, 15, 16)
    for d in range(4):
        for h in range(2):
            piece = slice(h * 128, (h + 1) * 128)
            send_s[d, h : h + 1, :] = v_slot[d : d + 1, piece].astype(F32)
            send_s[d, 2 + h : 3 + h, :] = v_oth[d : d + 1, piece]
    live_own = zero8
    for d in range(4):
        bound = s_count[0, d]
        live_own = jnp.where(
            (heading8 == d) & ((row8 - 2 * d) * 128 + lane8 < bound), 1.0, live_own
        )
    for d in range(4):
        send_s[d, 4:6, :] = live_own[2 * d : 2 * d + 2]

    pl.semaphore_wait(barrier, len(known))

    sent = []

    def remote(src, dst, step, d, to):
        copy = pltpu.make_async_remote_copy(
            src_ref=src,
            dst_ref=dst,
            send_sem=ex_send.at[step, d],
            recv_sem=ex_recv.at[step, d],
            device_id=to,
            device_id_type=MESH,
        )
        copy.start()
        sent.append(copy)
        return copy

    partner = [place(dx, dy) for dx, dy in OFFSETS]
    owner = [place(-dx, -dy) for dx, dy in OFFSETS]
    copies_s = [remote(send_s.at[d], recv_s.at[d], 0, d, partner[d]) for d in range(4)]

    need(0, 3)

    def table_row(c, r):
        if c < 3:
            return jnp.broadcast_to(v_cent[c : c + 1, r * 128 : (r + 1) * 128], (8, 128))
        if c == 3:
            return spread_rows(v_rad, r)
        return jnp.broadcast_to(t_seg[c - 4, r : r + 1, :], (8, 128))

    def move_row(c, r):
        return jnp.broadcast_to(t_move[c, r : r + 1, :], (8, 128))

    def picked(index, row_of, count):
        block = index >> 7
        lane = index & 127
        out = [None] * count
        for r in range(16):
            here = block == r
            for c in range(count):
                taken = lanes_of(row_of(c, r), lane)
                out[c] = taken if r == 0 else jnp.where(here, taken, out[c])
        return out

    def endpoint(values, arc):
        lever = [arc * values[4 + c] for c in range(3)]
        place_of = [values[c] + lever[c] for c in range(3)]
        turned = cross3(values[10:13], lever)
        moving = [values[7 + c] + turned[c] for c in range(3)]
        return dict(lever=lever, at=place_of, radius=values[3], moving=moving)

    need(17)
    exports = v_exp[...]
    offered = picked(jnp.concatenate([exports, exports], axis=0), table_row, 13)
    for d in range(4):
        for c in range(13):
            send_e[d, c : c + 1, :] = offered[c][d : d + 1]
    copies_e = [remote(send_e.at[d], recv_e.at[d], 1, d, owner[d]) for d in range(4)]

    need(12, 14)
    index = [None] * 8
    index[6] = unpacked(v_mine, pk_int, 0)
    arc_own = unpacked(v_own, pk, 1)
    own = endpoint(picked(index[6], table_row, 13), arc_own)
    for i, value in enumerate(own["at"] + [own["radius"]] + own["moving"]):
        for d in range(4):
            send_d[d, 2 * i : 2 * i + 2, :] = value[2 * d : 2 * d + 2]
    copies_d = [remote(send_d.at[d], recv_d.at[d], 2, d, partner[d]) for d in range(4)]

    def pair(one, two, live):
        apart = [one["at"][c] - two["at"][c] for c in range(3)]
        spacing = jnp.sqrt(dot3(apart, apart))
        scale = 1.0 / jnp.maximum(spacing, FLOOR_GAP)
        if live is not None:
            scale = scale * live
        normal = [a * scale for a in apart]
        clearance = spacing - one["radius"] - two["radius"]
        if live is not None:
            clearance = clearance * live
        rate = dot3(normal, [one["moving"][c] - two["moving"][c] for c in range(3)])
        slope = clearance * (1.0 / STEP_TIME) + rate
        return dict(normal=normal, slope=slope, down=jnp.maximum(0.0, -slope))

    def split(value):
        pieces = []
        for _ in range(PARTS):
            piece = value.astype(jnp.bfloat16).astype(F32)
            pieces.append(piece)
            value = value - piece
        return pieces

    def set_keys(e):
        key_hi[e] = (index[e] >> 7) & 7
        key_lo[e] = ((index[e] >> 10) << 7) | (index[e] & 127)

    def set_push(e, first, normal, arm, amounts):
        sign = 1.0 if first else -1.0
        for i, amount in enumerate(amounts):
            scaled = amount * sign
            for c in range(6):
                value = scaled * (normal[c] if c < 3 else arm[c - 3])
                for p, piece in enumerate(split(value)):
                    push[p * 6 * len(amounts) + i * 6 + c, e] = piece

    def set_columns(chunks, start):
        low = lax.broadcasted_iota(I32, (256, 128), 0)
        for n, (e, s) in enumerate(chunks):
            at = (start + n) * 128
            key = jnp.broadcast_to(key_lo[e, s : s + 1, :], (256, 128))
            o_mat[:, at : at + 128] = jnp.where(low == key, 1.0, 0.0).astype(jnp.bfloat16)

    def set_rows(chunks, start, count):
        for n, (e, s) in enumerate(chunks):
            at = (start + n) * 128
            here = row8 == jnp.broadcast_to(key_hi[e, s : s + 1, :], (8, 128))
            for k in range(0, count, 2):
                two = [
                    jnp.where(here, jnp.broadcast_to(push[k + j, e, s : s + 1, :], (8, 128)), 0.0)
                    for j in range(2)
                ]
                a_mat[k * 8 : k * 8 + 16, at : at + 128] = jnp.concatenate(two, axis=0).astype(jnp.bfloat16)

    def summed(start, chunks, count):
        cols = slice(start * 128, (start + chunks) * 128)
        return lax.dot_general(
            a_mat[0 : count * 8, cols],
            o_mat[:, cols],
            (((1,), (1,)), ((), ())),
            preferred_element_type=F32,
        )

    def loads_of(total, groups):
        out = []
        for i in range(groups * 6):
            value = None
            for p in reversed(range(PARTS)):
                at = (p * 6 * groups + i) * 8
                piece = jnp.concatenate(
                    [total[at : at + 8, 0:128], total[at : at + 8, 128:256]], axis=0
                )
                value = piece if value is None else value + piece
            out.append(value)
        return out

    need(8, 9, 10, 11)
    pairs = [None] * 5
    ends = [None] * 8
    for b, start in enumerate(LOCAL_STARTS):
        index[b] = v_lf[start : start + 8, :]
        index[3 + b] = v_ls[start : start + 8, :]
        ends[b] = endpoint(picked(index[b], table_row, 13), v_a1[start : start + 8, :])
        ends[3 + b] = endpoint(picked(index[3 + b], table_row, 13), v_a2[start : start + 8, :])
        pairs[b] = pair(ends[b], ends[3 + b], None)
    ends[6] = own

    def set_ends(b, one, two, amounts):
        if one is not None:
            set_push(one, True, pairs[b]["normal"], cross3(ends[one]["lever"], pairs[b]["normal"]), amounts)
        if two is not None:
            set_push(two, False, pairs[b]["normal"], cross3(ends[two]["lever"], pairs[b]["normal"]), amounts)

    wide = 12 * PARTS
    narrow = 6 * PARTS
    for b in range(3):
        set_keys(b)
        set_keys(3 + b)
        set_ends(b, b, 3 + b, (pairs[b]["slope"], pairs[b]["down"]))
    set_keys(6)
    set_columns(CHUNKS[:48], 0)
    set_rows(CHUNKS[:LOCAL_CHUNKS], 0, wide)
    total = summed(0, LOCAL_CHUNKS, wide)

    for copy in copies_s:
        copy.wait_recv()

    def repacked(ref, field, slot):
        for d in range(4):
            pk[slot, 2 * d : 2 * d + 2, :] = ref[d, 2 * field : 2 * field + 2, :]
        return pk[slot]

    def by_heading(row_of):
        out = row_of(0)
        for d in range(1, 4):
            out = jnp.where(heading8 == d, row_of(d), out)
        return out

    slot_in = repacked(recv_s, 0, 2).astype(I32)
    arc_in = repacked(recv_s, 1, 3)
    live_in = repacked(recv_s, 2, 4)
    index[7] = lanes_of(by_heading(lambda d: spread_rows(v_exp, d)), slot_in)
    ends[7] = endpoint(picked(index[7], table_row, 13), arc_in)
    set_keys(7)
    set_columns(CHUNKS[48:], 48)

    slot_own = unpacked(v_slot, pk_int, 1)
    arc_oth = unpacked(v_oth, pk, 6)
    for copy in copies_e:
        copy.wait_recv()
    far = [
        lanes_of(
            by_heading(lambda d, c=c: jnp.broadcast_to(recv_e[d, c : c + 1, :], (8, 128))), slot_own
        )
        for c in range(13)
    ]
    pairs[3] = pair(own, endpoint(far, arc_oth), live_own)
    set_ends(3, 6, None, (pairs[3]["slope"], pairs[3]["down"]))
    for copy in copies_d:
        copy.wait_recv()
    near = [repacked(recv_d, i, 7 + i) for i in range(7)]
    pairs[4] = pair(dict(at=near[0:3], radius=near[3], moving=near[4:7]), ends[7], live_in)
    set_ends(4, None, 7, (pairs[4]["slope"], pairs[4]["down"]))

    set_rows(CHUNKS[LOCAL_CHUNKS:], LOCAL_CHUNKS, wide)
    total = total + summed(LOCAL_CHUNKS, len(CHUNKS) - LOCAL_CHUNKS, wide)
    both = loads_of(total, 2)
    moved_all = mobile(both[0:6])
    moved_down = mobile(both[6:12])
    for c in range(6):
        t_move[c] = moved_down[c]

    def folded(value):
        return jnp.sum(value, axis=0, keepdims=True)

    def halved(row):
        row = row + pltpu.roll(row, 64, 1)
        return row + pltpu.roll(row, 32, 1)

    def counted(name):
        value = pairs[0][name] * pairs[0][name] + pairs[1][name] * pairs[1][name]
        last = pairs[2][name] * pairs[2][name]
        return value + jnp.where(row8 >= 4, last, 0.0) + pairs[3][name] * pairs[3][name]

    def power(one, two):
        value = one[0] * two[0]
        for c in range(1, 6):
            value = value + one[c] * two[c]
        return value

    rows = [
        halved(folded(v))
        for v in (counted("slope"), power(both[0:6], moved_all), counted("down"), power(both[6:12], moved_down))
    ]
    quarter = lax.broadcasted_iota(I32, (1, 128), 1) // 32
    mine = rows[0]
    for i in range(1, 4):
        mine = jnp.where(quarter == i, rows[i], mine)
    sum_a[...] = mine

    def ring(src, dst, send, recv, o, to):
        copy = pltpu.make_async_remote_copy(
            src_ref=src,
            dst_ref=dst.at[o - 1],
            send_sem=send.at[o - 1],
            recv_sem=recv.at[o - 1],
            device_id=to,
            device_id_type=MESH,
        )
        copy.start()
        sent.append(copy)
        return copy

    copies_a = [ring(sum_a, got_a, a_send, a_recv, o, place(0, o)) for o in range(1, n_gy)]

    def contact(e):
        values = picked(index[e], move_row, 6)
        turned = cross3(values[3:6], ends[e]["lever"])
        return [values[c] + turned[c] for c in range(3)]

    moved_own = contact(6)
    for c in range(3):
        for d in range(4):
            send_f[d, 2 * c : 2 * c + 2, :] = moved_own[c][2 * d : 2 * d + 2]
    copies_f = [remote(send_f.at[d], recv_f.at[d], 3, d, partner[d]) for d in range(4)]
    moved_in = contact(7)
    for c in range(3):
        for d in range(4):
            send_g[d, 2 * c : 2 * c + 2, :] = moved_in[c][2 * d : 2 * d + 2]
    copies_g = [remote(send_g.at[d], recv_g.at[d], 4, d, owner[d]) for d in range(4)]

    for copy in copies_a:
        copy.wait_recv()
    mine = sum_a[...]
    for o in range(1, n_gy):
        mine = mine + got_a[o - 1]
    sum_b[...] = mine
    copies_b = [ring(sum_b, got_b, b_send, b_recv, o, place(o, 0)) for o in range(1, n_gx)]

    def curve(b, one, two):
        return dot3(pairs[b]["normal"], [one[c] - two[c] for c in range(3)])

    curved = [None] * 5
    for b in range(3):
        curved[b] = curve(b, contact(b), contact(3 + b))
    for copy in copies_f + copies_g:
        copy.wait_recv()
    curved[3] = curve(3, moved_own, [repacked(recv_g, c, c) for c in range(3)])
    curved[4] = curve(4, [repacked(recv_f, c, 3 + c) for c in range(3)], moved_in)

    for copy in copies_b:
        copy.wait_recv()
    mine = sum_b[...]
    for o in range(1, n_gx):
        mine = mine + got_b[o - 1]
    sums = [
        jnp.sum(jnp.where(quarter == i, mine, 0.0), axis=1, keepdims=True) for i in range(4)
    ]
    step_first = sums[0] / (sums[1] + TINY)
    square = step_first * step_first
    step_second = (square * sums[2]) / (square * sums[3] + TINY)
    step_first = jnp.broadcast_to(step_first, (8, 128))
    step_second = jnp.broadcast_to(step_second, (8, 128))

    force = []
    for b in range(5):
        thrust = step_first * pairs[b]["down"]
        slope = pairs[b]["slope"] + step_first * curved[b]
        force.append(jnp.maximum(0.0, thrust - step_second * slope))
    for b, start in enumerate(LOCAL_STARTS):
        w_fl[start : start + 8, :] = force[b]
    for d in range(4):
        for h in range(2):
            w_fc[d : d + 1, h * 128 : (h + 1) * 128] = force[3][2 * d + h : 2 * d + h + 1]
    out_fl = pltpu.make_async_copy(w_fl, o_fl, out_sem.at[0])
    out_fl.start()
    out_fc = pltpu.make_async_copy(w_fc, o_fc, out_sem.at[1])
    out_fc.start()
    for b in range(3):
        set_ends(b, b, 3 + b, (force[b],))
    set_ends(3, 6, None, (force[3],))
    set_ends(4, None, 7, (force[4],))
    set_rows(CHUNKS, 0, narrow)
    moved = mobile(loads_of(summed(0, len(CHUNKS), narrow), 1))
    for c in range(6):
        velocity = t_seg[3 + c] + moved[c]
        for r in range(16):
            w_vel[c : c + 1, r * 128 : (r + 1) * 128] = velocity[r : r + 1]
    out_vel = pltpu.make_async_copy(w_vel, o_vel, out_sem.at[2])
    out_vel.start()
    for copy in sent:
        copy.wait_send()
    out_fl.wait()
    out_fc.wait()
    out_vel.wait()


def on_device(n_gx, n_gy, cent, tilt, turn, rad, perp, axial, rot, load, lf, ls, a1, a2, mine, slot, own, oth, count, exports):
    segs = [v.reshape(16, 128) for v in (tilt, turn, rad, perp, axial, rot)]
    local = [v.reshape(20, 128) for v in (lf, ls, a1, a2)]
    cross = [v.reshape(4, 256) for v in (mine, slot, own, oth)]
    operands = [cent, *segs, load, *local, *cross, count, exports.reshape(4, 128)]
    anyspace = pl.BlockSpec(memory_space=pltpu.HBM)

    def held(v):
        return pltpu.VMEM(v.shape, v.dtype)

    inputs = [held(v) for v in operands]
    inputs[16] = pltpu.SMEM(count.shape, count.dtype)
    dma = pltpu.SemaphoreType.DMA
    scratch = inputs + [
        pltpu.VMEM((6, 2048), F32),
        pltpu.VMEM((20, 128), F32),
        pltpu.VMEM((4, 256), F32),
        pltpu.VMEM((9, 16, 128), F32),
        pltpu.VMEM((6, 16, 128), F32),
        pltpu.VMEM((6, 16, 128), F32),
        pltpu.VMEM((14, 8, 128), F32),
        pltpu.VMEM((2, 8, 128), I32),
        pltpu.VMEM((8, 8, 128), I32),
        pltpu.VMEM((8, 8, 128), I32),
        pltpu.VMEM((12 * PARTS, 8, 8, 128), F32),
        pltpu.VMEM((96 * PARTS, 128 * len(CHUNKS)), jnp.bfloat16),
        pltpu.VMEM((256, 128 * len(CHUNKS)), jnp.bfloat16),
        pltpu.VMEM((4, 8, 128), F32),
        pltpu.VMEM((4, 8, 128), F32),
        pltpu.VMEM((4, 16, 128), F32),
        pltpu.VMEM((4, 16, 128), F32),
        pltpu.VMEM((4, 16, 128), F32),
        pltpu.VMEM((4, 16, 128), F32),
        pltpu.VMEM((4, 8, 128), F32),
        pltpu.VMEM((4, 8, 128), F32),
        pltpu.VMEM((4, 8, 128), F32),
        pltpu.VMEM((4, 8, 128), F32),
        pltpu.VMEM((1, 128), F32),
        pltpu.VMEM((n_gy - 1, 1, 128), F32),
        pltpu.VMEM((1, 128), F32),
        pltpu.VMEM((n_gx - 1, 1, 128), F32),
        dma((18,)),
        dma((3,)),
        dma((5, 4)),
        dma((5, 4)),
        dma((n_gy - 1,)),
        dma((n_gy - 1,)),
        dma((n_gx - 1,)),
        dma((n_gx - 1,)),
    ]
    velocity, force_local, force_cross = pl.pallas_call(
        functools.partial(kernel, n_gx, n_gy),
        out_shape=(
            jax.ShapeDtypeStruct((6, 2048), F32),
            jax.ShapeDtypeStruct((20, 128), F32),
            jax.ShapeDtypeStruct((4, 256), F32),
        ),
        in_specs=[anyspace] * 18,
        out_specs=(anyspace,) * 3,
        scratch_shapes=scratch,
        compiler_params=pltpu.CompilerParams(
            collective_id=0, has_side_effects=True, vmem_limit_bytes=67_043_328
        ),
    )(*operands)
    return velocity, force_local.reshape(2560), force_cross.reshape(1, 4, 256)


def solution(mesh):
    both = ("gx", "gy")
    flat = P(both)
    wide = P(None, both)
    cube = P(both, None, None)
    return jax.shard_map(
        functools.partial(on_device, mesh.shape["gx"], mesh.shape["gy"]),
        mesh=mesh,
        in_specs=(wide, *[flat] * 6, wide, *[flat] * 4, *[cube] * 4, P(both, None), cube),
        out_specs=(wide, flat, cube),
        check_vma=False,
    )
```

```python
import functools

import jax
import jax.numpy as jnp
from jax import lax
from jax.experimental import pallas as pl
from jax.experimental.pallas import tpu as pltpu
from jax.sharding import PartitionSpec as P


F32 = jnp.float32
I32 = jnp.int32
STEP_TIME = 0.5
FLOOR_GAP = 0.25
TINY = 1e-06
PARTS = 2
OFFSETS = ((0, 1), (1, 1), (1, 0), (1, -1))
MESH = pl.DeviceIdType.MESH
LOCAL_STARTS = (0, 8, 12)
CHUNKS = (
    [(0, s) for s in range(8)]
    + [(1, s) for s in range(8)]
    + [(2, s) for s in range(4, 8)]
    + [(3, s) for s in range(8)]
    + [(4, s) for s in range(8)]
    + [(5, s) for s in range(4, 8)]
    + [(6, s) for s in range(8)]
    + [(7, s) for s in range(8)]
)
LOCAL_CHUNKS = 40


def cross3(a, b):
    return [a[1] * b[2] - a[2] * b[1], a[2] * b[0] - a[0] * b[2], a[0] * b[1] - a[1] * b[0]]


def dot3(a, b):
    return a[0] * b[0] + a[1] * b[1] + a[2] * b[2]


def lanes_of(table, index):
    return jnp.take_along_axis(table, index, axis=1, mode="promise_in_bounds")


def kernel(
    n_gx,
    n_gy,
    h_cent,
    h_tilt,
    h_turn,
    h_rad,
    h_perp,
    h_axial,
    h_rot,
    h_load,
    h_lf,
    h_ls,
    h_a1,
    h_a2,
    h_mine,
    h_slot,
    h_own,
    h_oth,
    h_count,
    h_exp,
    o_vel,
    o_fl,
    o_fc,
    v_cent,
    v_tilt,
    v_turn,
    v_rad,
    v_perp,
    v_axial,
    v_rot,
    v_load,
    v_lf,
    v_ls,
    v_a1,
    v_a2,
    v_mine,
    v_slot,
    v_own,
    v_oth,
    s_count,
    v_exp,
    t_seg,
    t_move,
    x_seg,
    pk,
    pk_int,
    key_hi,
    key_lo,
    push,
    o_mat,
    acc,
    send_s,
    recv_s,
    send_d,
    recv_d,
    send_e,
    recv_e,
    send_f,
    recv_f,
    send_g,
    recv_g,
    sum_a,
    got_a,
    sum_b,
    got_b,
    in_sem,
    ex_send,
    ex_recv,
    a_send,
    a_recv,
    b_send,
    b_recv,
    relay,
):
    gx = lax.axis_index("gx")
    gy = lax.axis_index("gy")

    def place(dx, dy):
        return (lax.rem(gx + (dx + n_gx), n_gx), lax.rem(gy + (dy + n_gy), n_gy))

    n_y = grid_y(n_gx)
    n_z = n_gx // n_y
    at_y, at_z = lax.rem(gx, n_y), gx // n_y

    def plane(oy, oz):
        return (lax.rem(at_z + oz, n_z) * n_y + lax.rem(at_y + oy, n_y), gy)

    def inside(dx, dy):
        row, column = gx + dx, gy + dy
        return (row >= 0) & (row < n_gx) & (column >= 0) & (column < n_gy)

    has_partner = [inside(dx, dy) for dx, dy in OFFSETS]
    has_owner = [inside(-dx, -dy) for dx, dy in OFFSETS]

    sources = (h_cent, h_tilt, h_turn, h_rad, h_perp, h_axial, h_rot, h_load, h_lf, h_ls, h_a1, h_a2, h_mine, h_slot, h_own, h_oth, h_count, h_exp)
    targets = (v_cent, v_tilt, v_turn, v_rad, v_perp, v_axial, v_rot, v_load, v_lf, v_ls, v_a1, v_a2, v_mine, v_slot, v_own, v_oth, s_count, v_exp)
    loads_in = {}
    for i in (1, 2, 7, 4, 5, 6, 13, 15, 16, 17, 12, 14, 0, 3, 8, 9, 10, 11):
        loads_in[i] = pltpu.make_async_copy(sources[i], targets[i], in_sem.at[i])
        loads_in[i].start()

    barrier = pltpu.get_barrier_semaphore()

    def greet(to):
        pl.semaphore_signal(barrier, inc=1, device_id=to, device_id_type=MESH)

    greetings = (n_gy - 1) + (n_y - 1) + (n_z - 1)
    for d in (1, 2, 3):
        dx, dy = OFFSETS[d]
        pl.when(has_partner[d])(functools.partial(greet, place(dx, dy)))
        pl.when(has_owner[d])(functools.partial(greet, place(-dx, -dy)))
        greetings = greetings + has_partner[d].astype(I32) + has_owner[d].astype(I32)
    for o in range(1, n_gy):
        greet(place(0, o))
    for o in range(1, n_y):
        greet(plane(o, 0))
    for o in range(1, n_z):
        greet(plane(0, o))

    def need(*which):
        for i in which:
            loads_in[i].wait()

    row8 = lax.broadcasted_iota(I32, (8, 128), 0)
    lane8 = lax.broadcasted_iota(I32, (8, 128), 1)
    heading8 = row8 // 2
    zero8 = jnp.zeros((8, 128), F32)

    def spread_rows(ref, row, *lead):
        return ref[(*lead, pl.ds(row, 8, stride=0), slice(None))]

    need(1, 2)
    lifted = jnp.sin(v_tilt[...])
    tangent = [lifted * jnp.cos(v_turn[...]), lifted * jnp.sin(v_turn[...]), jnp.cos(v_tilt[...])]
    need(7, 4, 5, 6)
    for c in range(6):
        for r in range(16):
            x_seg[c, r : r + 1, :] = v_load[c : c + 1, r * 128 : (r + 1) * 128]

    def mobile(applied):
        along = dot3(tangent, applied)
        pulled = v_axial[...] * along
        return [v_perp[...] * applied[c] + pulled * tangent[c] for c in range(3)] + [
            v_rot[...] * applied[3 + c] for c in range(3)
        ]

    drift = mobile([x_seg[c] for c in range(6)])
    for c in range(3):
        t_seg[c] = tangent[c]
    for c in range(6):
        t_seg[3 + c] = drift[c]

    def unpacked(ref, into, field):
        for d in range(4):
            for h in range(2):
                into[field, 2 * d + h : 2 * d + h + 1, :] = ref[d : d + 1, h * 128 : (h + 1) * 128]
        return into[field]

    need(13, 15, 16)
    for d in range(4):
        for h in range(2):
            piece = slice(h * 128, (h + 1) * 128)
            send_s[d, h : h + 1, :] = v_slot[d : d + 1, piece].astype(F32)
            send_s[d, 2 + h : 3 + h, :] = v_oth[d : d + 1, piece]
    live_own = zero8
    for d in range(4):
        bound = s_count[0, d]
        live_own = jnp.where(
            (heading8 == d) & ((row8 - 2 * d) * 128 + lane8 < bound), 1.0, live_own
        )
    for d in range(4):
        send_s[d, 4:6, :] = live_own[2 * d : 2 * d + 2]

    def blank(refs, d):
        for ref in refs:
            ref[d] = jnp.zeros(ref.shape[1:], F32)

    for d in range(4):
        pl.when(~has_partner[d])(functools.partial(blank, (recv_e, recv_g), d))
        pl.when(~has_owner[d])(functools.partial(blank, (recv_s, recv_d, recv_f), d))

    pl.semaphore_wait(barrier, greetings)
    for o in range(1, n_z):
        pl.semaphore_signal(relay.at[0], inc=1, device_id=plane(0, o), device_id_type=MESH)

    partner = [place(dx, dy) for dx, dy in OFFSETS]
    owner = [place(-dx, -dy) for dx, dy in OFFSETS]
    moves = {}

    def launch(src, dst, step, to_partner):
        moves[step] = to_partner, []
        for d in range(4):
            copy = pltpu.make_async_remote_copy(
                src_ref=src.at[d],
                dst_ref=dst.at[d],
                send_sem=ex_send.at[step, d],
                recv_sem=ex_recv.at[step, d],
                device_id=partner[d] if to_partner else owner[d],
                device_id_type=MESH,
            )
            moves[step][1].append(copy)
            pl.when(has_partner[d] if to_partner else has_owner[d])(copy.start)

    def arrive(step):
        to_partner, copies = moves[step]
        for d in range(4):
            pl.when(has_owner[d] if to_partner else has_partner[d])(copies[d].wait_recv)

    launch(send_s, recv_s, 0, True)

    need(0, 3)
    for c in range(3):
        for r in range(16):
            t_seg[9 + c, r : r + 1, :] = v_cent[c : c + 1, r * 128 : (r + 1) * 128]

    def table_row(c, r):
        if c < 3:
            return spread_rows(t_seg, r, 9 + c)
        if c == 3:
            return spread_rows(v_rad, r)
        return spread_rows(t_seg, r, c - 4)

    def move_row(c, r):
        return spread_rows(t_move, r, c)

    beside = []

    def picked(index, row_of, count):
        block = index >> 7
        lane = index & 127
        out = [None] * count
        for r in range(16):
            here = block == r
            for c in range(count):
                taken = lanes_of(row_of(c, r), lane)
                out[c] = taken if r == 0 else jnp.where(here, taken, out[c])
            if beside:
                beside.pop(0)()
        return out

    def endpoint(values, arc):
        lever = [arc * values[4 + c] for c in range(3)]
        place_of = [values[c] + lever[c] for c in range(3)]
        turned = cross3(values[10:13], lever)
        moving = [values[7 + c] + turned[c] for c in range(3)]
        return dict(lever=lever, at=place_of, radius=values[3], moving=moving)

    need(17)
    exports = v_exp[...]
    offered = picked(jnp.concatenate([exports, exports], axis=0), table_row, 13)
    for d in range(4):
        for c in range(13):
            send_e[d, c : c + 1, :] = offered[c][d : d + 1]
    launch(send_e, recv_e, 1, False)

    need(12, 14)
    index = [None] * 8
    index[6] = unpacked(v_mine, pk_int, 0)
    arc_own = unpacked(v_own, pk, 1)
    own = endpoint(picked(index[6], table_row, 13), arc_own)
    for i, value in enumerate(own["at"] + [own["radius"]] + own["moving"]):
        for d in range(4):
            send_d[d, 2 * i : 2 * i + 2, :] = value[2 * d : 2 * d + 2]
    launch(send_d, recv_d, 2, True)

    def pair(one, two, live):
        apart = [one["at"][c] - two["at"][c] for c in range(3)]
        spacing = jnp.sqrt(dot3(apart, apart))
        scale = 1.0 / jnp.maximum(spacing, FLOOR_GAP)
        if live is not None:
            scale = scale * live
        normal = [a * scale for a in apart]
        clearance = spacing - one["radius"] - two["radius"]
        if live is not None:
            clearance = clearance * live
        rate = dot3(normal, [one["moving"][c] - two["moving"][c] for c in range(3)])
        slope = clearance * (1.0 / STEP_TIME) + rate
        return dict(normal=normal, slope=slope, down=jnp.maximum(0.0, -slope))

    def split(value):
        pieces = []
        for _ in range(PARTS):
            piece = value.astype(jnp.bfloat16).astype(F32)
            pieces.append(piece)
            value = value - piece
        return pieces

    def set_keys(e):
        key_hi[e] = ((index[e] >> 7) & 7).astype(F32)
        key_lo[e] = (((index[e] >> 10) << 7) | (index[e] & 127)).astype(F32)

    def tall_row(first, second):
        return jnp.concatenate([first, second], axis=0).astype(jnp.bfloat16)

    low = [
        tall_row(row8.astype(F32) + float(k), row8.astype(F32) + float(k + 8)) for k in range(0, 256, 16)
    ]
    high = tall_row(row8.astype(F32), row8.astype(F32))
    one16 = jnp.ones((16, 128), jnp.bfloat16)
    none16 = jnp.zeros((16, 128), jnp.bfloat16)

    def set_push(e, first, normal, arm, amounts):
        sign = 1.0 if first else -1.0
        for i, amount in enumerate(amounts):
            scaled = amount * sign
            for c in range(6):
                value = scaled * (normal[c] if c < 3 else arm[c - 3])
                for p, piece in enumerate(split(value)):
                    push[(i * PARTS + p) * 6 + c, e] = piece

    def set_columns(n):
        e, s = CHUNKS[n]
        key = spread_rows(key_lo, s, e)
        key = tall_row(key, key)
        for k in range(0, 256, 16):
            o_mat[n, k : k + 16, :] = jnp.where(low[k // 16] == key, one16, none16)

    def columns_beside(first, last, every):
        for n in range(first, last):
            beside.append(functools.partial(set_columns, n))
            beside.extend([lambda: None] * (every - 1))

    def loads_from(chunk, count):
        e, s = chunk
        key = spread_rows(key_hi, s, e)
        here = high == tall_row(key, key)
        out = []
        for k in range(0, count, 2):
            value = tall_row(spread_rows(push, s, k, e), spread_rows(push, s, k + 1, e))
            out.append(jnp.where(here, value, none16))
        return out

    def product(start, rows, group):
        tiles = 3 * PARTS
        left = [jnp.concatenate(r[group * tiles : (group + 1) * tiles], axis=0) for r in rows]
        return lax.dot_general(
            jnp.concatenate(left, axis=1),
            jnp.concatenate([o_mat[start + n] for n in range(len(rows))], axis=1),
            (((1,), (1,)), ((), ())),
            preferred_element_type=F32,
        )

    def loads_of(total):
        out = []
        for c in range(6):
            value = None
            for p in reversed(range(PARTS)):
                at = (p * 6 + c) * 8
                piece = jnp.concatenate([total[at : at + 8, 0:128], total[at : at + 8, 128:256]], axis=0)
                value = piece if value is None else value + piece
            out.append(value)
        return out

    need(8, 9, 10, 11)
    pairs = [None] * 5
    ends = [None] * 8
    for b, start in enumerate(LOCAL_STARTS):
        index[b] = v_lf[start : start + 8, :]
        index[3 + b] = v_ls[start : start + 8, :]
        set_keys(b)
        set_keys(3 + b)
    set_keys(6)
    columns_beside(0, 48, 2)
    for b, start in enumerate(LOCAL_STARTS):
        ends[b] = endpoint(picked(index[b], table_row, 13), v_a1[start : start + 8, :])
        ends[3 + b] = endpoint(picked(index[3 + b], table_row, 13), v_a2[start : start + 8, :])
        pairs[b] = pair(ends[b], ends[3 + b], None)
    ends[6] = own

    def set_ends(b, one, two, amounts):
        if one is not None:
            set_push(one, True, pairs[b]["normal"], cross3(ends[one]["lever"], pairs[b]["normal"]), amounts)
        if two is not None:
            set_push(two, False, pairs[b]["normal"], cross3(ends[two]["lever"], pairs[b]["normal"]), amounts)

    wide = 12 * PARTS
    narrow = 6 * PARTS
    for b in range(3):
        set_ends(b, b, 3 + b, (pairs[b]["slope"], pairs[b]["down"]))
    rows = [loads_from(chunk, wide) for chunk in CHUNKS[:LOCAL_CHUNKS]]
    for group in range(2):
        acc[group] = product(0, rows, group)

    arrive(0)

    def repacked(ref, field, slot):
        for d in range(4):
            pk[slot, 2 * d : 2 * d + 2, :] = ref[d, 2 * field : 2 * field + 2, :]
        return pk[slot]

    def by_heading(row_of):
        out = row_of(0)
        for d in range(1, 4):
            out = jnp.where(heading8 == d, row_of(d), out)
        return out

    slot_in = repacked(recv_s, 0, 2).astype(I32)
    arc_in = repacked(recv_s, 1, 3)
    live_in = repacked(recv_s, 2, 4)
    index[7] = lanes_of(by_heading(lambda d: spread_rows(v_exp, d)), slot_in)
    set_keys(7)
    columns_beside(48, 56, 2)
    ends[7] = endpoint(picked(index[7], table_row, 13), arc_in)

    slot_own = unpacked(v_slot, pk_int, 1)
    arc_oth = unpacked(v_oth, pk, 6)
    arrive(1)
    far = [
        lanes_of(
            by_heading(lambda d, c=c: spread_rows(recv_e, c, d)), slot_own
        )
        for c in range(13)
    ]
    pairs[3] = pair(own, endpoint(far, arc_oth), live_own)
    set_ends(3, 6, None, (pairs[3]["slope"], pairs[3]["down"]))
    arrive(2)
    near = [repacked(recv_d, i, 7 + i) for i in range(7)]
    pairs[4] = pair(dict(at=near[0:3], radius=near[3], moving=near[4:7]), ends[7], live_in)
    set_ends(4, None, 7, (pairs[4]["slope"], pairs[4]["down"]))

    rows = [loads_from(chunk, wide) for chunk in CHUNKS[LOCAL_CHUNKS:]]
    both = []
    for group in range(2):
        both += loads_of(acc[group] + product(LOCAL_CHUNKS, rows, group))
    moved_all = mobile(both[0:6])
    moved_down = mobile(both[6:12])
    for c in range(6):
        t_move[c] = moved_down[c]

    def folded(value):
        return jnp.sum(value, axis=0, keepdims=True)

    def halved(row):
        row = row + pltpu.roll(row, 64, 1)
        return row + pltpu.roll(row, 32, 1)

    def counted(name):
        value = pairs[0][name] * pairs[0][name] + pairs[1][name] * pairs[1][name]
        last = pairs[2][name] * pairs[2][name]
        return value + jnp.where(row8 >= 4, last, 0.0) + pairs[3][name] * pairs[3][name]

    def power(one, two):
        value = one[0] * two[0]
        for c in range(1, 6):
            value = value + one[c] * two[c]
        return value

    rows = [
        halved(folded(v))
        for v in (counted("slope"), power(both[0:6], moved_all), counted("down"), power(both[6:12], moved_down))
    ]
    quarter = lax.broadcasted_iota(I32, (1, 128), 1) // 32
    mine = rows[0]
    for i in range(1, 4):
        mine = jnp.where(quarter == i, rows[i], mine)
    sum_a[...] = mine

    def ring(src, dst, sems, slot, to):
        return pltpu.make_async_remote_copy(
            src_ref=src,
            dst_ref=dst.at[slot],
            send_sem=sems[0].at[0],
            recv_sem=sems[1].at[0],
            device_id=to,
            device_id_type=MESH,
        )

    def whole(dst, sems):
        return pltpu.make_async_remote_copy(
            src_ref=dst,
            dst_ref=dst,
            send_sem=sems[0].at[0],
            recv_sem=sems[1].at[0],
            device_id=place(0, 1),
            device_id_type=MESH,
        )

    for o in range(1, n_gy):
        ring(sum_a, got_a, (a_send, a_recv), o - 1, place(0, o)).start()

    def contact(e):
        values = picked(index[e], move_row, 6)
        turned = cross3(values[3:6], ends[e]["lever"])
        return [values[c] + turned[c] for c in range(3)]

    moved_own = contact(6)
    for c in range(3):
        for d in range(4):
            send_f[d, 2 * c : 2 * c + 2, :] = moved_own[c][2 * d : 2 * d + 2]
    launch(send_f, recv_f, 3, True)
    moved_in = contact(7)
    for c in range(3):
        for d in range(4):
            send_g[d, 2 * c : 2 * c + 2, :] = moved_in[c][2 * d : 2 * d + 2]
    launch(send_g, recv_g, 4, False)

    whole(got_a, (a_send, a_recv)).wait_recv()
    mine = sum_a[...]
    for o in range(1, n_gy):
        mine = mine + got_a[o - 1]
    sum_b[...] = mine
    pl.semaphore_wait(relay.at[0], n_z - 1)
    for o in range(1, n_gx):
        ring(sum_b, got_b, (b_send, b_recv), o - 1, plane(o % n_y, o // n_y)).start()

    def curve(b, one, two):
        return dot3(pairs[b]["normal"], [one[c] - two[c] for c in range(3)])

    curved = [None] * 5
    for b in range(3):
        curved[b] = curve(b, contact(b), contact(3 + b))
    arrive(3)
    arrive(4)
    curved[3] = curve(3, moved_own, [repacked(recv_g, c, c) for c in range(3)])
    curved[4] = curve(4, [repacked(recv_f, c, 3 + c) for c in range(3)], moved_in)

    whole(got_b, (b_send, b_recv)).wait_recv()
    mine = sum_b[...]
    for o in range(1, n_gx):
        mine = mine + got_b[o - 1]
    sums = [
        jnp.sum(jnp.where(quarter == i, mine, 0.0), axis=1, keepdims=True) for i in range(4)
    ]
    step_first = sums[0] / (sums[1] + TINY)
    square = step_first * step_first
    step_second = (square * sums[2]) / (square * sums[3] + TINY)
    step_first = jnp.broadcast_to(step_first, (8, 128))
    step_second = jnp.broadcast_to(step_second, (8, 128))

    force = []
    for b in range(5):
        thrust = step_first * pairs[b]["down"]
        slope = pairs[b]["slope"] + step_first * curved[b]
        force.append(jnp.maximum(0.0, thrust - step_second * slope))
    for b, start in enumerate(LOCAL_STARTS):
        o_fl[start : start + 8, :] = force[b]
    for d in range(4):
        for h in range(2):
            o_fc[d : d + 1, h * 128 : (h + 1) * 128] = force[3][2 * d + h : 2 * d + h + 1]
    for b in range(3):
        set_ends(b, b, 3 + b, (force[b],))
    set_ends(3, 6, None, (force[3],))
    set_ends(4, None, 7, (force[4],))
    half = len(CHUNKS) // 2
    rows = [loads_from(chunk, narrow) for chunk in CHUNKS]
    acc[0] = product(0, rows[:half], 0)
    acc[1] = product(half, rows[half:], 0)
    moved = mobile(loads_of(acc[0] + acc[1]))
    for c in range(6):
        velocity = t_seg[3 + c] + moved[c]
        for r in range(16):
            o_vel[c : c + 1, r * 128 : (r + 1) * 128] = velocity[r : r + 1]
    whole(got_a, (a_send, a_recv)).wait_send()
    whole(got_b, (b_send, b_recv)).wait_send()
    for to_partner, copies in moves.values():
        for d in range(4):
            pl.when(has_partner[d] if to_partner else has_owner[d])(copies[d].wait_send)


def hand_out(vel, fl, fc, o_vel, o_fl, o_fc, sem):
    copies = [
        pltpu.make_async_copy(src, dst, sem.at[i])
        for i, (src, dst) in enumerate(((vel, o_vel), (fl, o_fl), (fc, o_fc)))
    ]
    for copy in copies:
        copy.start()
    for copy in copies:
        copy.wait()


def grid_y(n_gx):
    return max(k for k in range(1, n_gx + 1) if n_gx % k == 0 and k * k <= n_gx)


def on_device(n_gx, n_gy, cent, tilt, turn, rad, perp, axial, rot, load, lf, ls, a1, a2, mine, slot, own, oth, count, exports):
    segs = [v.reshape(16, 128) for v in (tilt, turn, rad, perp, axial, rot)]
    local = [v.reshape(20, 128) for v in (lf, ls, a1, a2)]
    cross = [v.reshape(4, 256) for v in (mine, slot, own, oth)]
    operands = [cent, *segs, load, *local, *cross, count, exports.reshape(4, 128)]
    anyspace = pl.BlockSpec(memory_space=pltpu.HBM)

    def held(v):
        return pltpu.VMEM(v.shape, v.dtype)

    inputs = [held(v) for v in operands]
    inputs[16] = pltpu.SMEM(count.shape, count.dtype)
    dma = pltpu.SemaphoreType.DMA
    scratch = inputs + [
        pltpu.VMEM((12, 16, 128), F32),
        pltpu.VMEM((6, 16, 128), F32),
        pltpu.VMEM((6, 16, 128), F32),
        pltpu.VMEM((14, 8, 128), F32),
        pltpu.VMEM((2, 8, 128), I32),
        pltpu.VMEM((8, 8, 128), F32),
        pltpu.VMEM((8, 8, 128), F32),
        pltpu.VMEM((12 * PARTS, 8, 8, 128), F32),
        pltpu.VMEM((len(CHUNKS), 256, 128), jnp.bfloat16),
        pltpu.VMEM((2, 48 * PARTS, 256), F32),
        pltpu.VMEM((4, 8, 128), F32),
        pltpu.VMEM((4, 8, 128), F32),
        pltpu.VMEM((4, 16, 128), F32),
        pltpu.VMEM((4, 16, 128), F32),
        pltpu.VMEM((4, 16, 128), F32),
        pltpu.VMEM((4, 16, 128), F32),
        pltpu.VMEM((4, 8, 128), F32),
        pltpu.VMEM((4, 8, 128), F32),
        pltpu.VMEM((4, 8, 128), F32),
        pltpu.VMEM((4, 8, 128), F32),
        pltpu.VMEM((1, 128), F32),
        pltpu.VMEM((n_gy - 1, 1, 128), F32),
        pltpu.VMEM((1, 128), F32),
        pltpu.VMEM((n_gx - 1, 1, 128), F32),
        dma((18,)),
        dma((5, 4)),
        dma((5, 4)),
        dma((1,)),
        dma((1,)),
        dma((1,)),
        dma((1,)),
        pltpu.SemaphoreType.REGULAR((1,)),
    ]
    operands = [pltpu.with_memory_space_constraint(v, pltpu.HBM) for v in operands]
    outs = ((6, 2048), (20, 128), (4, 256))
    near = pl.BlockSpec(memory_space=pltpu.VMEM)
    solved = pl.pallas_call(
        functools.partial(kernel, n_gx, n_gy),
        out_shape=tuple(pltpu.VMEM(shape, F32) for shape in outs),
        in_specs=[anyspace] * 18,
        out_specs=(near,) * 3,
        scratch_shapes=scratch,
        compiler_params=pltpu.CompilerParams(
            collective_id=0, has_side_effects=True, vmem_limit_bytes=48 * 1024 * 1024
        ),
    )(*operands)
    velocity, force_local, force_cross = pl.pallas_call(
        hand_out,
        out_shape=tuple(jax.ShapeDtypeStruct(shape, F32) for shape in outs),
        in_specs=[near] * 3,
        out_specs=(anyspace,) * 3,
        scratch_shapes=[dma((3,))],
        compiler_params=pltpu.CompilerParams(vmem_limit_bytes=1024 * 1024),
    )(*[pltpu.with_memory_space_constraint(v, pltpu.VMEM) for v in solved])
    return velocity, force_local.reshape(2560), force_cross.reshape(1, 4, 256)


def solution(mesh):
    both = ("gx", "gy")
    flat = P(both)
    wide = P(None, both)
    cube = P(both, None, None)
    return jax.shard_map(
        functools.partial(on_device, mesh.shape["gx"], mesh.shape["gy"]),
        mesh=mesh,
        in_specs=(wide, *[flat] * 6, wide, *[flat] * 4, *[cube] * 4, P(both, None), cube),
        out_specs=(wide, flat, cube),
        check_vma=False,
    )
```

```python
import functools

import jax
import jax.numpy as jnp
from jax import lax
from jax.experimental import pallas as pl
from jax.experimental.pallas import tpu as pltpu
from jax.sharding import PartitionSpec as P


F32 = jnp.float32
I32 = jnp.int32
STEP_TIME = 0.5
FLOOR_GAP = 0.25
TINY = 1e-06
PARTS = 2
OFFSETS = ((0, 1), (1, 1), (1, 0), (1, -1))
MESH = pl.DeviceIdType.MESH
LOCAL_STARTS = (0, 8, 12)
CHUNKS = (
    [(0, s) for s in range(8)]
    + [(1, s) for s in range(8)]
    + [(2, s) for s in range(4, 8)]
    + [(3, s) for s in range(8)]
    + [(4, s) for s in range(8)]
    + [(5, s) for s in range(4, 8)]
    + [(6, s) for s in range(8)]
    + [(7, s) for s in range(8)]
)
LOCAL_CHUNKS = 40


def cross3(a, b):
    return [a[1] * b[2] - a[2] * b[1], a[2] * b[0] - a[0] * b[2], a[0] * b[1] - a[1] * b[0]]


def dot3(a, b):
    return a[0] * b[0] + a[1] * b[1] + a[2] * b[2]


def lanes_of(table, index):
    return jnp.take_along_axis(table, index, axis=1, mode="promise_in_bounds")


def kernel(
    n_gx,
    n_gy,
    h_cent,
    h_tilt,
    h_turn,
    h_rad,
    h_perp,
    h_axial,
    h_rot,
    h_load,
    h_lf,
    h_ls,
    h_a1,
    h_a2,
    h_mine,
    h_slot,
    h_own,
    h_oth,
    h_count,
    h_exp,
    o_vel,
    o_fl,
    o_fc,
    v_cent,
    v_tilt,
    v_turn,
    v_rad,
    v_perp,
    v_axial,
    v_rot,
    v_load,
    v_lf,
    v_ls,
    v_a1,
    v_a2,
    v_mine,
    v_slot,
    v_own,
    v_oth,
    s_count,
    v_exp,
    t_seg,
    t_move,
    x_seg,
    pk,
    pk_int,
    key_hi,
    key_lo,
    push,
    o_mat,
    send_s,
    recv_s,
    send_d,
    recv_d,
    send_e,
    recv_e,
    send_f,
    recv_f,
    send_g,
    recv_g,
    sum_a,
    got_a,
    sum_b,
    got_b,
    in_sem,
    ex_send,
    ex_recv,
    a_send,
    a_recv,
    b_send,
    b_recv,
    relay,
    wide_0,
    wide_1,
    narrow_0,
    narrow_1,
):
    gx = lax.axis_index("gx")
    gy = lax.axis_index("gy")

    def place(dx, dy):
        return (lax.rem(gx + (dx + n_gx), n_gx), lax.rem(gy + (dy + n_gy), n_gy))

    n_y = grid_y(n_gx)
    n_z = n_gx // n_y
    at_y, at_z = lax.rem(gx, n_y), gx // n_y

    def plane(oy, oz):
        return (lax.rem(at_z + oz, n_z) * n_y + lax.rem(at_y + oy, n_y), gy)

    def inside(dx, dy):
        row, column = gx + dx, gy + dy
        return (row >= 0) & (row < n_gx) & (column >= 0) & (column < n_gy)

    has_partner = [inside(dx, dy) for dx, dy in OFFSETS]
    has_owner = [inside(-dx, -dy) for dx, dy in OFFSETS]

    sources = (h_cent, h_tilt, h_turn, h_rad, h_perp, h_axial, h_rot, h_load, h_lf, h_ls, h_a1, h_a2, h_mine, h_slot, h_own, h_oth, h_count, h_exp)
    targets = (v_cent, v_tilt, v_turn, v_rad, v_perp, v_axial, v_rot, v_load, v_lf, v_ls, v_a1, v_a2, v_mine, v_slot, v_own, v_oth, s_count, v_exp)
    loads_in = {}
    for i in (1, 2, 7, 4, 5, 6, 13, 15, 16, 17, 12, 14, 0, 3, 8, 9, 10, 11):
        loads_in[i] = pltpu.make_async_copy(sources[i], targets[i], in_sem.at[i])
        loads_in[i].start()

    barrier = pltpu.get_barrier_semaphore()

    def greet(to):
        pl.semaphore_signal(barrier, inc=1, device_id=to, device_id_type=MESH)

    greetings = (n_gy - 1) + (n_y - 1) + (n_z - 1)
    for d in (1, 2, 3):
        dx, dy = OFFSETS[d]
        pl.when(has_partner[d])(functools.partial(greet, place(dx, dy)))
        pl.when(has_owner[d])(functools.partial(greet, place(-dx, -dy)))
        greetings = greetings + has_partner[d].astype(I32) + has_owner[d].astype(I32)
    for o in range(1, n_gy):
        greet(place(0, o))
    for o in range(1, n_y):
        greet(plane(o, 0))
    for o in range(1, n_z):
        greet(plane(0, o))

    def need(*which):
        for i in which:
            loads_in[i].wait()

    row8 = lax.broadcasted_iota(I32, (8, 128), 0)
    lane8 = lax.broadcasted_iota(I32, (8, 128), 1)
    heading8 = row8 // 2
    zero8 = jnp.zeros((8, 128), F32)

    def spread_rows(ref, row, *lead):
        return ref[(*lead, pl.ds(row, 8, stride=0), slice(None))]

    need(1, 2)
    lifted = jnp.sin(v_tilt[...])
    tangent = [lifted * jnp.cos(v_turn[...]), lifted * jnp.sin(v_turn[...]), jnp.cos(v_tilt[...])]
    need(7, 4, 5, 6)
    for c in range(6):
        for r in range(16):
            x_seg[c, r : r + 1, :] = v_load[c : c + 1, r * 128 : (r + 1) * 128]

    def mobile(applied):
        along = dot3(tangent, applied)
        pulled = v_axial[...] * along
        return [v_perp[...] * applied[c] + pulled * tangent[c] for c in range(3)] + [
            v_rot[...] * applied[3 + c] for c in range(3)
        ]

    drift = mobile([x_seg[c] for c in range(6)])
    for c in range(3):
        t_seg[c] = tangent[c]
    for c in range(6):
        t_seg[3 + c] = drift[c]

    def unpacked(ref, into, field):
        for d in range(4):
            for h in range(2):
                into[field, 2 * d + h : 2 * d + h + 1, :] = ref[d : d + 1, h * 128 : (h + 1) * 128]
        return into[field]

    need(13, 15, 16)
    for d in range(4):
        for h in range(2):
            piece = slice(h * 128, (h + 1) * 128)
            send_s[d, h : h + 1, :] = v_slot[d : d + 1, piece].astype(F32)
            send_s[d, 2 + h : 3 + h, :] = v_oth[d : d + 1, piece]
    live_own = zero8
    for d in range(4):
        bound = s_count[0, d]
        live_own = jnp.where(
            (heading8 == d) & ((row8 - 2 * d) * 128 + lane8 < bound), 1.0, live_own
        )
    for d in range(4):
        send_s[d, 4:6, :] = live_own[2 * d : 2 * d + 2]

    def blank(refs, d):
        for ref in refs:
            ref[d] = jnp.zeros(ref.shape[1:], F32)

    for d in range(4):
        pl.when(~has_partner[d])(functools.partial(blank, (recv_e, recv_g), d))
        pl.when(~has_owner[d])(functools.partial(blank, (recv_s, recv_d, recv_f), d))

    pl.semaphore_wait(barrier, greetings)
    for o in range(1, n_z):
        pl.semaphore_signal(relay.at[0], inc=1, device_id=plane(0, o), device_id_type=MESH)

    partner = [place(dx, dy) for dx, dy in OFFSETS]
    owner = [place(-dx, -dy) for dx, dy in OFFSETS]
    moves = {}

    def launch(src, dst, step, to_partner):
        moves[step] = to_partner, []
        for d in range(4):
            copy = pltpu.make_async_remote_copy(
                src_ref=src.at[d],
                dst_ref=dst.at[d],
                send_sem=ex_send.at[step, d],
                recv_sem=ex_recv.at[step, d],
                device_id=partner[d] if to_partner else owner[d],
                device_id_type=MESH,
            )
            moves[step][1].append(copy)
            pl.when(has_partner[d] if to_partner else has_owner[d])(copy.start)

    def arrive(step):
        to_partner, copies = moves[step]
        for d in range(4):
            pl.when(has_owner[d] if to_partner else has_partner[d])(copies[d].wait_recv)

    launch(send_s, recv_s, 0, True)

    need(0, 3)
    for c in range(3):
        for r in range(16):
            t_seg[9 + c, r : r + 1, :] = v_cent[c : c + 1, r * 128 : (r + 1) * 128]

    def table_row(c, r):
        if c < 3:
            return spread_rows(t_seg, r, 9 + c)
        if c == 3:
            return spread_rows(v_rad, r)
        return spread_rows(t_seg, r, c - 4)

    def move_row(c, r):
        return spread_rows(t_move, r, c)

    beside = []

    def picked(index, row_of, count):
        block = index >> 7
        lane = index & 127
        out = [None] * count
        for r in range(16):
            here = block == r
            for c in range(count):
                taken = lanes_of(row_of(c, r), lane)
                out[c] = taken if r == 0 else jnp.where(here, taken, out[c])
            if beside:
                beside.pop(0)()
        return out

    def endpoint(values, arc):
        lever = [arc * values[4 + c] for c in range(3)]
        place_of = [values[c] + lever[c] for c in range(3)]
        turned = cross3(values[10:13], lever)
        moving = [values[7 + c] + turned[c] for c in range(3)]
        return dict(lever=lever, at=place_of, radius=values[3], moving=moving)

    need(17)
    exports = v_exp[...]
    offered = picked(jnp.concatenate([exports, exports], axis=0), table_row, 13)
    for d in range(4):
        for c in range(13):
            send_e[d, c : c + 1, :] = offered[c][d : d + 1]
    launch(send_e, recv_e, 1, False)

    need(12, 14)
    index = [None] * 8
    index[6] = unpacked(v_mine, pk_int, 0)
    arc_own = unpacked(v_own, pk, 1)
    own = endpoint(picked(index[6], table_row, 13), arc_own)
    for i, value in enumerate(own["at"] + [own["radius"]] + own["moving"]):
        for d in range(4):
            send_d[d, 2 * i : 2 * i + 2, :] = value[2 * d : 2 * d + 2]
    launch(send_d, recv_d, 2, True)

    def pair(one, two, live):
        apart = [one["at"][c] - two["at"][c] for c in range(3)]
        spacing = jnp.sqrt(dot3(apart, apart))
        scale = 1.0 / jnp.maximum(spacing, FLOOR_GAP)
        if live is not None:
            scale = scale * live
        normal = [a * scale for a in apart]
        clearance = spacing - one["radius"] - two["radius"]
        if live is not None:
            clearance = clearance * live
        rate = dot3(normal, [one["moving"][c] - two["moving"][c] for c in range(3)])
        slope = clearance * (1.0 / STEP_TIME) + rate
        return dict(normal=normal, slope=slope, down=jnp.maximum(0.0, -slope))

    def split(value):
        pieces = []
        for _ in range(PARTS):
            piece = value.astype(jnp.bfloat16).astype(F32)
            pieces.append(piece)
            value = value - piece
        return pieces

    def set_keys(e):
        key_hi[e] = ((index[e] >> 7) & 7).astype(F32)
        key_lo[e] = (((index[e] >> 10) << 7) | (index[e] & 127)).astype(F32)

    def tall_row(first, second):
        return jnp.concatenate([first, second], axis=0).astype(jnp.bfloat16)

    low = [
        tall_row(row8.astype(F32) + float(k), row8.astype(F32) + float(k + 8)) for k in range(0, 256, 16)
    ]
    high = tall_row(row8.astype(F32), row8.astype(F32))
    one16 = jnp.ones((16, 128), jnp.bfloat16)
    none16 = jnp.zeros((16, 128), jnp.bfloat16)

    def set_push(e, first, normal, arm, amounts):
        sign = 1.0 if first else -1.0
        for i, amount in enumerate(amounts):
            scaled = amount * sign
            for c in range(6):
                value = scaled * (normal[c] if c < 3 else arm[c - 3])
                for p, piece in enumerate(split(value)):
                    push[(i * PARTS + p) * 6 + c, e] = piece

    def set_columns(n):
        e, s = CHUNKS[n]
        key = spread_rows(key_lo, s, e)
        key = tall_row(key, key)
        for k in range(0, 256, 16):
            o_mat[n, k : k + 16, :] = jnp.where(low[k // 16] == key, one16, none16)

    def columns_beside(first, last, every):
        for n in range(first, last):
            beside.append(functools.partial(set_columns, n))
            beside.extend([lambda: None] * (every - 1))

    def loads_from(chunk, count):
        e, s = chunk
        key = spread_rows(key_hi, s, e)
        here = high == tall_row(key, key)
        out = []
        for k in range(0, count, 2):
            value = tall_row(spread_rows(push, s, k, e), spread_rows(push, s, k + 1, e))
            out.append(jnp.where(here, value, none16))
        return out

    def accumulate(into, start, rows):
        for n in range(0, len(rows), 2):
            unit = (start + n) // 2 % 2
            stage = (start + n) // 4 % 2
            pltpu.matmul_push_rhs(
                jnp.concatenate([o_mat[start + n], o_mat[start + n + 1]], axis=1),
                staging_register=stage,
                mxu_index=unit,
                transpose=True,
            )
            left = [jnp.concatenate(r, axis=0) for r in rows[n : n + 2]]
            pltpu.matmul_acc_lhs(into[unit], jnp.concatenate(left, axis=1), load_staged_rhs=stage)

    def total_of(into):
        return pltpu.matmul_pop(into[0]) + pltpu.matmul_pop(into[1])

    def loads_of(total, group):
        out = []
        for c in range(6):
            value = None
            for p in reversed(range(PARTS)):
                at = ((group * PARTS + p) * 6 + c) * 8
                piece = jnp.concatenate([total[at : at + 8, 0:128], total[at : at + 8, 128:256]], axis=0)
                value = piece if value is None else value + piece
            out.append(value)
        return out

    need(8, 9, 10, 11)
    pairs = [None] * 5
    ends = [None] * 8
    for b, start in enumerate(LOCAL_STARTS):
        index[b] = v_lf[start : start + 8, :]
        index[3 + b] = v_ls[start : start + 8, :]
        set_keys(b)
        set_keys(3 + b)
    set_keys(6)
    columns_beside(0, 48, 2)
    for b, start in enumerate(LOCAL_STARTS):
        ends[b] = endpoint(picked(index[b], table_row, 13), v_a1[start : start + 8, :])
        ends[3 + b] = endpoint(picked(index[3 + b], table_row, 13), v_a2[start : start + 8, :])
        pairs[b] = pair(ends[b], ends[3 + b], None)
    ends[6] = own

    def set_ends(b, one, two, amounts):
        if one is not None:
            set_push(one, True, pairs[b]["normal"], cross3(ends[one]["lever"], pairs[b]["normal"]), amounts)
        if two is not None:
            set_push(two, False, pairs[b]["normal"], cross3(ends[two]["lever"], pairs[b]["normal"]), amounts)

    wide = 12 * PARTS
    narrow = 6 * PARTS
    for b in range(3):
        set_ends(b, b, 3 + b, (pairs[b]["slope"], pairs[b]["down"]))
    both_units = (wide_0, wide_1)
    accumulate(both_units, 0, [loads_from(chunk, wide) for chunk in CHUNKS[:LOCAL_CHUNKS]])

    arrive(0)

    def repacked(ref, field, slot):
        for d in range(4):
            pk[slot, 2 * d : 2 * d + 2, :] = ref[d, 2 * field : 2 * field + 2, :]
        return pk[slot]

    def by_heading(row_of):
        out = row_of(0)
        for d in range(1, 4):
            out = jnp.where(heading8 == d, row_of(d), out)
        return out

    slot_in = repacked(recv_s, 0, 2).astype(I32)
    arc_in = repacked(recv_s, 1, 3)
    live_in = repacked(recv_s, 2, 4)
    index[7] = lanes_of(by_heading(lambda d: spread_rows(v_exp, d)), slot_in)
    set_keys(7)
    columns_beside(48, 56, 2)
    ends[7] = endpoint(picked(index[7], table_row, 13), arc_in)

    slot_own = unpacked(v_slot, pk_int, 1)
    arc_oth = unpacked(v_oth, pk, 6)
    arrive(1)
    far = [
        lanes_of(
            by_heading(lambda d, c=c: spread_rows(recv_e, c, d)), slot_own
        )
        for c in range(13)
    ]
    pairs[3] = pair(own, endpoint(far, arc_oth), live_own)
    set_ends(3, 6, None, (pairs[3]["slope"], pairs[3]["down"]))
    arrive(2)
    near = [repacked(recv_d, i, 7 + i) for i in range(7)]
    pairs[4] = pair(dict(at=near[0:3], radius=near[3], moving=near[4:7]), ends[7], live_in)
    set_ends(4, None, 7, (pairs[4]["slope"], pairs[4]["down"]))

    accumulate(both_units, LOCAL_CHUNKS, [loads_from(chunk, wide) for chunk in CHUNKS[LOCAL_CHUNKS:]])
    total = total_of(both_units)
    both = loads_of(total, 0) + loads_of(total, 1)
    moved_all = mobile(both[0:6])
    moved_down = mobile(both[6:12])
    for c in range(6):
        t_move[c] = moved_down[c]

    def folded(value):
        return jnp.sum(value, axis=0, keepdims=True)

    def halved(row):
        row = row + pltpu.roll(row, 64, 1)
        return row + pltpu.roll(row, 32, 1)

    def counted(name):
        value = pairs[0][name] * pairs[0][name] + pairs[1][name] * pairs[1][name]
        last = pairs[2][name] * pairs[2][name]
        return value + jnp.where(row8 >= 4, last, 0.0) + pairs[3][name] * pairs[3][name]

    def power(one, two):
        value = one[0] * two[0]
        for c in range(1, 6):
            value = value + one[c] * two[c]
        return value

    rows = [
        halved(folded(v))
        for v in (counted("slope"), power(both[0:6], moved_all), counted("down"), power(both[6:12], moved_down))
    ]
    quarter = lax.broadcasted_iota(I32, (1, 128), 1) // 32
    mine = rows[0]
    for i in range(1, 4):
        mine = jnp.where(quarter == i, rows[i], mine)
    sum_a[...] = mine

    def ring(src, dst, sems, slot, to):
        return pltpu.make_async_remote_copy(
            src_ref=src,
            dst_ref=dst.at[slot],
            send_sem=sems[0].at[0],
            recv_sem=sems[1].at[0],
            device_id=to,
            device_id_type=MESH,
        )

    def whole(dst, sems):
        return pltpu.make_async_remote_copy(
            src_ref=dst,
            dst_ref=dst,
            send_sem=sems[0].at[0],
            recv_sem=sems[1].at[0],
            device_id=place(0, 1),
            device_id_type=MESH,
        )

    for o in range(1, n_gy):
        ring(sum_a, got_a, (a_send, a_recv), o - 1, place(0, o)).start()

    def contact(e):
        values = picked(index[e], move_row, 6)
        turned = cross3(values[3:6], ends[e]["lever"])
        return [values[c] + turned[c] for c in range(3)]

    moved_own = contact(6)
    for c in range(3):
        for d in range(4):
            send_f[d, 2 * c : 2 * c + 2, :] = moved_own[c][2 * d : 2 * d + 2]
    launch(send_f, recv_f, 3, True)
    moved_in = contact(7)
    for c in range(3):
        for d in range(4):
            send_g[d, 2 * c : 2 * c + 2, :] = moved_in[c][2 * d : 2 * d + 2]
    launch(send_g, recv_g, 4, False)

    whole(got_a, (a_send, a_recv)).wait_recv()
    mine = sum_a[...]
    for o in range(1, n_gy):
        mine = mine + got_a[o - 1]
    sum_b[...] = mine
    pl.semaphore_wait(relay.at[0], n_z - 1)
    for o in range(1, n_gx):
        ring(sum_b, got_b, (b_send, b_recv), o - 1, plane(o % n_y, o // n_y)).start()

    def curve(b, one, two):
        return dot3(pairs[b]["normal"], [one[c] - two[c] for c in range(3)])

    curved = [None] * 5
    for b in range(3):
        curved[b] = curve(b, contact(b), contact(3 + b))
    arrive(3)
    arrive(4)
    curved[3] = curve(3, moved_own, [repacked(recv_g, c, c) for c in range(3)])
    curved[4] = curve(4, [repacked(recv_f, c, 3 + c) for c in range(3)], moved_in)

    whole(got_b, (b_send, b_recv)).wait_recv()
    mine = sum_b[...]
    for o in range(1, n_gx):
        mine = mine + got_b[o - 1]
    sums = [
        jnp.sum(jnp.where(quarter == i, mine, 0.0), axis=1, keepdims=True) for i in range(4)
    ]
    step_first = sums[0] / (sums[1] + TINY)
    square = step_first * step_first
    step_second = (square * sums[2]) / (square * sums[3] + TINY)
    step_first = jnp.broadcast_to(step_first, (8, 128))
    step_second = jnp.broadcast_to(step_second, (8, 128))

    force = []
    for b in range(5):
        thrust = step_first * pairs[b]["down"]
        slope = pairs[b]["slope"] + step_first * curved[b]
        force.append(jnp.maximum(0.0, thrust - step_second * slope))
    for b, start in enumerate(LOCAL_STARTS):
        o_fl[start : start + 8, :] = force[b]
    for d in range(4):
        for h in range(2):
            o_fc[d : d + 1, h * 128 : (h + 1) * 128] = force[3][2 * d + h : 2 * d + h + 1]
    for b in range(3):
        set_ends(b, b, 3 + b, (force[b],))
    set_ends(3, 6, None, (force[3],))
    set_ends(4, None, 7, (force[4],))
    both_units = (narrow_0, narrow_1)
    accumulate(both_units, 0, [loads_from(chunk, narrow) for chunk in CHUNKS])
    moved = mobile(loads_of(total_of(both_units), 0))
    for c in range(6):
        velocity = t_seg[3 + c] + moved[c]
        for r in range(16):
            o_vel[c : c + 1, r * 128 : (r + 1) * 128] = velocity[r : r + 1]
    whole(got_a, (a_send, a_recv)).wait_send()
    whole(got_b, (b_send, b_recv)).wait_send()
    for to_partner, copies in moves.values():
        for d in range(4):
            pl.when(has_partner[d] if to_partner else has_owner[d])(copies[d].wait_send)


def kernel_with_sums(*refs):
    sums = [pltpu.ACC(unit)((rows * PARTS, 256), F32) for rows in (96, 48) for unit in range(2)]
    pl.run_scoped(functools.partial(kernel, *refs), *sums)


def hand_out(vel, fl, fc, o_vel, o_fl, o_fc, sem):
    copies = [
        pltpu.make_async_copy(src, dst, sem.at[i])
        for i, (src, dst) in enumerate(((vel, o_vel), (fl, o_fl), (fc, o_fc)))
    ]
    for copy in copies:
        copy.start()
    for copy in copies:
        copy.wait()


def grid_y(n_gx):
    return max(k for k in range(1, n_gx + 1) if n_gx % k == 0 and k * k <= n_gx)


def on_device(n_gx, n_gy, cent, tilt, turn, rad, perp, axial, rot, load, lf, ls, a1, a2, mine, slot, own, oth, count, exports):
    segs = [v.reshape(16, 128) for v in (tilt, turn, rad, perp, axial, rot)]
    local = [v.reshape(20, 128) for v in (lf, ls, a1, a2)]
    cross = [v.reshape(4, 256) for v in (mine, slot, own, oth)]
    operands = [cent, *segs, load, *local, *cross, count, exports.reshape(4, 128)]
    anyspace = pl.BlockSpec(memory_space=pltpu.HBM)

    def held(v):
        return pltpu.VMEM(v.shape, v.dtype)

    inputs = [held(v) for v in operands]
    inputs[16] = pltpu.SMEM(count.shape, count.dtype)
    dma = pltpu.SemaphoreType.DMA
    scratch = inputs + [
        pltpu.VMEM((12, 16, 128), F32),
        pltpu.VMEM((6, 16, 128), F32),
        pltpu.VMEM((6, 16, 128), F32),
        pltpu.VMEM((14, 8, 128), F32),
        pltpu.VMEM((2, 8, 128), I32),
        pltpu.VMEM((8, 8, 128), F32),
        pltpu.VMEM((8, 8, 128), F32),
        pltpu.VMEM((12 * PARTS, 8, 8, 128), F32),
        pltpu.VMEM((len(CHUNKS), 256, 128), jnp.bfloat16),
        pltpu.VMEM((4, 8, 128), F32),
        pltpu.VMEM((4, 8, 128), F32),
        pltpu.VMEM((4, 16, 128), F32),
        pltpu.VMEM((4, 16, 128), F32),
        pltpu.VMEM((4, 16, 128), F32),
        pltpu.VMEM((4, 16, 128), F32),
        pltpu.VMEM((4, 8, 128), F32),
        pltpu.VMEM((4, 8, 128), F32),
        pltpu.VMEM((4, 8, 128), F32),
        pltpu.VMEM((4, 8, 128), F32),
        pltpu.VMEM((1, 128), F32),
        pltpu.VMEM((n_gy - 1, 1, 128), F32),
        pltpu.VMEM((1, 128), F32),
        pltpu.VMEM((n_gx - 1, 1, 128), F32),
        dma((18,)),
        dma((5, 4)),
        dma((5, 4)),
        dma((1,)),
        dma((1,)),
        dma((1,)),
        dma((1,)),
        pltpu.SemaphoreType.REGULAR((1,)),
    ]
    operands = [pltpu.with_memory_space_constraint(v, pltpu.HBM) for v in operands]
    outs = ((6, 2048), (20, 128), (4, 256))
    near = pl.BlockSpec(memory_space=pltpu.VMEM)
    solved = pl.pallas_call(
        functools.partial(kernel_with_sums, n_gx, n_gy),
        out_shape=tuple(pltpu.VMEM(shape, F32) for shape in outs),
        in_specs=[anyspace] * 18,
        out_specs=(near,) * 3,
        scratch_shapes=scratch,
        compiler_params=pltpu.CompilerParams(
            collective_id=0, has_side_effects=True, vmem_limit_bytes=48 * 1024 * 1024
        ),
    )(*operands)
    velocity, force_local, force_cross = pl.pallas_call(
        hand_out,
        out_shape=tuple(jax.ShapeDtypeStruct(shape, F32) for shape in outs),
        in_specs=[near] * 3,
        out_specs=(anyspace,) * 3,
        scratch_shapes=[dma((3,))],
        compiler_params=pltpu.CompilerParams(vmem_limit_bytes=1024 * 1024),
    )(*[pltpu.with_memory_space_constraint(v, pltpu.VMEM) for v in solved])
    return velocity, force_local.reshape(2560), force_cross.reshape(1, 4, 256)


def solution(mesh):
    both = ("gx", "gy")
    flat = P(both)
    wide = P(None, both)
    cube = P(both, None, None)
    return jax.shard_map(
        functools.partial(on_device, mesh.shape["gx"], mesh.shape["gy"]),
        mesh=mesh,
        in_specs=(wide, *[flat] * 6, wide, *[flat] * 4, *[cube] * 4, P(both, None), cube),
        out_specs=(wide, flat, cube),
        check_vma=False,
    )
```

```python
import functools

import jax
import jax.numpy as jnp
from jax import lax
from jax.experimental import pallas as pl
from jax.experimental.pallas import tpu as pltpu
from jax.sharding import PartitionSpec as P


F32 = jnp.float32
I32 = jnp.int32
STEP_TIME = 0.5
FLOOR_GAP = 0.25
TINY = 1e-06
PARTS = 2
OFFSETS = ((0, 1), (1, 1), (1, 0), (1, -1))
MESH = pl.DeviceIdType.MESH
LOCAL_STARTS = (0, 8, 12)
CHUNKS = (
    [(0, s) for s in range(8)]
    + [(1, s) for s in range(8)]
    + [(2, s) for s in range(4, 8)]
    + [(3, s) for s in range(8)]
    + [(4, s) for s in range(8)]
    + [(5, s) for s in range(4, 8)]
    + [(6, s) for s in range(8)]
    + [(7, s) for s in range(8)]
)
LOCAL_CHUNKS = 40
EARLY = 48


def cross3(a, b):
    return [a[1] * b[2] - a[2] * b[1], a[2] * b[0] - a[0] * b[2], a[0] * b[1] - a[1] * b[0]]


def dot3(a, b):
    return a[0] * b[0] + a[1] * b[1] + a[2] * b[2]


def lanes_of(table, index):
    return jnp.take_along_axis(table, index, axis=1, mode="promise_in_bounds")


def kernel(
    n_gx,
    n_gy,
    h_cent,
    h_tilt,
    h_turn,
    h_rad,
    h_perp,
    h_axial,
    h_rot,
    h_load,
    h_lf,
    h_ls,
    h_a1,
    h_a2,
    h_mine,
    h_slot,
    h_own,
    h_oth,
    h_count,
    h_exp,
    o_vel,
    o_fl,
    o_fc,
    v_cent,
    v_tilt,
    v_turn,
    v_rad,
    v_perp,
    v_axial,
    v_rot,
    v_load,
    v_lf,
    v_ls,
    v_a1,
    v_a2,
    v_mine,
    v_slot,
    v_own,
    v_oth,
    s_count,
    v_exp,
    t_seg,
    t_move,
    x_seg,
    pk,
    pk_int,
    key_hi,
    key_lo,
    push,
    o_mat,
    o_turned,
    key_rows,
    key_columns,
    turned,
    send_d,
    recv_d,
    send_e,
    recv_e,
    send_f,
    recv_f,
    send_g,
    recv_g,
    sum_a,
    got_a,
    sum_b,
    got_b,
    in_sem,
    ex_send,
    ex_recv,
    a_send,
    a_recv,
    b_send,
    b_recv,
    relay,
    wide_0,
    wide_1,
    narrow_0,
    narrow_1,
):
    gx = lax.axis_index("gx")
    gy = lax.axis_index("gy")

    def place(dx, dy):
        return (lax.rem(gx + (dx + n_gx), n_gx), lax.rem(gy + (dy + n_gy), n_gy))

    n_y = grid_y(n_gx)
    n_z = n_gx // n_y
    at_y, at_z = lax.rem(gx, n_y), gx // n_y

    def plane(oy, oz):
        return (lax.rem(at_z + oz, n_z) * n_y + lax.rem(at_y + oy, n_y), gy)

    def inside(dx, dy):
        row, column = gx + dx, gy + dy
        return (row >= 0) & (row < n_gx) & (column >= 0) & (column < n_gy)

    has_partner = [inside(dx, dy) for dx, dy in OFFSETS]
    has_owner = [inside(-dx, -dy) for dx, dy in OFFSETS]

    sources = (h_cent, h_tilt, h_turn, h_rad, h_perp, h_axial, h_rot, h_load, h_lf, h_ls, h_a1, h_a2, h_mine, h_slot, h_own, h_oth, h_count, h_exp)
    targets = (v_cent, v_tilt, v_turn, v_rad, v_perp, v_axial, v_rot, v_load, v_lf, v_ls, v_a1, v_a2, v_mine, v_slot, v_own, v_oth, s_count, v_exp)
    loads_in = {}
    for i in (1, 2, 7, 4, 5, 6, 13, 15, 16, 17, 12, 14, 0, 3, 8, 9, 10, 11):
        loads_in[i] = pltpu.make_async_copy(sources[i], targets[i], in_sem.at[i])
        loads_in[i].start()

    barrier = pltpu.get_barrier_semaphore()

    def greet(to):
        pl.semaphore_signal(barrier, inc=1, device_id=to, device_id_type=MESH)

    greetings = (n_gy - 1) + (n_y - 1) + (n_z - 1)
    for d in (1, 2, 3):
        dx, dy = OFFSETS[d]
        pl.when(has_partner[d])(functools.partial(greet, place(dx, dy)))
        pl.when(has_owner[d])(functools.partial(greet, place(-dx, -dy)))
        greetings = greetings + has_partner[d].astype(I32) + has_owner[d].astype(I32)
    for o in range(1, n_gy):
        greet(place(0, o))
    for o in range(1, n_y):
        greet(plane(o, 0))
    for o in range(1, n_z):
        greet(plane(0, o))

    def need(*which):
        for i in which:
            loads_in[i].wait()

    row8 = lax.broadcasted_iota(I32, (8, 128), 0)
    lane8 = lax.broadcasted_iota(I32, (8, 128), 1)
    heading8 = row8 // 2
    zero8 = jnp.zeros((8, 128), F32)

    def spread_rows(ref, row, *lead):
        return ref[(*lead, pl.ds(row, 8, stride=0), slice(None))]

    need(1, 2)
    lifted = jnp.sin(v_tilt[...])
    tangent = [lifted * jnp.cos(v_turn[...]), lifted * jnp.sin(v_turn[...]), jnp.cos(v_tilt[...])]
    need(7, 4, 5, 6)
    for c in range(6):
        for r in range(16):
            x_seg[c, r : r + 1, :] = v_load[c : c + 1, r * 128 : (r + 1) * 128]

    def mobile(applied):
        along = dot3(tangent, applied)
        pulled = v_axial[...] * along
        return [v_perp[...] * applied[c] + pulled * tangent[c] for c in range(3)] + [
            v_rot[...] * applied[3 + c] for c in range(3)
        ]

    drift = mobile([x_seg[c] for c in range(6)])
    for c in range(3):
        t_seg[c] = tangent[c]
    for c in range(6):
        t_seg[3 + c] = drift[c]

    def unpacked(ref, into, field):
        for d in range(4):
            for h in range(2):
                into[field, 2 * d + h : 2 * d + h + 1, :] = ref[d : d + 1, h * 128 : (h + 1) * 128]
        return into[field]

    need(13, 15, 16)
    for d in range(4):
        for h in range(2):
            piece = slice(h * 128, (h + 1) * 128)
            send_d[d, 16 + h : 17 + h, :] = v_slot[d : d + 1, piece].astype(F32)
            send_d[d, 18 + h : 19 + h, :] = v_oth[d : d + 1, piece]
    live_own = zero8
    for d in range(4):
        bound = s_count[0, d]
        live_own = jnp.where(
            (heading8 == d) & ((row8 - 2 * d) * 128 + lane8 < bound), 1.0, live_own
        )
    for d in range(4):
        send_d[d, 20:22, :] = live_own[2 * d : 2 * d + 2]

    def blank(refs, d):
        for ref in refs:
            ref[d] = jnp.zeros(ref.shape[1:], F32)

    for d in range(4):
        pl.when(~has_partner[d])(functools.partial(blank, (recv_e, recv_g), d))
        pl.when(~has_owner[d])(functools.partial(blank, (recv_d, recv_f), d))

    partner = [place(dx, dy) for dx, dy in OFFSETS]
    owner = [place(-dx, -dy) for dx, dy in OFFSETS]
    moves = {}

    def launch(src, dst, step, to_partner):
        moves[step] = to_partner, []
        for d in range(4):
            copy = pltpu.make_async_remote_copy(
                src_ref=src.at[d],
                dst_ref=dst.at[d],
                send_sem=ex_send.at[step, d],
                recv_sem=ex_recv.at[step, d],
                device_id=partner[d] if to_partner else owner[d],
                device_id_type=MESH,
            )
            moves[step][1].append(copy)
            pl.when(has_partner[d] if to_partner else has_owner[d])(copy.start)

    def arrive(step):
        to_partner, copies = moves[step]
        for d in range(4):
            pl.when(has_owner[d] if to_partner else has_partner[d])(copies[d].wait_recv)


    need(0, 3)
    for c in range(3):
        for r in range(16):
            t_seg[9 + c, r : r + 1, :] = v_cent[c : c + 1, r * 128 : (r + 1) * 128]

    def table_row(c, r):
        if c < 3:
            return spread_rows(t_seg, r, 9 + c)
        if c == 3:
            return spread_rows(v_rad, r)
        return spread_rows(t_seg, r, c - 4)

    def move_row(c, r):
        return spread_rows(t_move, r, c)

    beside = []

    def picked(index, row_of, count):
        block = index >> 7
        lane = index & 127
        out = [None] * count
        for r in range(16):
            here = block == r
            for c in range(count):
                taken = lanes_of(row_of(c, r), lane)
                out[c] = taken if r == 0 else jnp.where(here, taken, out[c])
            if beside:
                beside.pop(0)()
        return out

    def endpoint(values, arc):
        lever = [arc * values[4 + c] for c in range(3)]
        place_of = [values[c] + lever[c] for c in range(3)]
        turned = cross3(values[10:13], lever)
        moving = [values[7 + c] + turned[c] for c in range(3)]
        return dict(lever=lever, at=place_of, radius=values[3], moving=moving)

    need(17)
    exports = v_exp[...]
    offered = picked(jnp.concatenate([exports, exports], axis=0), table_row, 13)
    for d in range(4):
        for c in range(13):
            send_e[d, c : c + 1, :] = offered[c][d : d + 1]

    need(12, 14)
    index = [None] * 8
    index[6] = unpacked(v_mine, pk_int, 0)
    arc_own = unpacked(v_own, pk, 1)
    own = endpoint(picked(index[6], table_row, 13), arc_own)
    for i, value in enumerate(own["at"] + [own["radius"]] + own["moving"]):
        for d in range(4):
            send_d[d, 2 * i : 2 * i + 2, :] = value[2 * d : 2 * d + 2]
    pl.semaphore_wait(barrier, greetings)
    for o in range(1, n_z):
        pl.semaphore_signal(relay.at[0], inc=1, device_id=plane(0, o), device_id_type=MESH)

    launch(send_e, recv_e, 0, False)
    launch(send_d, recv_d, 1, True)

    def pair(one, two, live):
        apart = [one["at"][c] - two["at"][c] for c in range(3)]
        spacing = jnp.sqrt(dot3(apart, apart))
        scale = 1.0 / jnp.maximum(spacing, FLOOR_GAP)
        if live is not None:
            scale = scale * live
        normal = [a * scale for a in apart]
        clearance = spacing - one["radius"] - two["radius"]
        if live is not None:
            clearance = clearance * live
        rate = dot3(normal, [one["moving"][c] - two["moving"][c] for c in range(3)])
        slope = clearance * (1.0 / STEP_TIME) + rate
        return dict(normal=normal, slope=slope, down=jnp.maximum(0.0, -slope))

    def split(value):
        pieces = []
        for _ in range(PARTS):
            piece = value.astype(jnp.bfloat16).astype(F32)
            pieces.append(piece)
            value = value - piece
        return pieces

    def set_keys(e):
        key_hi[e] = ((index[e] >> 7) & 7).astype(F32)
        key_lo[e] = (((index[e] >> 10) << 7) | (index[e] & 127)).astype(F32)

    def tall_row(first, second):
        return jnp.concatenate([first, second], axis=0).astype(jnp.bfloat16)

    low = [
        tall_row(row8.astype(F32) + float(k), row8.astype(F32) + float(k + 8)) for k in range(0, 256, 16)
    ]
    high = tall_row(row8.astype(F32), row8.astype(F32))
    one16 = jnp.ones((16, 128), jnp.bfloat16)
    none16 = jnp.zeros((16, 128), jnp.bfloat16)

    def set_push(e, first, normal, arm, amounts):
        sign = 1.0 if first else -1.0
        for i, amount in enumerate(amounts):
            scaled = amount * sign
            for c in range(6):
                value = scaled * (normal[c] if c < 3 else arm[c - 3])
                for p, piece in enumerate(split(value)):
                    push[(i * PARTS + p) * 6 + c, e] = piece

    lanes = [
        tall_row((lane8 + 128 * h).astype(F32), (lane8 + 128 * h).astype(F32)) for h in range(2)
    ]

    def turn_keys():
        for n, (e, s) in enumerate(CHUNKS[:EARLY]):
            key_rows[n : n + 1, :] = key_lo[e, s : s + 1, :]
        key_rows[EARLY:, :] = jnp.zeros((128 - EARLY, 128), F32)
        key_columns[...] = jnp.transpose(key_rows[...])

    def set_columns(n):
        if n < EARLY:
            for k in range(0, 128, 16):
                key = jnp.broadcast_to(key_columns[k : k + 16, n : n + 1], (16, 128)).astype(jnp.bfloat16)
                for h in range(2):
                    o_turned[n, h, k : k + 16, :] = jnp.where(lanes[h] == key, one16, none16)
            return
        e, s = CHUNKS[n]
        key = spread_rows(key_lo, s, e)
        key = tall_row(key, key)
        for k in range(0, 256, 16):
            o_mat[n - EARLY, k : k + 16, :] = jnp.where(low[k // 16] == key, one16, none16)

    def columns_beside(first, last, every):
        for n in range(first, last):
            beside.append(functools.partial(set_columns, n))
            beside.extend([lambda: None] * (every - 1))

    def loads_from(chunk, count):
        e, s = chunk
        key = spread_rows(key_hi, s, e)
        here = high == tall_row(key, key)
        out = []
        for k in range(0, count, 2):
            value = tall_row(spread_rows(push, s, k, e), spread_rows(push, s, k + 1, e))
            out.append(jnp.where(here, value, none16))
        return out

    def accumulate(into, start, rows):
        for n in range(0, len(rows), 2):
            unit = (start + n) // 2 % 2
            stage = (start + n) // 4 % 2
            if start + n < EARLY:
                tile = [
                    jnp.concatenate([o_turned[at, 0], o_turned[at, 1]], axis=1)
                    for at in (start + n, start + n + 1)
                ]
                tile = jnp.concatenate(tile, axis=0)
            else:
                at = start + n - EARLY
                tile = jnp.concatenate([o_mat[at], o_mat[at + 1]], axis=1)
            pltpu.matmul_push_rhs(
                tile, staging_register=stage, mxu_index=unit, transpose=start + n >= EARLY
            )
            left = [jnp.concatenate(r, axis=0) for r in rows[n : n + 2]]
            pltpu.matmul_acc_lhs(into[unit], jnp.concatenate(left, axis=1), load_staged_rhs=stage)

    def total_of(into):
        return pltpu.matmul_pop(into[0]) + pltpu.matmul_pop(into[1])

    def loads_of(total, group):
        out = []
        for c in range(6):
            value = None
            for p in reversed(range(PARTS)):
                at = ((group * PARTS + p) * 6 + c) * 8
                piece = jnp.concatenate([total[at : at + 8, 0:128], total[at : at + 8, 128:256]], axis=0)
                value = piece if value is None else value + piece
            out.append(value)
        return out

    need(8, 9, 10, 11)
    pairs = [None] * 5
    ends = [None] * 8
    for b, start in enumerate(LOCAL_STARTS):
        index[b] = v_lf[start : start + 8, :]
        index[3 + b] = v_ls[start : start + 8, :]
        set_keys(b)
        set_keys(3 + b)
    set_keys(6)
    turn_keys()
    columns_beside(0, EARLY, 2)
    for b, start in enumerate(LOCAL_STARTS):
        ends[b] = endpoint(picked(index[b], table_row, 13), v_a1[start : start + 8, :])
        ends[3 + b] = endpoint(picked(index[3 + b], table_row, 13), v_a2[start : start + 8, :])
        pairs[b] = pair(ends[b], ends[3 + b], None)
    ends[6] = own

    def set_ends(b, one, two, amounts):
        if one is not None:
            set_push(one, True, pairs[b]["normal"], cross3(ends[one]["lever"], pairs[b]["normal"]), amounts)
        if two is not None:
            set_push(two, False, pairs[b]["normal"], cross3(ends[two]["lever"], pairs[b]["normal"]), amounts)

    wide = 12 * PARTS
    narrow = 6 * PARTS
    for b in range(3):
        set_ends(b, b, 3 + b, (pairs[b]["slope"], pairs[b]["down"]))
    both_units = (wide_0, wide_1)
    accumulate(both_units, 0, [loads_from(chunk, wide) for chunk in CHUNKS[:LOCAL_CHUNKS]])

    arrive(0)
    arrive(1)

    def repacked(ref, field, slot):
        for d in range(4):
            pk[slot, 2 * d : 2 * d + 2, :] = ref[d, 2 * field : 2 * field + 2, :]
        return pk[slot]

    def by_heading(row_of):
        out = row_of(0)
        for d in range(1, 4):
            out = jnp.where(heading8 == d, row_of(d), out)
        return out

    slot_in = repacked(recv_d, 8, 2).astype(I32)
    arc_in = repacked(recv_d, 9, 3)
    live_in = repacked(recv_d, 10, 4)
    index[7] = lanes_of(by_heading(lambda d: spread_rows(v_exp, d)), slot_in)
    set_keys(7)
    columns_beside(EARLY, len(CHUNKS), 2)
    ends[7] = endpoint(picked(index[7], table_row, 13), arc_in)

    slot_own = unpacked(v_slot, pk_int, 1)
    arc_oth = unpacked(v_oth, pk, 6)
    far = [
        lanes_of(
            by_heading(lambda d, c=c: spread_rows(recv_e, c, d)), slot_own
        )
        for c in range(13)
    ]
    pairs[3] = pair(own, endpoint(far, arc_oth), live_own)
    set_ends(3, 6, None, (pairs[3]["slope"], pairs[3]["down"]))
    near = [repacked(recv_d, i, 7 + i) for i in range(7)]
    pairs[4] = pair(dict(at=near[0:3], radius=near[3], moving=near[4:7]), ends[7], live_in)
    set_ends(4, None, 7, (pairs[4]["slope"], pairs[4]["down"]))

    accumulate(both_units, LOCAL_CHUNKS, [loads_from(chunk, wide) for chunk in CHUNKS[LOCAL_CHUNKS:]])
    total = total_of(both_units)
    both = loads_of(total, 0) + loads_of(total, 1)
    moved_all = mobile(both[0:6])
    moved_down = mobile(both[6:12])
    for c in range(6):
        t_move[c] = moved_down[c]

    def folded(value):
        return jnp.sum(value, axis=0, keepdims=True)

    def halved(row):
        row = row + pltpu.roll(row, 64, 1)
        return row + pltpu.roll(row, 32, 1)

    def counted(name):
        value = pairs[0][name] * pairs[0][name] + pairs[1][name] * pairs[1][name]
        last = pairs[2][name] * pairs[2][name]
        return value + jnp.where(row8 >= 4, last, 0.0) + pairs[3][name] * pairs[3][name]

    def power(one, two):
        value = one[0] * two[0]
        for c in range(1, 6):
            value = value + one[c] * two[c]
        return value

    rows = [
        halved(folded(v))
        for v in (counted("slope"), power(both[0:6], moved_all), counted("down"), power(both[6:12], moved_down))
    ]
    quarter = lax.broadcasted_iota(I32, (1, 128), 1) // 32
    mine = rows[0]
    for i in range(1, 4):
        mine = jnp.where(quarter == i, rows[i], mine)
    sum_a[...] = mine

    def ring(src, dst, sems, slot, to):
        return pltpu.make_async_remote_copy(
            src_ref=src,
            dst_ref=dst.at[slot],
            send_sem=sems[0].at[0],
            recv_sem=sems[1].at[0],
            device_id=to,
            device_id_type=MESH,
        )

    def whole(dst, sems):
        return pltpu.make_async_remote_copy(
            src_ref=dst,
            dst_ref=dst,
            send_sem=sems[0].at[0],
            recv_sem=sems[1].at[0],
            device_id=place(0, 1),
            device_id_type=MESH,
        )

    for o in range(1, n_gy):
        ring(sum_a, got_a, (a_send, a_recv), o - 1, place(0, o)).start()

    def contact(e):
        values = picked(index[e], move_row, 6)
        turned = cross3(values[3:6], ends[e]["lever"])
        return [values[c] + turned[c] for c in range(3)]

    moved_own = contact(6)
    for c in range(3):
        for d in range(4):
            send_f[d, 2 * c : 2 * c + 2, :] = moved_own[c][2 * d : 2 * d + 2]
    launch(send_f, recv_f, 2, True)
    moved_in = contact(7)
    for c in range(3):
        for d in range(4):
            send_g[d, 2 * c : 2 * c + 2, :] = moved_in[c][2 * d : 2 * d + 2]
    launch(send_g, recv_g, 3, False)

    whole(got_a, (a_send, a_recv)).wait_recv()
    mine = sum_a[...]
    for o in range(1, n_gy):
        mine = mine + got_a[o - 1]
    sum_b[...] = mine
    pl.semaphore_wait(relay.at[0], n_z - 1)
    for o in range(1, n_gx):
        ring(sum_b, got_b, (b_send, b_recv), o - 1, plane(o % n_y, o // n_y)).start()

    def curve(b, one, two):
        return dot3(pairs[b]["normal"], [one[c] - two[c] for c in range(3)])

    curved = [None] * 5
    for b in range(3):
        curved[b] = curve(b, contact(b), contact(3 + b))
    arrive(2)
    arrive(3)
    curved[3] = curve(3, moved_own, [repacked(recv_g, c, c) for c in range(3)])
    curved[4] = curve(4, [repacked(recv_f, c, 3 + c) for c in range(3)], moved_in)

    whole(got_b, (b_send, b_recv)).wait_recv()
    mine = sum_b[...]
    for o in range(1, n_gx):
        mine = mine + got_b[o - 1]
    sums = [
        jnp.sum(jnp.where(quarter == i, mine, 0.0), axis=1, keepdims=True) for i in range(4)
    ]
    step_first = sums[0] / (sums[1] + TINY)
    square = step_first * step_first
    step_second = (square * sums[2]) / (square * sums[3] + TINY)
    step_first = jnp.broadcast_to(step_first, (8, 128))
    step_second = jnp.broadcast_to(step_second, (8, 128))

    force = []
    for b in range(5):
        thrust = step_first * pairs[b]["down"]
        slope = pairs[b]["slope"] + step_first * curved[b]
        force.append(jnp.maximum(0.0, thrust - step_second * slope))
    for b, start in enumerate(LOCAL_STARTS):
        o_fl[start : start + 8, :] = force[b]
    for d in range(4):
        for h in range(2):
            o_fc[d : d + 1, h * 128 : (h + 1) * 128] = force[3][2 * d + h : 2 * d + h + 1]
    for b in range(3):
        set_ends(b, b, 3 + b, (force[b],))
    set_ends(3, 6, None, (force[3],))
    set_ends(4, None, 7, (force[4],))
    both_units = (narrow_0, narrow_1)
    accumulate(both_units, 0, [loads_from(chunk, narrow) for chunk in CHUNKS])
    moved = mobile(loads_of(total_of(both_units), 0))
    for c in range(6):
        velocity = t_seg[3 + c] + moved[c]
        for j in range(2):
            turned[j, c * 8 : c * 8 + 8, :] = velocity[j * 8 : j * 8 + 8]
    for r in range(16):
        o_vel[:, r * 128 : (r + 1) * 128] = turned[r // 8, pl.ds(r % 8, 8, stride=8), :][0:6]
    whole(got_a, (a_send, a_recv)).wait_send()
    whole(got_b, (b_send, b_recv)).wait_send()
    for to_partner, copies in moves.values():
        for d in range(4):
            pl.when(has_partner[d] if to_partner else has_owner[d])(copies[d].wait_send)


def kernel_with_sums(*refs):
    sums = [pltpu.ACC(unit)((rows * PARTS, 256), F32) for rows in (96, 48) for unit in range(2)]
    pl.run_scoped(functools.partial(kernel, *refs), *sums)


def hand_out(vel, fl, fc, o_vel, o_fl, o_fc, sem):
    copies = [
        pltpu.make_async_copy(src, dst, sem.at[i])
        for i, (src, dst) in enumerate(((vel, o_vel), (fl, o_fl), (fc, o_fc)))
    ]
    for copy in copies:
        copy.start()
    for copy in copies:
        copy.wait()


def grid_y(n_gx):
    return max(k for k in range(1, n_gx + 1) if n_gx % k == 0 and k * k <= n_gx)


def on_device(n_gx, n_gy, cent, tilt, turn, rad, perp, axial, rot, load, lf, ls, a1, a2, mine, slot, own, oth, count, exports):
    segs = [v.reshape(16, 128) for v in (tilt, turn, rad, perp, axial, rot)]
    local = [v.reshape(20, 128) for v in (lf, ls, a1, a2)]
    cross = [v.reshape(4, 256) for v in (mine, slot, own, oth)]
    operands = [cent, *segs, load, *local, *cross, count, exports.reshape(4, 128)]
    anyspace = pl.BlockSpec(memory_space=pltpu.HBM)

    def held(v):
        return pltpu.VMEM(v.shape, v.dtype)

    inputs = [held(v) for v in operands]
    inputs[16] = pltpu.SMEM(count.shape, count.dtype)
    dma = pltpu.SemaphoreType.DMA
    scratch = inputs + [
        pltpu.VMEM((12, 16, 128), F32),
        pltpu.VMEM((6, 16, 128), F32),
        pltpu.VMEM((6, 16, 128), F32),
        pltpu.VMEM((14, 8, 128), F32),
        pltpu.VMEM((2, 8, 128), I32),
        pltpu.VMEM((8, 8, 128), F32),
        pltpu.VMEM((8, 8, 128), F32),
        pltpu.VMEM((12 * PARTS, 8, 8, 128), F32),
        pltpu.VMEM((len(CHUNKS) - EARLY, 256, 128), jnp.bfloat16),
        pltpu.VMEM((EARLY, 2, 128, 128), jnp.bfloat16),
        pltpu.VMEM((128, 128), F32),
        pltpu.VMEM((128, 128), F32),
        pltpu.VMEM((2, 64, 128), F32),
        pltpu.VMEM((4, 24, 128), F32),
        pltpu.VMEM((4, 24, 128), F32),
        pltpu.VMEM((4, 16, 128), F32),
        pltpu.VMEM((4, 16, 128), F32),
        pltpu.VMEM((4, 8, 128), F32),
        pltpu.VMEM((4, 8, 128), F32),
        pltpu.VMEM((4, 8, 128), F32),
        pltpu.VMEM((4, 8, 128), F32),
        pltpu.VMEM((1, 128), F32),
        pltpu.VMEM((n_gy - 1, 1, 128), F32),
        pltpu.VMEM((1, 128), F32),
        pltpu.VMEM((n_gx - 1, 1, 128), F32),
        dma((18,)),
        dma((4, 4)),
        dma((4, 4)),
        dma((1,)),
        dma((1,)),
        dma((1,)),
        dma((1,)),
        pltpu.SemaphoreType.REGULAR((1,)),
    ]
    operands = [pltpu.with_memory_space_constraint(v, pltpu.HBM) for v in operands]
    outs = ((6, 2048), (20, 128), (4, 256))
    near = pl.BlockSpec(memory_space=pltpu.VMEM)
    solved = pl.pallas_call(
        functools.partial(kernel_with_sums, n_gx, n_gy),
        out_shape=tuple(pltpu.VMEM(shape, F32) for shape in outs),
        in_specs=[anyspace] * 18,
        out_specs=(near,) * 3,
        scratch_shapes=scratch,
        compiler_params=pltpu.CompilerParams(
            collective_id=0, has_side_effects=True, vmem_limit_bytes=48 * 1024 * 1024
        ),
    )(*operands)
    velocity, force_local, force_cross = pl.pallas_call(
        hand_out,
        out_shape=tuple(jax.ShapeDtypeStruct(shape, F32) for shape in outs),
        in_specs=[near] * 3,
        out_specs=(anyspace,) * 3,
        scratch_shapes=[dma((3,))],
        compiler_params=pltpu.CompilerParams(vmem_limit_bytes=1024 * 1024),
    )(*[pltpu.with_memory_space_constraint(v, pltpu.VMEM) for v in solved])
    return velocity, force_local.reshape(2560), force_cross.reshape(1, 4, 256)


def solution(mesh):
    both = ("gx", "gy")
    flat = P(both)
    wide = P(None, both)
    cube = P(both, None, None)
    return jax.shard_map(
        functools.partial(on_device, mesh.shape["gx"], mesh.shape["gy"]),
        mesh=mesh,
        in_specs=(wide, *[flat] * 6, wide, *[flat] * 4, *[cube] * 4, P(both, None), cube),
        out_specs=(wide, flat, cube),
        check_vma=False,
    )
```

```python
import functools

import jax
import jax.numpy as jnp
from jax import lax
from jax.experimental import pallas as pl
from jax.experimental.pallas import tpu as pltpu
from jax.sharding import PartitionSpec as P


F32 = jnp.float32
I32 = jnp.int32
STEP_TIME = 0.5
FLOOR_GAP = 0.25
TINY = 1e-06
PARTS = 2
OFFSETS = ((0, 1), (1, 1), (1, 0), (1, -1))
MESH = pl.DeviceIdType.MESH
LOCAL_STARTS = (0, 8, 12)
CHUNKS = (
    [(0, s) for s in range(8)]
    + [(1, s) for s in range(8)]
    + [(2, s) for s in range(4, 8)]
    + [(3, s) for s in range(8)]
    + [(4, s) for s in range(8)]
    + [(5, s) for s in range(4, 8)]
    + [(6, s) for s in range(8)]
    + [(7, s) for s in range(8)]
)
LOCAL_CHUNKS = 40
EARLY = 48


def cross3(a, b):
    return [a[1] * b[2] - a[2] * b[1], a[2] * b[0] - a[0] * b[2], a[0] * b[1] - a[1] * b[0]]


def dot3(a, b):
    return a[0] * b[0] + a[1] * b[1] + a[2] * b[2]


def lanes_of(table, index):
    return jnp.take_along_axis(table, index, axis=1, mode="promise_in_bounds")


def kernel(
    n_gx,
    n_gy,
    h_cent,
    h_tilt,
    h_turn,
    h_rad,
    h_perp,
    h_axial,
    h_rot,
    h_load,
    h_lf,
    h_ls,
    h_a1,
    h_a2,
    h_mine,
    h_slot,
    h_own,
    h_oth,
    h_count,
    h_exp,
    o_vel,
    o_fl,
    o_fc,
    v_cent,
    v_tilt,
    v_turn,
    v_rad,
    v_perp,
    v_axial,
    v_rot,
    v_load,
    v_lf,
    v_ls,
    v_a1,
    v_a2,
    v_mine,
    v_slot,
    v_own,
    v_oth,
    s_count,
    v_exp,
    t_seg,
    t_move,
    x_seg,
    pk,
    pk_int,
    key_hi,
    key_lo,
    push,
    o_mat,
    o_turned,
    key_rows,
    key_columns,
    turned,
    send_d,
    recv_d,
    send_e,
    recv_e,
    send_f,
    recv_f,
    send_g,
    recv_g,
    sum_a,
    got_a,
    in_sem,
    ex_send,
    ex_recv,
    a_send,
    a_recv,
    relay,
    wide_0,
    wide_1,
    narrow_0,
    narrow_1,
):
    gx = lax.axis_index("gx")
    gy = lax.axis_index("gy")

    def place(dx, dy):
        return (lax.rem(gx + (dx + n_gx), n_gx), lax.rem(gy + (dy + n_gy), n_gy))

    n_y = grid_y(n_gx)
    n_z = n_gx // n_y
    at_y, at_z = lax.rem(gx, n_y), gx // n_y

    def plane(oy, oz):
        return (lax.rem(at_z + oz, n_z) * n_y + lax.rem(at_y + oy, n_y), gy)

    def inside(dx, dy):
        row, column = gx + dx, gy + dy
        return (row >= 0) & (row < n_gx) & (column >= 0) & (column < n_gy)

    has_partner = [inside(dx, dy) for dx, dy in OFFSETS]
    has_owner = [inside(-dx, -dy) for dx, dy in OFFSETS]

    sources = (h_cent, h_tilt, h_turn, h_rad, h_perp, h_axial, h_rot, h_load, h_lf, h_ls, h_a1, h_a2, h_mine, h_slot, h_own, h_oth, h_count, h_exp)
    targets = (v_cent, v_tilt, v_turn, v_rad, v_perp, v_axial, v_rot, v_load, v_lf, v_ls, v_a1, v_a2, v_mine, v_slot, v_own, v_oth, s_count, v_exp)
    loads_in = {}
    for i in (1, 2, 7, 4, 5, 6, 13, 15, 16, 17, 12, 14, 0, 3, 8, 9, 10, 11):
        loads_in[i] = pltpu.make_async_copy(sources[i], targets[i], in_sem.at[i])
        loads_in[i].start()

    barrier = pltpu.get_barrier_semaphore()

    def greet(to):
        pl.semaphore_signal(barrier, inc=1, device_id=to, device_id_type=MESH)

    greetings = (n_gy - 1) + (n_y - 1) + (n_z - 1)
    for d in (1, 2, 3):
        dx, dy = OFFSETS[d]
        pl.when(has_partner[d])(functools.partial(greet, place(dx, dy)))
        pl.when(has_owner[d])(functools.partial(greet, place(-dx, -dy)))
        greetings = greetings + has_partner[d].astype(I32) + has_owner[d].astype(I32)
    for o in range(1, n_gy):
        greet(place(0, o))
    for o in range(1, n_y):
        greet(plane(o, 0))
    for o in range(1, n_z):
        greet(plane(0, o))

    def need(*which):
        for i in which:
            loads_in[i].wait()

    row8 = lax.broadcasted_iota(I32, (8, 128), 0)
    lane8 = lax.broadcasted_iota(I32, (8, 128), 1)
    heading8 = row8 // 2
    zero8 = jnp.zeros((8, 128), F32)

    def spread_rows(ref, row, *lead):
        return ref[(*lead, pl.ds(row, 8, stride=0), slice(None))]

    need(1, 2)
    lifted = jnp.sin(v_tilt[...])
    tangent = [lifted * jnp.cos(v_turn[...]), lifted * jnp.sin(v_turn[...]), jnp.cos(v_tilt[...])]
    need(7, 4, 5, 6)
    for c in range(6):
        for r in range(16):
            x_seg[c, r : r + 1, :] = v_load[c : c + 1, r * 128 : (r + 1) * 128]

    def mobile(applied):
        along = dot3(tangent, applied)
        pulled = v_axial[...] * along
        return [v_perp[...] * applied[c] + pulled * tangent[c] for c in range(3)] + [
            v_rot[...] * applied[3 + c] for c in range(3)
        ]

    drift = mobile([x_seg[c] for c in range(6)])
    for c in range(3):
        t_seg[c] = tangent[c]
    for c in range(6):
        t_seg[3 + c] = drift[c]

    def unpacked(ref, into, field):
        for d in range(4):
            for h in range(2):
                into[field, 2 * d + h : 2 * d + h + 1, :] = ref[d : d + 1, h * 128 : (h + 1) * 128]
        return into[field]

    need(13, 15, 16)
    for d in range(4):
        for h in range(2):
            piece = slice(h * 128, (h + 1) * 128)
            send_d[d, 16 + h : 17 + h, :] = v_slot[d : d + 1, piece].astype(F32)
            send_d[d, 18 + h : 19 + h, :] = v_oth[d : d + 1, piece]
    live_own = zero8
    for d in range(4):
        bound = s_count[0, d]
        live_own = jnp.where(
            (heading8 == d) & ((row8 - 2 * d) * 128 + lane8 < bound), 1.0, live_own
        )
    for d in range(4):
        send_d[d, 20:22, :] = live_own[2 * d : 2 * d + 2]

    def blank(refs, d):
        for ref in refs:
            ref[d] = jnp.zeros(ref.shape[1:], F32)

    for d in range(4):
        pl.when(~has_partner[d])(functools.partial(blank, (recv_e, recv_g), d))
        pl.when(~has_owner[d])(functools.partial(blank, (recv_d, recv_f), d))

    partner = [place(dx, dy) for dx, dy in OFFSETS]
    owner = [place(-dx, -dy) for dx, dy in OFFSETS]
    moves = {}

    def launch(src, dst, step, to_partner):
        moves[step] = to_partner, []
        for d in range(4):
            copy = pltpu.make_async_remote_copy(
                src_ref=src.at[d],
                dst_ref=dst.at[d],
                send_sem=ex_send.at[step, d],
                recv_sem=ex_recv.at[step, d],
                device_id=partner[d] if to_partner else owner[d],
                device_id_type=MESH,
            )
            moves[step][1].append(copy)
            pl.when(has_partner[d] if to_partner else has_owner[d])(copy.start)

    def arrive(step):
        to_partner, copies = moves[step]
        for d in range(4):
            pl.when(has_owner[d] if to_partner else has_partner[d])(copies[d].wait_recv)


    need(0, 3)
    for c in range(3):
        for r in range(16):
            t_seg[9 + c, r : r + 1, :] = v_cent[c : c + 1, r * 128 : (r + 1) * 128]

    def table_row(c, r):
        if c < 3:
            return spread_rows(t_seg, r, 9 + c)
        if c == 3:
            return spread_rows(v_rad, r)
        return spread_rows(t_seg, r, c - 4)

    def move_row(c, r):
        return spread_rows(t_move, r, c)

    beside = []

    def picked(index, row_of, count):
        block = index >> 7
        lane = index & 127
        out = [None] * count
        for r in range(16):
            here = block == r
            for c in range(count):
                taken = lanes_of(row_of(c, r), lane)
                out[c] = taken if r == 0 else jnp.where(here, taken, out[c])
            if beside:
                beside.pop(0)()
        return out

    def endpoint(values, arc):
        lever = [arc * values[4 + c] for c in range(3)]
        place_of = [values[c] + lever[c] for c in range(3)]
        turned = cross3(values[10:13], lever)
        moving = [values[7 + c] + turned[c] for c in range(3)]
        return dict(lever=lever, at=place_of, radius=values[3], moving=moving)

    need(17)
    exports = v_exp[...]
    offered = picked(jnp.concatenate([exports, exports], axis=0), table_row, 13)
    for d in range(4):
        for c in range(13):
            send_e[d, c : c + 1, :] = offered[c][d : d + 1]

    need(12, 14)
    index = [None] * 8
    index[6] = unpacked(v_mine, pk_int, 0)
    arc_own = unpacked(v_own, pk, 1)
    own = endpoint(picked(index[6], table_row, 13), arc_own)
    for i, value in enumerate(own["at"] + [own["radius"]] + own["moving"]):
        for d in range(4):
            send_d[d, 2 * i : 2 * i + 2, :] = value[2 * d : 2 * d + 2]
    pl.semaphore_wait(barrier, greetings)
    for o in range(1, n_y):
        pl.semaphore_signal(relay.at[0], inc=1, device_id=plane(o, 0), device_id_type=MESH)

    launch(send_e, recv_e, 0, False)
    launch(send_d, recv_d, 1, True)

    def pair(one, two, live):
        apart = [one["at"][c] - two["at"][c] for c in range(3)]
        spacing = jnp.sqrt(dot3(apart, apart))
        scale = 1.0 / jnp.maximum(spacing, FLOOR_GAP)
        if live is not None:
            scale = scale * live
        normal = [a * scale for a in apart]
        clearance = spacing - one["radius"] - two["radius"]
        if live is not None:
            clearance = clearance * live
        rate = dot3(normal, [one["moving"][c] - two["moving"][c] for c in range(3)])
        slope = clearance * (1.0 / STEP_TIME) + rate
        return dict(normal=normal, slope=slope, down=jnp.maximum(0.0, -slope))

    def split(value):
        pieces = []
        for _ in range(PARTS):
            piece = value.astype(jnp.bfloat16).astype(F32)
            pieces.append(piece)
            value = value - piece
        return pieces

    def set_keys(e):
        key_hi[e] = ((index[e] >> 7) & 7).astype(F32)
        key_lo[e] = (((index[e] >> 10) << 7) | (index[e] & 127)).astype(F32)

    def tall_row(first, second):
        return jnp.concatenate([first, second], axis=0).astype(jnp.bfloat16)

    low = [
        tall_row(row8.astype(F32) + float(k), row8.astype(F32) + float(k + 8)) for k in range(0, 256, 16)
    ]
    high = tall_row(row8.astype(F32), row8.astype(F32))
    one16 = jnp.ones((16, 128), jnp.bfloat16)
    none16 = jnp.zeros((16, 128), jnp.bfloat16)

    def set_push(e, first, normal, arm, amounts):
        sign = 1.0 if first else -1.0
        for i, amount in enumerate(amounts):
            scaled = amount * sign
            for c in range(6):
                value = scaled * (normal[c] if c < 3 else arm[c - 3])
                for p, piece in enumerate(split(value)):
                    push[(i * PARTS + p) * 6 + c, e] = piece

    lanes = [
        tall_row((lane8 + 128 * h).astype(F32), (lane8 + 128 * h).astype(F32)) for h in range(2)
    ]

    def turn_keys():
        for n, (e, s) in enumerate(CHUNKS[:EARLY]):
            key_rows[n : n + 1, :] = key_lo[e, s : s + 1, :]
        key_rows[EARLY:, :] = jnp.zeros((128 - EARLY, 128), F32)
        key_columns[...] = jnp.transpose(key_rows[...])

    def set_columns(n):
        if n < EARLY:
            for k in range(0, 128, 16):
                key = jnp.broadcast_to(key_columns[k : k + 16, n : n + 1], (16, 128)).astype(jnp.bfloat16)
                for h in range(2):
                    o_turned[n, h, k : k + 16, :] = jnp.where(lanes[h] == key, one16, none16)
            return
        e, s = CHUNKS[n]
        key = spread_rows(key_lo, s, e)
        key = tall_row(key, key)
        for k in range(0, 256, 16):
            o_mat[n - EARLY, k : k + 16, :] = jnp.where(low[k // 16] == key, one16, none16)

    def columns_beside(first, last, every):
        for n in range(first, last):
            beside.append(functools.partial(set_columns, n))
            beside.extend([lambda: None] * (every - 1))

    def loads_from(chunk, count):
        e, s = chunk
        key = spread_rows(key_hi, s, e)
        here = high == tall_row(key, key)
        out = []
        for k in range(0, count, 2):
            value = tall_row(spread_rows(push, s, k, e), spread_rows(push, s, k + 1, e))
            out.append(jnp.where(here, value, none16))
        return out

    def accumulate(into, start, rows):
        for n in range(0, len(rows), 2):
            unit = (start + n) // 2 % 2
            stage = (start + n) // 4 % 2
            if start + n < EARLY:
                tile = [
                    jnp.concatenate([o_turned[at, 0], o_turned[at, 1]], axis=1)
                    for at in (start + n, start + n + 1)
                ]
                tile = jnp.concatenate(tile, axis=0)
            else:
                at = start + n - EARLY
                tile = jnp.concatenate([o_mat[at], o_mat[at + 1]], axis=1)
            pltpu.matmul_push_rhs(
                tile, staging_register=stage, mxu_index=unit, transpose=start + n >= EARLY
            )
            left = [jnp.concatenate(r, axis=0) for r in rows[n : n + 2]]
            pltpu.matmul_acc_lhs(into[unit], jnp.concatenate(left, axis=1), load_staged_rhs=stage)

    def total_of(into):
        return pltpu.matmul_pop(into[0]) + pltpu.matmul_pop(into[1])

    def loads_of(total, group):
        out = []
        for c in range(6):
            value = None
            for p in reversed(range(PARTS)):
                at = ((group * PARTS + p) * 6 + c) * 8
                piece = jnp.concatenate([total[at : at + 8, 0:128], total[at : at + 8, 128:256]], axis=0)
                value = piece if value is None else value + piece
            out.append(value)
        return out

    need(8, 9, 10, 11)
    pairs = [None] * 5
    ends = [None] * 8
    for b, start in enumerate(LOCAL_STARTS):
        index[b] = v_lf[start : start + 8, :]
        index[3 + b] = v_ls[start : start + 8, :]
        set_keys(b)
        set_keys(3 + b)
    set_keys(6)
    turn_keys()
    columns_beside(0, EARLY, 2)
    for b, start in enumerate(LOCAL_STARTS):
        ends[b] = endpoint(picked(index[b], table_row, 13), v_a1[start : start + 8, :])
        ends[3 + b] = endpoint(picked(index[3 + b], table_row, 13), v_a2[start : start + 8, :])
        pairs[b] = pair(ends[b], ends[3 + b], None)
    ends[6] = own

    def set_ends(b, one, two, amounts):
        if one is not None:
            set_push(one, True, pairs[b]["normal"], cross3(ends[one]["lever"], pairs[b]["normal"]), amounts)
        if two is not None:
            set_push(two, False, pairs[b]["normal"], cross3(ends[two]["lever"], pairs[b]["normal"]), amounts)

    wide = 12 * PARTS
    narrow = 6 * PARTS
    for b in range(3):
        set_ends(b, b, 3 + b, (pairs[b]["slope"], pairs[b]["down"]))
    both_units = (wide_0, wide_1)
    accumulate(both_units, 0, [loads_from(chunk, wide) for chunk in CHUNKS[:LOCAL_CHUNKS]])

    pl.semaphore_wait(relay.at[0], n_y - 1)
    for o in range(1, n_z):
        pl.semaphore_signal(relay.at[1], inc=1, device_id=plane(0, o), device_id_type=MESH)
    arrive(0)
    arrive(1)

    def repacked(ref, field, slot):
        for d in range(4):
            pk[slot, 2 * d : 2 * d + 2, :] = ref[d, 2 * field : 2 * field + 2, :]
        return pk[slot]

    def by_heading(row_of):
        out = row_of(0)
        for d in range(1, 4):
            out = jnp.where(heading8 == d, row_of(d), out)
        return out

    slot_in = repacked(recv_d, 8, 2).astype(I32)
    arc_in = repacked(recv_d, 9, 3)
    live_in = repacked(recv_d, 10, 4)
    index[7] = lanes_of(by_heading(lambda d: spread_rows(v_exp, d)), slot_in)
    set_keys(7)
    columns_beside(EARLY, len(CHUNKS), 2)
    ends[7] = endpoint(picked(index[7], table_row, 13), arc_in)

    slot_own = unpacked(v_slot, pk_int, 1)
    arc_oth = unpacked(v_oth, pk, 6)
    far = [
        lanes_of(
            by_heading(lambda d, c=c: spread_rows(recv_e, c, d)), slot_own
        )
        for c in range(13)
    ]
    pairs[3] = pair(own, endpoint(far, arc_oth), live_own)
    set_ends(3, 6, None, (pairs[3]["slope"], pairs[3]["down"]))
    near = [repacked(recv_d, i, 7 + i) for i in range(7)]
    pairs[4] = pair(dict(at=near[0:3], radius=near[3], moving=near[4:7]), ends[7], live_in)
    set_ends(4, None, 7, (pairs[4]["slope"], pairs[4]["down"]))

    accumulate(both_units, LOCAL_CHUNKS, [loads_from(chunk, wide) for chunk in CHUNKS[LOCAL_CHUNKS:]])
    total = total_of(both_units)
    both = loads_of(total, 0) + loads_of(total, 1)
    moved_all = mobile(both[0:6])
    moved_down = mobile(both[6:12])
    for c in range(6):
        t_move[c] = moved_down[c]

    def folded(value):
        return jnp.sum(value, axis=0, keepdims=True)

    def halved(row):
        row = row + pltpu.roll(row, 64, 1)
        return row + pltpu.roll(row, 32, 1)

    def counted(name):
        value = pairs[0][name] * pairs[0][name] + pairs[1][name] * pairs[1][name]
        last = pairs[2][name] * pairs[2][name]
        return value + jnp.where(row8 >= 4, last, 0.0) + pairs[3][name] * pairs[3][name]

    def power(one, two):
        value = one[0] * two[0]
        for c in range(1, 6):
            value = value + one[c] * two[c]
        return value

    rows = [
        halved(folded(v))
        for v in (counted("slope"), power(both[0:6], moved_all), counted("down"), power(both[6:12], moved_down))
    ]
    quarter = lax.broadcasted_iota(I32, (1, 128), 1) // 32
    mine = rows[0]
    for i in range(1, 4):
        mine = jnp.where(quarter == i, rows[i], mine)
    sum_a[...] = mine

    def ring(src, dst, sems, slot, to):
        return pltpu.make_async_remote_copy(
            src_ref=src,
            dst_ref=dst.at[slot],
            send_sem=sems[0].at[0],
            recv_sem=sems[1].at[0],
            device_id=to,
            device_id_type=MESH,
        )

    def whole(dst, sems):
        return pltpu.make_async_remote_copy(
            src_ref=dst,
            dst_ref=dst,
            send_sem=sems[0].at[0],
            recv_sem=sems[1].at[0],
            device_id=place(0, 1),
            device_id_type=MESH,
        )

    def hops(offset):
        o, oy, oz = offset
        return min(o, n_gy - o) / 2 + min(oy, n_y - oy) + min(oz, n_z - oz)

    others = [(o, oy, oz) for o in range(n_gy) for oy in range(n_y) for oz in range(n_z)][1:]
    others.sort(key=hops, reverse=True)
    columns = [lax.rem(gy + o, n_gy) for o in range(n_gy)]
    planes = {(oy, oz): plane(oy, oz)[0] for oy in range(n_y) for oz in range(n_z)}
    pl.semaphore_wait(relay.at[1], n_z - 1)
    for slot, (o, oy, oz) in enumerate(others):
        ring(sum_a, got_a, (a_send, a_recv), slot, (planes[oy, oz], columns[o])).start()

    def contact(e):
        values = picked(index[e], move_row, 6)
        turned = cross3(values[3:6], ends[e]["lever"])
        return [values[c] + turned[c] for c in range(3)]

    moved_own = contact(6)
    for c in range(3):
        for d in range(4):
            send_f[d, 2 * c : 2 * c + 2, :] = moved_own[c][2 * d : 2 * d + 2]
    launch(send_f, recv_f, 2, True)
    moved_in = contact(7)
    for c in range(3):
        for d in range(4):
            send_g[d, 2 * c : 2 * c + 2, :] = moved_in[c][2 * d : 2 * d + 2]
    launch(send_g, recv_g, 3, False)

    def curve(b, one, two):
        return dot3(pairs[b]["normal"], [one[c] - two[c] for c in range(3)])

    curved = [None] * 5
    for b in range(3):
        curved[b] = curve(b, contact(b), contact(3 + b))
    arrive(2)
    arrive(3)
    curved[3] = curve(3, moved_own, [repacked(recv_g, c, c) for c in range(3)])
    curved[4] = curve(4, [repacked(recv_f, c, 3 + c) for c in range(3)], moved_in)

    whole(got_a, (a_send, a_recv)).wait_recv()
    parts = [sum_a[...]] + [got_a[slot] for slot in range(len(others))]
    while len(parts) > 1:
        parts = [
            parts[i] + parts[i + 1] if i + 1 < len(parts) else parts[i] for i in range(0, len(parts), 2)
        ]
    mine = parts[0]
    sums = [
        jnp.sum(jnp.where(quarter == i, mine, 0.0), axis=1, keepdims=True) for i in range(4)
    ]
    step_first = sums[0] / (sums[1] + TINY)
    square = step_first * step_first
    step_second = (square * sums[2]) / (square * sums[3] + TINY)
    step_first = jnp.broadcast_to(step_first, (8, 128))
    step_second = jnp.broadcast_to(step_second, (8, 128))

    force = []
    for b in range(5):
        thrust = step_first * pairs[b]["down"]
        slope = pairs[b]["slope"] + step_first * curved[b]
        force.append(jnp.maximum(0.0, thrust - step_second * slope))
    for b, start in enumerate(LOCAL_STARTS):
        o_fl[start : start + 8, :] = force[b]
    for d in range(4):
        for h in range(2):
            o_fc[d : d + 1, h * 128 : (h + 1) * 128] = force[3][2 * d + h : 2 * d + h + 1]
    for b in range(3):
        set_ends(b, b, 3 + b, (force[b],))
    set_ends(3, 6, None, (force[3],))
    set_ends(4, None, 7, (force[4],))
    both_units = (narrow_0, narrow_1)
    accumulate(both_units, 0, [loads_from(chunk, narrow) for chunk in CHUNKS])
    moved = mobile(loads_of(total_of(both_units), 0))
    for c in range(6):
        velocity = t_seg[3 + c] + moved[c]
        for j in range(2):
            turned[j, c * 8 : c * 8 + 8, :] = velocity[j * 8 : j * 8 + 8]
    for r in range(16):
        o_vel[:, r * 128 : (r + 1) * 128] = turned[r // 8, pl.ds(r % 8, 8, stride=8), :][0:6]
    whole(got_a, (a_send, a_recv)).wait_send()
    for to_partner, copies in moves.values():
        for d in range(4):
            pl.when(has_partner[d] if to_partner else has_owner[d])(copies[d].wait_send)


def kernel_with_sums(*refs):
    sums = [pltpu.ACC(unit)((rows * PARTS, 256), F32) for rows in (96, 48) for unit in range(2)]
    pl.run_scoped(functools.partial(kernel, *refs), *sums)


def hand_out(vel, fl, fc, o_vel, o_fl, o_fc, sem):
    copies = [
        pltpu.make_async_copy(src, dst, sem.at[i])
        for i, (src, dst) in enumerate(((vel, o_vel), (fl, o_fl), (fc, o_fc)))
    ]
    for copy in copies:
        copy.start()
    for copy in copies:
        copy.wait()


def grid_y(n_gx):
    return max(k for k in range(1, n_gx + 1) if n_gx % k == 0 and k * k <= n_gx)


def on_device(n_gx, n_gy, cent, tilt, turn, rad, perp, axial, rot, load, lf, ls, a1, a2, mine, slot, own, oth, count, exports):
    segs = [v.reshape(16, 128) for v in (tilt, turn, rad, perp, axial, rot)]
    local = [v.reshape(20, 128) for v in (lf, ls, a1, a2)]
    cross = [v.reshape(4, 256) for v in (mine, slot, own, oth)]
    operands = [cent, *segs, load, *local, *cross, count, exports.reshape(4, 128)]
    anyspace = pl.BlockSpec(memory_space=pltpu.HBM)

    def held(v):
        return pltpu.VMEM(v.shape, v.dtype)

    inputs = [held(v) for v in operands]
    inputs[16] = pltpu.SMEM(count.shape, count.dtype)
    dma = pltpu.SemaphoreType.DMA
    scratch = inputs + [
        pltpu.VMEM((12, 16, 128), F32),
        pltpu.VMEM((6, 16, 128), F32),
        pltpu.VMEM((6, 16, 128), F32),
        pltpu.VMEM((14, 8, 128), F32),
        pltpu.VMEM((2, 8, 128), I32),
        pltpu.VMEM((8, 8, 128), F32),
        pltpu.VMEM((8, 8, 128), F32),
        pltpu.VMEM((12 * PARTS, 8, 8, 128), F32),
        pltpu.VMEM((len(CHUNKS) - EARLY, 256, 128), jnp.bfloat16),
        pltpu.VMEM((EARLY, 2, 128, 128), jnp.bfloat16),
        pltpu.VMEM((128, 128), F32),
        pltpu.VMEM((128, 128), F32),
        pltpu.VMEM((2, 64, 128), F32),
        pltpu.VMEM((4, 24, 128), F32),
        pltpu.VMEM((4, 24, 128), F32),
        pltpu.VMEM((4, 16, 128), F32),
        pltpu.VMEM((4, 16, 128), F32),
        pltpu.VMEM((4, 8, 128), F32),
        pltpu.VMEM((4, 8, 128), F32),
        pltpu.VMEM((4, 8, 128), F32),
        pltpu.VMEM((4, 8, 128), F32),
        pltpu.VMEM((1, 128), F32),
        pltpu.VMEM((n_gx * n_gy - 1, 1, 128), F32),
        dma((18,)),
        dma((4, 4)),
        dma((4, 4)),
        dma((1,)),
        dma((1,)),
        pltpu.SemaphoreType.REGULAR((2,)),
    ]
    operands = [pltpu.with_memory_space_constraint(v, pltpu.HBM) for v in operands]
    outs = ((6, 2048), (20, 128), (4, 256))
    near = pl.BlockSpec(memory_space=pltpu.VMEM)
    solved = pl.pallas_call(
        functools.partial(kernel_with_sums, n_gx, n_gy),
        out_shape=tuple(pltpu.VMEM(shape, F32) for shape in outs),
        in_specs=[anyspace] * 18,
        out_specs=(near,) * 3,
        scratch_shapes=scratch,
        compiler_params=pltpu.CompilerParams(
            collective_id=0, has_side_effects=True, vmem_limit_bytes=48 * 1024 * 1024
        ),
    )(*operands)
    velocity, force_local, force_cross = pl.pallas_call(
        hand_out,
        out_shape=tuple(jax.ShapeDtypeStruct(shape, F32) for shape in outs),
        in_specs=[near] * 3,
        out_specs=(anyspace,) * 3,
        scratch_shapes=[dma((3,))],
        compiler_params=pltpu.CompilerParams(vmem_limit_bytes=1024 * 1024),
    )(*[pltpu.with_memory_space_constraint(v, pltpu.VMEM) for v in solved])
    return velocity, force_local.reshape(2560), force_cross.reshape(1, 4, 256)


def solution(mesh):
    both = ("gx", "gy")
    flat = P(both)
    wide = P(None, both)
    cube = P(both, None, None)
    return jax.shard_map(
        functools.partial(on_device, mesh.shape["gx"], mesh.shape["gy"]),
        mesh=mesh,
        in_specs=(wide, *[flat] * 6, wide, *[flat] * 4, *[cube] * 4, P(both, None), cube),
        out_specs=(wide, flat, cube),
        check_vma=False,
    )
```

```python
import functools

import jax
import jax.numpy as jnp
from jax import lax
from jax.experimental import pallas as pl
from jax.experimental.pallas import tpu as pltpu
from jax.sharding import PartitionSpec as P


F32 = jnp.float32
I32 = jnp.int32
STEP_TIME = 0.5
FLOOR_GAP = 0.25
TINY = 1e-06
PARTS = 2
OFFSETS = ((0, 1), (1, 1), (1, 0), (1, -1))
MESH = pl.DeviceIdType.MESH
LOCAL_STARTS = (0, 8, 12)
CHUNKS = (
    [(0, s) for s in range(8)]
    + [(1, s) for s in range(8)]
    + [(2, s) for s in range(4, 8)]
    + [(3, s) for s in range(8)]
    + [(4, s) for s in range(8)]
    + [(5, s) for s in range(4, 8)]
    + [(6, s) for s in range(8)]
    + [(7, s) for s in range(8)]
)
LOCAL_CHUNKS = 40
EARLY = 48


def cross3(a, b):
    return [a[1] * b[2] - a[2] * b[1], a[2] * b[0] - a[0] * b[2], a[0] * b[1] - a[1] * b[0]]


def dot3(a, b):
    return a[0] * b[0] + a[1] * b[1] + a[2] * b[2]


def lanes_of(table, index):
    return jnp.take_along_axis(table, index, axis=1, mode="promise_in_bounds")


def kernel(
    n_gx,
    n_gy,
    h_cent,
    h_tilt,
    h_turn,
    h_rad,
    h_perp,
    h_axial,
    h_rot,
    h_load,
    h_lf,
    h_ls,
    h_a1,
    h_a2,
    h_mine,
    h_slot,
    h_own,
    h_oth,
    h_count,
    h_exp,
    o_vel,
    o_fl,
    o_fc,
    v_cent,
    v_tilt,
    v_turn,
    v_rad,
    v_perp,
    v_axial,
    v_rot,
    v_load,
    v_lf,
    v_ls,
    v_a1,
    v_a2,
    v_mine,
    v_slot,
    v_own,
    v_oth,
    s_count,
    v_exp,
    t_seg,
    t_move,
    x_seg,
    pk,
    pk_int,
    key_hi,
    key_lo,
    push,
    o_turned,
    key_rows,
    key_columns,
    turned,
    send_d,
    recv_d,
    send_e,
    recv_e,
    send_f,
    recv_f,
    send_g,
    recv_g,
    sum_a,
    got_a,
    in_sem,
    ex_send,
    ex_recv,
    a_send,
    a_recv,
    relay,
    wide_0,
    wide_1,
    narrow_0,
    narrow_1,
):
    gx = lax.axis_index("gx")
    gy = lax.axis_index("gy")

    def place(dx, dy):
        return (lax.rem(gx + (dx + n_gx), n_gx), lax.rem(gy + (dy + n_gy), n_gy))

    n_y = grid_y(n_gx)
    n_z = n_gx // n_y
    at_y, at_z = lax.rem(gx, n_y), gx // n_y

    def plane(oy, oz):
        return (lax.rem(at_z + oz, n_z) * n_y + lax.rem(at_y + oy, n_y), gy)

    def inside(dx, dy):
        row, column = gx + dx, gy + dy
        return (row >= 0) & (row < n_gx) & (column >= 0) & (column < n_gy)

    has_partner = [inside(dx, dy) for dx, dy in OFFSETS]
    has_owner = [inside(-dx, -dy) for dx, dy in OFFSETS]

    barrier = pltpu.get_barrier_semaphore()

    def greet(to):
        pl.semaphore_signal(barrier, inc=1, device_id=to, device_id_type=MESH)

    greetings = (n_gy - 1) + (n_y - 1) + (n_z - 1)
    for d in (1, 3, 2):
        dx, dy = OFFSETS[d]
        pl.when(has_partner[d])(functools.partial(greet, place(dx, dy)))
        pl.when(has_owner[d])(functools.partial(greet, place(-dx, -dy)))
        greetings = greetings + has_partner[d].astype(I32) + has_owner[d].astype(I32)
    for o in range(1, n_gy):
        greet(place(0, o))
    for o in range(1, n_y):
        greet(plane(o, 0))
    for o in range(1, n_z):
        greet(plane(0, o))

    sources = (h_cent, h_tilt, h_turn, h_rad, h_perp, h_axial, h_rot, h_load, h_lf, h_ls, h_a1, h_a2, h_mine, h_slot, h_own, h_oth, h_count, h_exp)
    targets = (v_cent, v_tilt, v_turn, v_rad, v_perp, v_axial, v_rot, v_load, v_lf, v_ls, v_a1, v_a2, v_mine, v_slot, v_own, v_oth, s_count, v_exp)
    loads_in = {}
    for i in (1, 2, 7, 4, 5, 6, 13, 15, 16, 17, 12, 14, 0, 3, 8, 9, 10, 11):
        loads_in[i] = pltpu.make_async_copy(sources[i], targets[i], in_sem.at[i])
        loads_in[i].start()

    def need(*which):
        for i in which:
            loads_in[i].wait()

    row8 = lax.broadcasted_iota(I32, (8, 128), 0)
    lane8 = lax.broadcasted_iota(I32, (8, 128), 1)
    heading8 = row8 // 2
    zero8 = jnp.zeros((8, 128), F32)

    def spread_rows(ref, row, *lead):
        return ref[(*lead, pl.ds(row, 8, stride=0), slice(None))]

    need(1, 2)
    lifted = jnp.sin(v_tilt[...])
    tangent = [lifted * jnp.cos(v_turn[...]), lifted * jnp.sin(v_turn[...]), jnp.cos(v_tilt[...])]
    need(7, 4, 5, 6)
    for c in range(6):
        for r in range(16):
            x_seg[c, r : r + 1, :] = v_load[c : c + 1, r * 128 : (r + 1) * 128]

    def mobile(applied):
        along = dot3(tangent, applied)
        pulled = v_axial[...] * along
        return [v_perp[...] * applied[c] + pulled * tangent[c] for c in range(3)] + [
            v_rot[...] * applied[3 + c] for c in range(3)
        ]

    drift = mobile([x_seg[c] for c in range(6)])
    for c in range(3):
        t_seg[c] = tangent[c]
    for c in range(6):
        t_seg[3 + c] = drift[c]

    def unpacked(ref, into, field):
        for d in range(4):
            for h in range(2):
                into[field, 2 * d + h : 2 * d + h + 1, :] = ref[d : d + 1, h * 128 : (h + 1) * 128]
        return into[field]

    need(13, 15, 16)
    for d in range(4):
        for h in range(2):
            piece = slice(h * 128, (h + 1) * 128)
            send_d[d, 14 + h : 15 + h, :] = v_slot[d : d + 1, piece].astype(F32)
            send_d[d, 16 + h : 17 + h, :] = v_oth[d : d + 1, piece]
    live_own = zero8
    for d in range(4):
        bound = s_count[0, d]
        live_own = jnp.where(
            (heading8 == d) & ((row8 - 2 * d) * 128 + lane8 < bound), 1.0, live_own
        )
    for d in range(4):
        send_d[d, 18:20, :] = live_own[2 * d : 2 * d + 2]

    def blank(refs, d):
        for ref in refs:
            ref[d] = jnp.zeros(ref.shape[1:], F32)

    for d in range(4):
        pl.when(~has_partner[d])(functools.partial(blank, (recv_e, recv_g), d))
        pl.when(~has_owner[d])(functools.partial(blank, (recv_d, recv_f), d))

    partner = [place(dx, dy) for dx, dy in OFFSETS]
    owner = [place(-dx, -dy) for dx, dy in OFFSETS]
    moves = {}

    def launch(src, dst, step, to_partner):
        moves[step] = to_partner, {}
        for d in (1, 3, 2, 0):
            copy = pltpu.make_async_remote_copy(
                src_ref=src.at[d],
                dst_ref=dst.at[d],
                send_sem=ex_send.at[step, d],
                recv_sem=ex_recv.at[step, d],
                device_id=partner[d] if to_partner else owner[d],
                device_id_type=MESH,
            )
            moves[step][1][d] = copy
            pl.when(has_partner[d] if to_partner else has_owner[d])(copy.start)

    def arrive(step):
        to_partner, copies = moves[step]
        for d in range(4):
            pl.when(has_owner[d] if to_partner else has_partner[d])(copies[d].wait_recv)


    need(0, 3)
    for c in range(3):
        for r in range(16):
            t_seg[9 + c, r : r + 1, :] = v_cent[c : c + 1, r * 128 : (r + 1) * 128]

    def table_row(c, r):
        if c < 3:
            return spread_rows(t_seg, r, 9 + c)
        if c == 3:
            return spread_rows(v_rad, r)
        return spread_rows(t_seg, r, c - 4)

    def move_row(c, r):
        return spread_rows(t_move, r, c)

    beside = []

    def picked(index, row_of, count):
        block = index >> 7
        lane = index & 127
        out = [None] * count
        for r in range(16):
            here = block == r
            for c in range(count):
                taken = lanes_of(row_of(c, r), lane)
                out[c] = taken if r == 0 else jnp.where(here, taken, out[c])
            if beside:
                beside.pop(0)()
        return out

    def endpoint(values, arc):
        lever = [arc * values[4 + c] for c in range(3)]
        place_of = [values[c] + lever[c] for c in range(3)]
        turned = cross3(values[10:13], lever)
        moving = [values[7 + c] + turned[c] for c in range(3)]
        return dict(lever=lever, at=place_of, radius=values[3], moving=moving)

    need(17)
    exports = v_exp[...]
    offered = picked(jnp.concatenate([exports, exports], axis=0), table_row, 13)
    for d in range(4):
        for c in range(13):
            send_e[d, c : c + 1, :] = offered[c][d : d + 1]

    need(12, 14)
    index = [None] * 8
    index[6] = unpacked(v_mine, pk_int, 0)
    arc_own = unpacked(v_own, pk, 1)
    own = endpoint(picked(index[6], table_row, 13), arc_own)
    for i, value in enumerate(own["at"] + [own["radius"]] + own["moving"]):
        for d in range(4):
            send_d[d, 2 * i : 2 * i + 2, :] = value[2 * d : 2 * d + 2]
    pl.semaphore_wait(barrier, greetings)
    for o in range(1, n_y):
        pl.semaphore_signal(relay.at[0], inc=1, device_id=plane(o, 0), device_id_type=MESH)

    launch(send_e, recv_e, 0, False)
    launch(send_d, recv_d, 1, True)

    def pair(one, two, live):
        apart = [one["at"][c] - two["at"][c] for c in range(3)]
        spacing = jnp.sqrt(dot3(apart, apart))
        scale = 1.0 / jnp.maximum(spacing, FLOOR_GAP)
        if live is not None:
            scale = scale * live
        normal = [a * scale for a in apart]
        clearance = spacing - one["radius"] - two["radius"]
        if live is not None:
            clearance = clearance * live
        rate = dot3(normal, [one["moving"][c] - two["moving"][c] for c in range(3)])
        slope = clearance * (1.0 / STEP_TIME) + rate
        return dict(normal=normal, slope=slope, down=jnp.maximum(0.0, -slope))

    def split(value):
        pieces = []
        for _ in range(PARTS):
            piece = value.astype(jnp.bfloat16).astype(F32)
            pieces.append(piece)
            value = value - piece
        return pieces

    def set_keys(e):
        key_hi[e] = ((index[e] >> 7) & 7).astype(F32)
        key_lo[e] = (((index[e] >> 10) << 7) | (index[e] & 127)).astype(F32)

    def tall_row(first, second):
        return jnp.concatenate([first, second], axis=0).astype(jnp.bfloat16)

    high = tall_row(row8.astype(F32), row8.astype(F32))
    one16 = jnp.ones((16, 128), jnp.bfloat16)
    none16 = jnp.zeros((16, 128), jnp.bfloat16)

    def set_push(e, first, normal, arm, amounts):
        sign = 1.0 if first else -1.0
        for i, amount in enumerate(amounts):
            scaled = amount * sign
            for c in range(6):
                value = scaled * (normal[c] if c < 3 else arm[c - 3])
                for p, piece in enumerate(split(value)):
                    push[(i * PARTS + p) * 6 + c, e] = piece

    lanes = [
        tall_row((lane8 + 128 * h).astype(F32), (lane8 + 128 * h).astype(F32)) for h in range(2)
    ]

    def turn_keys():
        for n, (e, s) in enumerate(CHUNKS[:EARLY]):
            key_rows[n : n + 1, :] = key_lo[e, s : s + 1, :]
        key_rows[EARLY:, :] = jnp.zeros((128 - EARLY, 128), F32)
        key_columns[0] = jnp.transpose(key_rows[...])

    def turn_late_keys():
        key_columns[1, :, 0:8] = jnp.transpose(key_lo[7])

    def set_columns(n):
        late, at = n // EARLY, n % EARLY
        for k in range(0, 128, 16):
            key = key_columns[late, k : k + 16, at : at + 1]
            key = jnp.broadcast_to(key, (16, 128)).astype(jnp.bfloat16)
            for h in range(2):
                o_turned[n, h, k : k + 16, :] = jnp.where(lanes[h] == key, one16, none16)

    def columns_beside(first, last, every):
        for n in range(first, last):
            beside.append(functools.partial(set_columns, n))
            beside.extend([lambda: None] * (every - 1))

    def loads_from(chunk, count):
        e, s = chunk
        key = spread_rows(key_hi, s, e)
        here = high == tall_row(key, key)
        out = []
        for k in range(0, count, 2):
            value = tall_row(spread_rows(push, s, k, e), spread_rows(push, s, k + 1, e))
            out.append(jnp.where(here, value, none16))
        return out

    slices = len(CHUNKS) // 2

    def push_tile(g):
        n = 2 * g
        tile = [jnp.concatenate([o_turned[at, 0], o_turned[at, 1]], axis=1) for at in (n, n + 1)]
        pltpu.matmul_push_rhs(
            jnp.concatenate(tile, axis=0), staging_register=g // 2 % 2, mxu_index=g % 2
        )

    def first_tiles():
        for g in range(4):
            push_tile(g)

    def accumulate(into, first, rows):
        for i in range(0, len(rows), 2):
            g = first + i // 2
            left = [jnp.concatenate(r, axis=0) for r in rows[i : i + 2]]
            pltpu.matmul_acc_lhs(
                into[g % 2], jnp.concatenate(left, axis=1), load_staged_rhs=g // 2 % 2
            )
            if g + 4 < slices:
                push_tile(g + 4)

    def total_of(into):
        return pltpu.matmul_pop(into[0]) + pltpu.matmul_pop(into[1])

    def loads_of(total, group):
        out = []
        for c in range(6):
            value = None
            for p in reversed(range(PARTS)):
                at = ((group * PARTS + p) * 6 + c) * 8
                piece = jnp.concatenate([total[at : at + 8, 0:128], total[at : at + 8, 128:256]], axis=0)
                value = piece if value is None else value + piece
            out.append(value)
        return out

    need(8, 9, 10, 11)
    pairs = [None] * 5
    ends = [None] * 8
    for b, start in enumerate(LOCAL_STARTS):
        index[b] = v_lf[start : start + 8, :]
        index[3 + b] = v_ls[start : start + 8, :]
        set_keys(b)
        set_keys(3 + b)
    set_keys(6)
    turn_keys()
    columns_beside(0, EARLY, 2)
    for b, start in enumerate(LOCAL_STARTS):
        ends[b] = endpoint(picked(index[b], table_row, 13), v_a1[start : start + 8, :])
        ends[3 + b] = endpoint(picked(index[3 + b], table_row, 13), v_a2[start : start + 8, :])
        pairs[b] = pair(ends[b], ends[3 + b], None)
    ends[6] = own

    def set_ends(b, one, two, amounts):
        if one is not None:
            set_push(one, True, pairs[b]["normal"], cross3(ends[one]["lever"], pairs[b]["normal"]), amounts)
        if two is not None:
            set_push(two, False, pairs[b]["normal"], cross3(ends[two]["lever"], pairs[b]["normal"]), amounts)

    wide = 12 * PARTS
    narrow = 6 * PARTS
    for b in range(3):
        set_ends(b, b, 3 + b, (pairs[b]["slope"], pairs[b]["down"]))
    both_units = (wide_0, wide_1)
    first_tiles()
    accumulate(both_units, 0, [loads_from(chunk, wide) for chunk in CHUNKS[:LOCAL_CHUNKS]])

    pl.semaphore_wait(relay.at[0], n_y - 1)
    for o in range(1, n_z):
        pl.semaphore_signal(relay.at[1], inc=1, device_id=plane(0, o), device_id_type=MESH)
    arrive(0)
    arrive(1)

    def repacked(ref, field, slot):
        for d in range(4):
            pk[slot, 2 * d : 2 * d + 2, :] = ref[d, 2 * field : 2 * field + 2, :]
        return pk[slot]

    def by_heading(row_of):
        out = row_of(0)
        for d in range(1, 4):
            out = jnp.where(heading8 == d, row_of(d), out)
        return out

    slot_in = repacked(recv_d, 7, 2).astype(I32)
    arc_in = repacked(recv_d, 8, 3)
    live_in = repacked(recv_d, 9, 4)
    index[7] = lanes_of(by_heading(lambda d: spread_rows(v_exp, d)), slot_in)
    set_keys(7)
    turn_late_keys()
    columns_beside(EARLY, len(CHUNKS), 2)
    offered_here = [
        lanes_of(by_heading(lambda d, c=c: spread_rows(send_e, c, d)), slot_in) for c in range(13)
    ]
    ends[7] = endpoint(offered_here, arc_in)
    while beside:
        beside.pop(0)()

    slot_own = unpacked(v_slot, pk_int, 1)
    arc_oth = unpacked(v_oth, pk, 6)
    far = [
        lanes_of(
            by_heading(lambda d, c=c: spread_rows(recv_e, c, d)), slot_own
        )
        for c in range(13)
    ]
    pairs[3] = pair(own, endpoint(far, arc_oth), live_own)
    set_ends(3, 6, None, (pairs[3]["slope"], pairs[3]["down"]))
    near = [repacked(recv_d, i, 7 + i) for i in range(7)]
    pairs[4] = pair(dict(at=near[0:3], radius=near[3], moving=near[4:7]), ends[7], live_in)
    set_ends(4, None, 7, (pairs[4]["slope"], pairs[4]["down"]))

    accumulate(both_units, LOCAL_CHUNKS // 2, [loads_from(chunk, wide) for chunk in CHUNKS[LOCAL_CHUNKS:]])
    total = total_of(both_units)
    both = loads_of(total, 0) + loads_of(total, 1)
    moved_all = mobile(both[0:6])
    moved_down = mobile(both[6:12])
    for c in range(6):
        t_move[c] = moved_down[c]

    def folded(value):
        return jnp.sum(value, axis=0, keepdims=True)

    def halved(row):
        row = row + pltpu.roll(row, 64, 1)
        return row + pltpu.roll(row, 32, 1)

    def counted(name):
        value = pairs[0][name] * pairs[0][name] + pairs[1][name] * pairs[1][name]
        last = pairs[2][name] * pairs[2][name]
        return value + jnp.where(row8 >= 4, last, 0.0) + pairs[3][name] * pairs[3][name]

    def power(one, two):
        value = one[0] * two[0]
        for c in range(1, 6):
            value = value + one[c] * two[c]
        return value

    rows = [
        halved(folded(v))
        for v in (counted("slope"), power(both[0:6], moved_all), counted("down"), power(both[6:12], moved_down))
    ]
    quarter = lax.broadcasted_iota(I32, (1, 128), 1) // 32
    mine = rows[0]
    for i in range(1, 4):
        mine = jnp.where(quarter == i, rows[i], mine)
    sum_a[...] = mine

    def ring(src, dst, sems, slot, to):
        return pltpu.make_async_remote_copy(
            src_ref=src,
            dst_ref=dst.at[slot],
            send_sem=sems[0].at[0],
            recv_sem=sems[1].at[0],
            device_id=to,
            device_id_type=MESH,
        )

    def whole(dst, sems):
        return pltpu.make_async_remote_copy(
            src_ref=dst,
            dst_ref=dst,
            send_sem=sems[0].at[0],
            recv_sem=sems[1].at[0],
            device_id=place(0, 1),
            device_id_type=MESH,
        )

    def hops(offset):
        o, oy, oz = offset
        return min(o, n_gy - o) / 2 + min(oy, n_y - oy) + min(oz, n_z - oz)

    others = [(o, oy, oz) for o in range(n_gy) for oy in range(n_y) for oz in range(n_z)][1:]
    others.sort(key=hops, reverse=True)
    columns = [lax.rem(gy + o, n_gy) for o in range(n_gy)]
    planes = {(oy, oz): plane(oy, oz)[0] for oy in range(n_y) for oz in range(n_z)}
    pl.semaphore_wait(relay.at[1], n_z - 1)
    for slot, (o, oy, oz) in enumerate(others):
        ring(sum_a, got_a, (a_send, a_recv), slot, (planes[oy, oz], columns[o])).start()

    def contact(e):
        values = picked(index[e], move_row, 6)
        turned = cross3(values[3:6], ends[e]["lever"])
        return [values[c] + turned[c] for c in range(3)]

    moved_own = contact(6)
    for c in range(3):
        for d in range(4):
            send_f[d, 2 * c : 2 * c + 2, :] = moved_own[c][2 * d : 2 * d + 2]
    launch(send_f, recv_f, 2, True)
    moved_in = contact(7)
    for c in range(3):
        for d in range(4):
            send_g[d, 2 * c : 2 * c + 2, :] = moved_in[c][2 * d : 2 * d + 2]
    launch(send_g, recv_g, 3, False)

    def curve(b, one, two):
        return dot3(pairs[b]["normal"], [one[c] - two[c] for c in range(3)])

    curved = [None] * 5
    for b in range(3):
        curved[b] = curve(b, contact(b), contact(3 + b))
    arrive(2)
    arrive(3)
    curved[3] = curve(3, moved_own, [repacked(recv_g, c, c) for c in range(3)])
    curved[4] = curve(4, [repacked(recv_f, c, 3 + c) for c in range(3)], moved_in)

    first_tiles()
    whole(got_a, (a_send, a_recv)).wait_recv()
    parts = [sum_a[...]] + [got_a[slot] for slot in range(len(others))]
    while len(parts) > 1:
        parts = [
            parts[i] + parts[i + 1] if i + 1 < len(parts) else parts[i] for i in range(0, len(parts), 2)
        ]
    mine = parts[0]
    sums = [
        jnp.sum(jnp.where(quarter == i, mine, 0.0), axis=1, keepdims=True) for i in range(4)
    ]
    step_first = sums[0] / (sums[1] + TINY)
    square = step_first * step_first
    step_second = (square * sums[2]) / (square * sums[3] + TINY)
    step_first = jnp.broadcast_to(step_first, (8, 128))
    step_second = jnp.broadcast_to(step_second, (8, 128))

    force = []
    for b in range(5):
        thrust = step_first * pairs[b]["down"]
        slope = pairs[b]["slope"] + step_first * curved[b]
        force.append(jnp.maximum(0.0, thrust - step_second * slope))
    for b, start in enumerate(LOCAL_STARTS):
        o_fl[start : start + 8, :] = force[b]
    for d in range(4):
        for h in range(2):
            o_fc[d : d + 1, h * 128 : (h + 1) * 128] = force[3][2 * d + h : 2 * d + h + 1]
    for b in range(3):
        set_ends(b, b, 3 + b, (force[b],))
    set_ends(3, 6, None, (force[3],))
    set_ends(4, None, 7, (force[4],))
    both_units = (narrow_0, narrow_1)
    accumulate(both_units, 0, [loads_from(chunk, narrow) for chunk in CHUNKS])
    moved = mobile(loads_of(total_of(both_units), 0))
    for c in range(6):
        velocity = t_seg[3 + c] + moved[c]
        for j in range(2):
            turned[j, c * 8 : c * 8 + 8, :] = velocity[j * 8 : j * 8 + 8]
    for r in range(16):
        o_vel[:, r * 128 : (r + 1) * 128] = turned[r // 8, pl.ds(r % 8, 8, stride=8), :][0:6]
    whole(got_a, (a_send, a_recv)).wait_send()
    for to_partner, copies in moves.values():
        for d in range(4):
            pl.when(has_partner[d] if to_partner else has_owner[d])(copies[d].wait_send)


def kernel_with_sums(*refs):
    sums = [pltpu.ACC(unit)((rows * PARTS, 256), F32) for rows in (96, 48) for unit in range(2)]
    pl.run_scoped(functools.partial(kernel, *refs), *sums)


def hand_out(vel, fl, fc, o_vel, o_fl, o_fc, sem):
    copies = [
        pltpu.make_async_copy(src, dst, sem.at[i])
        for i, (src, dst) in enumerate(((vel, o_vel), (fl, o_fl), (fc, o_fc)))
    ]
    for copy in copies:
        copy.start()
    for copy in copies:
        copy.wait()


def grid_y(n_gx):
    return max(k for k in range(1, n_gx + 1) if n_gx % k == 0 and k * k <= n_gx)


def on_device(n_gx, n_gy, cent, tilt, turn, rad, perp, axial, rot, load, lf, ls, a1, a2, mine, slot, own, oth, count, exports):
    segs = [v.reshape(16, 128) for v in (tilt, turn, rad, perp, axial, rot)]
    local = [v.reshape(20, 128) for v in (lf, ls, a1, a2)]
    cross = [v.reshape(4, 256) for v in (mine, slot, own, oth)]
    operands = [cent, *segs, load, *local, *cross, count, exports.reshape(4, 128)]
    anyspace = pl.BlockSpec(memory_space=pltpu.HBM)

    def held(v):
        return pltpu.VMEM(v.shape, v.dtype)

    inputs = [held(v) for v in operands]
    inputs[16] = pltpu.SMEM(count.shape, count.dtype)
    dma = pltpu.SemaphoreType.DMA
    scratch = inputs + [
        pltpu.VMEM((12, 16, 128), F32),
        pltpu.VMEM((6, 16, 128), F32),
        pltpu.VMEM((6, 16, 128), F32),
        pltpu.VMEM((14, 8, 128), F32),
        pltpu.VMEM((2, 8, 128), I32),
        pltpu.VMEM((8, 8, 128), F32),
        pltpu.VMEM((8, 8, 128), F32),
        pltpu.VMEM((12 * PARTS, 8, 8, 128), F32),
        pltpu.VMEM((len(CHUNKS), 2, 128, 128), jnp.bfloat16),
        pltpu.VMEM((128, 128), F32),
        pltpu.VMEM((2, 128, 128), F32),
        pltpu.VMEM((2, 64, 128), F32),
        pltpu.VMEM((4, 20, 128), F32),
        pltpu.VMEM((4, 20, 128), F32),
        pltpu.VMEM((4, 13, 128), F32),
        pltpu.VMEM((4, 13, 128), F32),
        pltpu.VMEM((4, 6, 128), F32),
        pltpu.VMEM((4, 6, 128), F32),
        pltpu.VMEM((4, 6, 128), F32),
        pltpu.VMEM((4, 6, 128), F32),
        pltpu.VMEM((1, 128), F32),
        pltpu.VMEM((n_gx * n_gy - 1, 1, 128), F32),
        dma((18,)),
        dma((4, 4)),
        dma((4, 4)),
        dma((1,)),
        dma((1,)),
        pltpu.SemaphoreType.REGULAR((2,)),
    ]
    operands = [pltpu.with_memory_space_constraint(v, pltpu.HBM) for v in operands]
    outs = ((6, 2048), (20, 128), (4, 256))
    near = pl.BlockSpec(memory_space=pltpu.VMEM)
    solved = pl.pallas_call(
        functools.partial(kernel_with_sums, n_gx, n_gy),
        out_shape=tuple(pltpu.VMEM(shape, F32) for shape in outs),
        in_specs=[anyspace] * 18,
        out_specs=(near,) * 3,
        scratch_shapes=scratch,
        compiler_params=pltpu.CompilerParams(
            collective_id=0, has_side_effects=True, vmem_limit_bytes=48 * 1024 * 1024
        ),
    )(*operands)
    velocity, force_local, force_cross = pl.pallas_call(
        hand_out,
        out_shape=tuple(jax.ShapeDtypeStruct(shape, F32) for shape in outs),
        in_specs=[near] * 3,
        out_specs=(anyspace,) * 3,
        scratch_shapes=[dma((3,))],
        compiler_params=pltpu.CompilerParams(vmem_limit_bytes=1024 * 1024),
    )(*[pltpu.with_memory_space_constraint(v, pltpu.VMEM) for v in solved])
    return velocity, force_local.reshape(2560), force_cross.reshape(1, 4, 256)


def solution(mesh):
    both = ("gx", "gy")
    flat = P(both)
    wide = P(None, both)
    cube = P(both, None, None)
    return jax.shard_map(
        functools.partial(on_device, mesh.shape["gx"], mesh.shape["gy"]),
        mesh=mesh,
        in_specs=(wide, *[flat] * 6, wide, *[flat] * 4, *[cube] * 4, P(both, None), cube),
        out_specs=(wide, flat, cube),
        check_vma=False,
    )
```

```python
import functools

import jax
import jax.numpy as jnp
from jax import lax
from jax.experimental import pallas as pl
from jax.experimental.pallas import tpu as pltpu
from jax.sharding import PartitionSpec as P


F32 = jnp.float32
I32 = jnp.int32
STEP_TIME = 0.5
FLOOR_GAP = 0.25
TINY = 1e-06
PARTS = 2
OFFSETS = ((0, 1), (1, 1), (1, 0), (1, -1))
MESH = pl.DeviceIdType.MESH
LOCAL_STARTS = (0, 8, 12)
CHUNKS = (
    [(0, s) for s in range(8)]
    + [(1, s) for s in range(8)]
    + [(2, s) for s in range(4, 8)]
    + [(3, s) for s in range(8)]
    + [(4, s) for s in range(8)]
    + [(5, s) for s in range(4, 8)]
    + [(6, s) for s in range(8)]
    + [(7, s) for s in range(8)]
)
LOCAL_CHUNKS = 40
EARLY = 48


def cross3(a, b):
    return [a[1] * b[2] - a[2] * b[1], a[2] * b[0] - a[0] * b[2], a[0] * b[1] - a[1] * b[0]]


def dot3(a, b):
    return a[0] * b[0] + a[1] * b[1] + a[2] * b[2]


def lanes_of(table, index):
    return jnp.take_along_axis(table, index, axis=1, mode="promise_in_bounds")


def kernel(
    n_gx,
    n_gy,
    h_cent,
    h_tilt,
    h_turn,
    h_rad,
    h_perp,
    h_axial,
    h_rot,
    h_load,
    h_lf,
    h_ls,
    h_a1,
    h_a2,
    h_mine,
    h_slot,
    h_own,
    h_oth,
    h_count,
    h_exp,
    o_vel,
    o_fl,
    o_fc,
    v_cent,
    v_tilt,
    v_turn,
    v_rad,
    v_perp,
    v_axial,
    v_rot,
    v_load,
    v_lf,
    v_ls,
    v_a1,
    v_a2,
    v_mine,
    v_slot,
    v_own,
    v_oth,
    s_count,
    v_exp,
    t_seg,
    t_move,
    x_seg,
    pk,
    pk_int,
    key_hi,
    key_lo,
    push,
    o_turned,
    key_rows,
    key_columns,
    turned,
    send_d,
    recv_d,
    send_e,
    recv_e,
    send_f,
    recv_f,
    send_g,
    recv_g,
    sum_a,
    got_a,
    in_sem,
    ex_send,
    ex_recv,
    a_send,
    a_recv,
    relay,
    wide_0,
    wide_1,
    narrow_0,
    narrow_1,
):
    gx = lax.axis_index("gx")
    gy = lax.axis_index("gy")

    def place(dx, dy):
        return (lax.rem(gx + (dx + n_gx), n_gx), lax.rem(gy + (dy + n_gy), n_gy))

    n_y = grid_y(n_gx)
    n_z = n_gx // n_y
    at_y, at_z = lax.rem(gx, n_y), gx // n_y

    def plane(oy, oz):
        return (lax.rem(at_z + oz, n_z) * n_y + lax.rem(at_y + oy, n_y), gy)

    def inside(dx, dy):
        row, column = gx + dx, gy + dy
        return (row >= 0) & (row < n_gx) & (column >= 0) & (column < n_gy)

    has_partner = [inside(dx, dy) for dx, dy in OFFSETS]
    has_owner = [inside(-dx, -dy) for dx, dy in OFFSETS]

    barrier = pltpu.get_barrier_semaphore()

    def greet(to):
        pl.semaphore_signal(barrier, inc=1, device_id=to, device_id_type=MESH)

    greetings = (n_gy - 1) + (n_y - 1) + (n_z - 1)
    for d in (1, 3, 2):
        dx, dy = OFFSETS[d]
        pl.when(has_partner[d])(functools.partial(greet, place(dx, dy)))
        pl.when(has_owner[d])(functools.partial(greet, place(-dx, -dy)))
        greetings = greetings + has_partner[d].astype(I32) + has_owner[d].astype(I32)
    for o in range(1, n_gy):
        greet(place(0, o))
    for o in range(1, n_y):
        greet(plane(o, 0))
    for o in range(1, n_z):
        greet(plane(0, o))

    sources = (h_cent, h_tilt, h_turn, h_rad, h_perp, h_axial, h_rot, h_load, h_lf, h_ls, h_a1, h_a2, h_mine, h_slot, h_own, h_oth, h_count, h_exp)
    targets = (v_cent, v_tilt, v_turn, v_rad, v_perp, v_axial, v_rot, v_load, v_lf, v_ls, v_a1, v_a2, v_mine, v_slot, v_own, v_oth, s_count, v_exp)
    loads_in = {}
    for i in (1, 2, 7, 4, 5, 6, 13, 15, 16, 17, 12, 14, 0, 3, 8, 9, 10, 11):
        loads_in[i] = pltpu.make_async_copy(sources[i], targets[i], in_sem.at[i])
        loads_in[i].start()

    def need(*which):
        for i in which:
            loads_in[i].wait()

    row8 = lax.broadcasted_iota(I32, (8, 128), 0)
    lane8 = lax.broadcasted_iota(I32, (8, 128), 1)
    heading8 = row8 // 2
    zero8 = jnp.zeros((8, 128), F32)

    def spread_rows(ref, row, *lead):
        return ref[(*lead, pl.ds(row, 8, stride=0), slice(None))]

    need(1, 2)
    lifted = jnp.sin(v_tilt[...])
    tangent = [lifted * jnp.cos(v_turn[...]), lifted * jnp.sin(v_turn[...]), jnp.cos(v_tilt[...])]
    need(7, 4, 5, 6)
    for c in range(6):
        for r in range(16):
            x_seg[c, r : r + 1, :] = v_load[c : c + 1, r * 128 : (r + 1) * 128]

    def mobile(applied):
        along = dot3(tangent, applied)
        pulled = v_axial[...] * along
        return [v_perp[...] * applied[c] + pulled * tangent[c] for c in range(3)] + [
            v_rot[...] * applied[3 + c] for c in range(3)
        ]

    drift = mobile([x_seg[c] for c in range(6)])
    for c in range(3):
        t_seg[c] = tangent[c]
    for c in range(6):
        t_seg[3 + c] = drift[c]

    def unpacked(ref, into, field):
        for d in range(4):
            for h in range(2):
                into[field, 2 * d + h : 2 * d + h + 1, :] = ref[d : d + 1, h * 128 : (h + 1) * 128]
        return into[field]

    need(13, 15, 16)
    for d in range(4):
        for h in range(2):
            piece = slice(h * 128, (h + 1) * 128)
            send_d[d, 14 + h : 15 + h, :] = v_slot[d : d + 1, piece].astype(F32)
            send_d[d, 16 + h : 17 + h, :] = v_oth[d : d + 1, piece]
    live_own = zero8
    for d in range(4):
        bound = s_count[0, d]
        live_own = jnp.where(
            (heading8 == d) & ((row8 - 2 * d) * 128 + lane8 < bound), 1.0, live_own
        )
    for d in range(4):
        send_d[d, 18:20, :] = live_own[2 * d : 2 * d + 2]

    def blank(refs, d):
        for ref in refs:
            ref[d] = jnp.zeros(ref.shape[1:], F32)

    for d in range(4):
        pl.when(~has_partner[d])(functools.partial(blank, (recv_e, recv_g), d))
        pl.when(~has_owner[d])(functools.partial(blank, (recv_d, recv_f), d))

    partner = [place(dx, dy) for dx, dy in OFFSETS]
    owner = [place(-dx, -dy) for dx, dy in OFFSETS]
    moves = {}

    def launch(src, dst, step, to_partner):
        moves[step] = to_partner, {}
        for d in (1, 3, 2, 0):
            copy = pltpu.make_async_remote_copy(
                src_ref=src.at[d],
                dst_ref=dst.at[d],
                send_sem=ex_send.at[step, d],
                recv_sem=ex_recv.at[step, d],
                device_id=partner[d] if to_partner else owner[d],
                device_id_type=MESH,
            )
            moves[step][1][d] = copy
            pl.when(has_partner[d] if to_partner else has_owner[d])(copy.start)

    def arrive(step):
        to_partner, copies = moves[step]
        for d in range(4):
            pl.when(has_owner[d] if to_partner else has_partner[d])(copies[d].wait_recv)


    need(0, 3)
    for c in range(3):
        for r in range(16):
            t_seg[9 + c, r : r + 1, :] = v_cent[c : c + 1, r * 128 : (r + 1) * 128]

    def table_row(c, r):
        if c < 3:
            return spread_rows(t_seg, r, 9 + c)
        if c == 3:
            return spread_rows(v_rad, r)
        return spread_rows(t_seg, r, c - 4)

    def move_row(c, r):
        return spread_rows(t_move, r, c)

    beside = []

    def picked(index, row_of, count):
        block = index >> 7
        lane = index & 127
        out = [None] * count
        for r in range(16):
            here = block == r
            for c in range(count):
                taken = lanes_of(row_of(c, r), lane)
                out[c] = taken if r == 0 else jnp.where(here, taken, out[c])
            if beside:
                beside.pop(0)()
        return out

    def endpoint(values, arc):
        lever = [arc * values[4 + c] for c in range(3)]
        place_of = [values[c] + lever[c] for c in range(3)]
        turned = cross3(values[10:13], lever)
        moving = [values[7 + c] + turned[c] for c in range(3)]
        return dict(lever=lever, at=place_of, radius=values[3], moving=moving)

    need(17)
    exports = v_exp[...]
    offered = picked(jnp.concatenate([exports, exports], axis=0), table_row, 13)
    for d in range(4):
        for c in range(13):
            send_e[d, c : c + 1, :] = offered[c][d : d + 1]

    need(12, 14)
    index = [None] * 8
    index[6] = unpacked(v_mine, pk_int, 0)
    arc_own = unpacked(v_own, pk, 1)
    own = endpoint(picked(index[6], table_row, 13), arc_own)
    for i, value in enumerate(own["at"] + [own["radius"]] + own["moving"]):
        for d in range(4):
            send_d[d, 2 * i : 2 * i + 2, :] = value[2 * d : 2 * d + 2]
    pl.semaphore_wait(barrier, greetings)
    for o in range(1, n_y):
        pl.semaphore_signal(relay.at[0], inc=1, device_id=plane(o, 0), device_id_type=MESH)

    launch(send_e, recv_e, 0, False)
    launch(send_d, recv_d, 1, True)

    def pair(one, two, live):
        apart = [one["at"][c] - two["at"][c] for c in range(3)]
        spacing = jnp.sqrt(dot3(apart, apart))
        scale = 1.0 / jnp.maximum(spacing, FLOOR_GAP)
        if live is not None:
            scale = scale * live
        normal = [a * scale for a in apart]
        clearance = spacing - one["radius"] - two["radius"]
        if live is not None:
            clearance = clearance * live
        rate = dot3(normal, [one["moving"][c] - two["moving"][c] for c in range(3)])
        slope = clearance * (1.0 / STEP_TIME) + rate
        return dict(normal=normal, slope=slope, down=jnp.maximum(0.0, -slope))

    def split(value):
        pieces = []
        for _ in range(PARTS):
            piece = value.astype(jnp.bfloat16).astype(F32)
            pieces.append(piece)
            value = value - piece
        return pieces

    def set_keys(e):
        key_hi[e] = ((index[e] >> 7) & 7).astype(F32)
        key_lo[e] = (((index[e] >> 10) << 7) | (index[e] & 127)).astype(F32)

    def tall_row(first, second):
        return jnp.concatenate([first, second], axis=0).astype(jnp.bfloat16)

    high = tall_row(row8.astype(F32), row8.astype(F32))
    one16 = jnp.ones((16, 128), jnp.bfloat16)
    none16 = jnp.zeros((16, 128), jnp.bfloat16)

    def set_push(e, first, normal, arm, amounts):
        sign = 1.0 if first else -1.0
        for i, amount in enumerate(amounts):
            scaled = amount * sign
            for c in range(6):
                value = scaled * (normal[c] if c < 3 else arm[c - 3])
                for p, piece in enumerate(split(value)):
                    push[(i * PARTS + p) * 6 + c, e] = piece

    lanes = [
        tall_row((lane8 + 128 * h).astype(F32), (lane8 + 128 * h).astype(F32)) for h in range(2)
    ]

    def turn_keys():
        for n, (e, s) in enumerate(CHUNKS[:EARLY]):
            key_rows[n : n + 1, :] = key_lo[e, s : s + 1, :]
        key_rows[EARLY:, :] = jnp.zeros((128 - EARLY, 128), F32)
        key_columns[0] = jnp.transpose(key_rows[...])

    def turn_late_keys():
        key_columns[1, :, 0:8] = jnp.transpose(key_lo[7])

    def set_columns(n):
        late, at = n // EARLY, n % EARLY
        for k in range(0, 128, 16):
            key = key_columns[late, k : k + 16, at : at + 1]
            key = jnp.broadcast_to(key, (16, 128)).astype(jnp.bfloat16)
            for h in range(2):
                o_turned[n, h, k : k + 16, :] = jnp.where(lanes[h] == key, one16, none16)

    def columns_beside(first, last, every):
        for n in range(first, last):
            beside.append(functools.partial(set_columns, n))
            beside.extend([lambda: None] * (every - 1))

    def loads_from(chunk, count):
        e, s = chunk
        key = spread_rows(key_hi, s, e)
        here = high == tall_row(key, key)
        out = []
        for k in range(0, count, 2):
            value = tall_row(spread_rows(push, s, k, e), spread_rows(push, s, k + 1, e))
            out.append(jnp.where(here, value, none16))
        return out

    slices = len(CHUNKS) // 2

    def push_tile(g):
        n = 2 * g
        tile = [jnp.concatenate([o_turned[at, 0], o_turned[at, 1]], axis=1) for at in (n, n + 1)]
        pltpu.matmul_push_rhs(
            jnp.concatenate(tile, axis=0), staging_register=g // 2 % 2, mxu_index=g % 2
        )

    def first_tiles():
        for g in range(4):
            push_tile(g)

    def accumulate(into, first, rows):
        for i in range(0, len(rows), 2):
            g = first + i // 2
            left = [jnp.concatenate(r, axis=0) for r in rows[i : i + 2]]
            pltpu.matmul_acc_lhs(
                into[g % 2], jnp.concatenate(left, axis=1), load_staged_rhs=g // 2 % 2
            )
            if g + 4 < slices:
                push_tile(g + 4)

    def total_of(into):
        return pltpu.matmul_pop(into[0]) + pltpu.matmul_pop(into[1])

    def loads_of(total, group):
        out = []
        for c in range(6):
            value = None
            for p in reversed(range(PARTS)):
                at = ((group * PARTS + p) * 6 + c) * 8
                piece = jnp.concatenate([total[at : at + 8, 0:128], total[at : at + 8, 128:256]], axis=0)
                value = piece if value is None else value + piece
            out.append(value)
        return out

    need(8, 9, 10, 11)
    pairs = [None] * 5
    ends = [None] * 8
    for b, start in enumerate(LOCAL_STARTS):
        index[b] = v_lf[start : start + 8, :]
        index[3 + b] = v_ls[start : start + 8, :]
        set_keys(b)
        set_keys(3 + b)
    set_keys(6)
    turn_keys()
    columns_beside(0, EARLY, 2)
    for b, start in enumerate(LOCAL_STARTS):
        ends[b] = endpoint(picked(index[b], table_row, 13), v_a1[start : start + 8, :])
        ends[3 + b] = endpoint(picked(index[3 + b], table_row, 13), v_a2[start : start + 8, :])
        pairs[b] = pair(ends[b], ends[3 + b], None)
    ends[6] = own

    def set_ends(b, one, two, amounts):
        if one is not None:
            set_push(one, True, pairs[b]["normal"], cross3(ends[one]["lever"], pairs[b]["normal"]), amounts)
        if two is not None:
            set_push(two, False, pairs[b]["normal"], cross3(ends[two]["lever"], pairs[b]["normal"]), amounts)

    wide = 12 * PARTS
    narrow = 6 * PARTS
    for b in range(3):
        set_ends(b, b, 3 + b, (pairs[b]["slope"], pairs[b]["down"]))
    both_units = (wide_0, wide_1)
    first_tiles()
    accumulate(both_units, 0, [loads_from(chunk, wide) for chunk in CHUNKS[:LOCAL_CHUNKS]])

    pl.semaphore_wait(relay.at[0], n_y - 1)
    for o in range(1, n_z):
        pl.semaphore_signal(relay.at[1], inc=1, device_id=plane(0, o), device_id_type=MESH)
    arrive(0)
    arrive(1)

    def repacked(ref, field, slot):
        for d in range(4):
            pk[slot, 2 * d : 2 * d + 2, :] = ref[d, 2 * field : 2 * field + 2, :]
        return pk[slot]

    def by_heading(row_of):
        out = row_of(0)
        for d in range(1, 4):
            out = jnp.where(heading8 == d, row_of(d), out)
        return out

    slot_in = repacked(recv_d, 7, 2).astype(I32)
    arc_in = repacked(recv_d, 8, 3)
    live_in = repacked(recv_d, 9, 4)
    index[7] = lanes_of(by_heading(lambda d: spread_rows(v_exp, d)), slot_in)
    set_keys(7)
    turn_late_keys()
    columns_beside(EARLY, len(CHUNKS), 2)
    offered_here = [
        lanes_of(by_heading(lambda d, c=c: spread_rows(send_e, c, d)), slot_in) for c in range(13)
    ]
    ends[7] = endpoint(offered_here, arc_in)
    while beside:
        beside.pop(0)()

    slot_own = unpacked(v_slot, pk_int, 1)
    arc_oth = unpacked(v_oth, pk, 6)
    far = [
        lanes_of(
            by_heading(lambda d, c=c: spread_rows(recv_e, c, d)), slot_own
        )
        for c in range(13)
    ]
    pairs[3] = pair(own, endpoint(far, arc_oth), live_own)
    set_ends(3, 6, None, (pairs[3]["slope"], pairs[3]["down"]))
    near = [repacked(recv_d, i, 7 + i) for i in range(7)]
    pairs[4] = pair(dict(at=near[0:3], radius=near[3], moving=near[4:7]), ends[7], live_in)
    set_ends(4, None, 7, (pairs[4]["slope"], pairs[4]["down"]))

    accumulate(both_units, LOCAL_CHUNKS // 2, [loads_from(chunk, wide) for chunk in CHUNKS[LOCAL_CHUNKS:]])
    total = total_of(both_units)
    both = loads_of(total, 0) + loads_of(total, 1)
    moved_all = mobile(both[0:6])
    moved_down = mobile(both[6:12])
    for c in range(6):
        t_move[c] = moved_down[c]

    def folded(value):
        return jnp.sum(value, axis=0, keepdims=True)

    def halved(row):
        row = row + pltpu.roll(row, 64, 1)
        return row + pltpu.roll(row, 32, 1)

    def counted(name):
        value = pairs[0][name] * pairs[0][name] + pairs[1][name] * pairs[1][name]
        last = pairs[2][name] * pairs[2][name]
        return value + jnp.where(row8 >= 4, last, 0.0) + pairs[3][name] * pairs[3][name]

    def power(one, two):
        value = one[0] * two[0]
        for c in range(1, 6):
            value = value + one[c] * two[c]
        return value

    rows = [
        halved(folded(v))
        for v in (counted("slope"), power(both[0:6], moved_all), counted("down"), power(both[6:12], moved_down))
    ]
    quarter = lax.broadcasted_iota(I32, (1, 128), 1) // 32
    mine = rows[0]
    for i in range(1, 4):
        mine = jnp.where(quarter == i, rows[i], mine)
    sum_a[...] = mine

    def ring(src, dst, sems, slot, to):
        return pltpu.make_async_remote_copy(
            src_ref=src,
            dst_ref=dst.at[slot],
            send_sem=sems[0].at[0],
            recv_sem=sems[1].at[0],
            device_id=to,
            device_id_type=MESH,
        )

    def whole(dst, sems):
        return pltpu.make_async_remote_copy(
            src_ref=dst,
            dst_ref=dst,
            send_sem=sems[0].at[0],
            recv_sem=sems[1].at[0],
            device_id=place(0, 1),
            device_id_type=MESH,
        )

    def hops(offset):
        o, oy, oz = offset
        return (min(o, n_gy - o) + 1) // 2 + min(oy, n_y - oy) + min(oz, n_z - oz)

    others = [(o, oy, oz) for o in range(n_gy) for oy in range(n_y) for oz in range(n_z)][1:]
    others.sort(key=hops, reverse=True)
    columns = [lax.rem(gy + o, n_gy) for o in range(n_gy)]
    planes = {(oy, oz): plane(oy, oz)[0] for oy in range(n_y) for oz in range(n_z)}
    pl.semaphore_wait(relay.at[1], n_z - 1)
    for slot, (o, oy, oz) in enumerate(others):
        ring(sum_a, got_a, (a_send, a_recv), slot, (planes[oy, oz], columns[o])).start()

    def contact(e):
        values = picked(index[e], move_row, 6)
        turned = cross3(values[3:6], ends[e]["lever"])
        return [values[c] + turned[c] for c in range(3)]

    moved_own = contact(6)
    for c in range(3):
        for d in range(4):
            send_f[d, 2 * c : 2 * c + 2, :] = moved_own[c][2 * d : 2 * d + 2]
    launch(send_f, recv_f, 2, True)
    moved_in = contact(7)
    for c in range(3):
        for d in range(4):
            send_g[d, 2 * c : 2 * c + 2, :] = moved_in[c][2 * d : 2 * d + 2]
    launch(send_g, recv_g, 3, False)

    def curve(b, one, two):
        return dot3(pairs[b]["normal"], [one[c] - two[c] for c in range(3)])

    curved = [None] * 5
    for b in range(3):
        curved[b] = curve(b, contact(b), contact(3 + b))
    arrive(2)
    arrive(3)
    curved[3] = curve(3, moved_own, [repacked(recv_g, c, c) for c in range(3)])
    curved[4] = curve(4, [repacked(recv_f, c, 3 + c) for c in range(3)], moved_in)

    first_tiles()
    whole(got_a, (a_send, a_recv)).wait_recv()
    parts = [sum_a[...]] + [got_a[slot] for slot in range(len(others))]
    while len(parts) > 1:
        parts = [
            parts[i] + parts[i + 1] if i + 1 < len(parts) else parts[i] for i in range(0, len(parts), 2)
        ]
    mine = parts[0]
    sums = [
        jnp.sum(jnp.where(quarter == i, mine, 0.0), axis=1, keepdims=True) for i in range(4)
    ]
    step_first = sums[0] / (sums[1] + TINY)
    square = step_first * step_first
    step_second = (square * sums[2]) / (square * sums[3] + TINY)
    step_first = jnp.broadcast_to(step_first, (8, 128))
    step_second = jnp.broadcast_to(step_second, (8, 128))

    force = []
    for b in range(5):
        thrust = step_first * pairs[b]["down"]
        slope = pairs[b]["slope"] + step_first * curved[b]
        force.append(jnp.maximum(0.0, thrust - step_second * slope))
    for b, start in enumerate(LOCAL_STARTS):
        o_fl[start : start + 8, :] = force[b]
    for d in range(4):
        for h in range(2):
            o_fc[d : d + 1, h * 128 : (h + 1) * 128] = force[3][2 * d + h : 2 * d + h + 1]
    for b in range(3):
        set_ends(b, b, 3 + b, (force[b],))
    set_ends(3, 6, None, (force[3],))
    set_ends(4, None, 7, (force[4],))
    both_units = (narrow_0, narrow_1)
    accumulate(both_units, 0, [loads_from(chunk, narrow) for chunk in CHUNKS])
    moved = mobile(loads_of(total_of(both_units), 0))
    for c in range(6):
        velocity = t_seg[3 + c] + moved[c]
        for j in range(2):
            turned[j, c * 8 : c * 8 + 8, :] = velocity[j * 8 : j * 8 + 8]
    for r in range(16):
        o_vel[:, r * 128 : (r + 1) * 128] = turned[r // 8, pl.ds(r % 8, 8, stride=8), :][0:6]
    whole(got_a, (a_send, a_recv)).wait_send()
    for to_partner, copies in moves.values():
        for d in range(4):
            pl.when(has_partner[d] if to_partner else has_owner[d])(copies[d].wait_send)


def kernel_with_sums(*refs):
    sums = [pltpu.ACC(unit)((rows * PARTS, 256), F32) for rows in (96, 48) for unit in range(2)]
    pl.run_scoped(functools.partial(kernel, *refs), *sums)


def hand_out(vel, fl, fc, o_vel, o_fl, o_fc, sem):
    copies = [
        pltpu.make_async_copy(src, dst, sem.at[i])
        for i, (src, dst) in enumerate(((vel, o_vel), (fl, o_fl), (fc, o_fc)))
    ]
    for copy in copies:
        copy.start()
    for copy in copies:
        copy.wait()


def grid_y(n_gx):
    return max(k for k in range(1, n_gx + 1) if n_gx % k == 0 and k * k <= n_gx)


def on_device(n_gx, n_gy, cent, tilt, turn, rad, perp, axial, rot, load, lf, ls, a1, a2, mine, slot, own, oth, count, exports):
    segs = [v.reshape(16, 128) for v in (tilt, turn, rad, perp, axial, rot)]
    local = [v.reshape(20, 128) for v in (lf, ls, a1, a2)]
    cross = [v.reshape(4, 256) for v in (mine, slot, own, oth)]
    operands = [cent, *segs, load, *local, *cross, count, exports.reshape(4, 128)]
    anyspace = pl.BlockSpec(memory_space=pltpu.HBM)

    def held(v):
        return pltpu.VMEM(v.shape, v.dtype)

    inputs = [held(v) for v in operands]
    inputs[16] = pltpu.SMEM(count.shape, count.dtype)
    dma = pltpu.SemaphoreType.DMA
    scratch = inputs + [
        pltpu.VMEM((12, 16, 128), F32),
        pltpu.VMEM((6, 16, 128), F32),
        pltpu.VMEM((6, 16, 128), F32),
        pltpu.VMEM((14, 8, 128), F32),
        pltpu.VMEM((2, 8, 128), I32),
        pltpu.VMEM((8, 8, 128), F32),
        pltpu.VMEM((8, 8, 128), F32),
        pltpu.VMEM((12 * PARTS, 8, 8, 128), F32),
        pltpu.VMEM((len(CHUNKS), 2, 128, 128), jnp.bfloat16),
        pltpu.VMEM((128, 128), F32),
        pltpu.VMEM((2, 128, 128), F32),
        pltpu.VMEM((2, 64, 128), F32),
        pltpu.VMEM((4, 20, 128), F32),
        pltpu.VMEM((4, 20, 128), F32),
        pltpu.VMEM((4, 13, 128), F32),
        pltpu.VMEM((4, 13, 128), F32),
        pltpu.VMEM((4, 6, 128), F32),
        pltpu.VMEM((4, 6, 128), F32),
        pltpu.VMEM((4, 6, 128), F32),
        pltpu.VMEM((4, 6, 128), F32),
        pltpu.VMEM((1, 128), F32),
        pltpu.VMEM((n_gx * n_gy - 1, 1, 128), F32),
        dma((18,)),
        dma((4, 4)),
        dma((4, 4)),
        dma((1,)),
        dma((1,)),
        pltpu.SemaphoreType.REGULAR((2,)),
    ]
    operands = [pltpu.with_memory_space_constraint(v, pltpu.HBM) for v in operands]
    outs = ((6, 2048), (20, 128), (4, 256))
    near = pl.BlockSpec(memory_space=pltpu.VMEM)
    solved = pl.pallas_call(
        functools.partial(kernel_with_sums, n_gx, n_gy),
        out_shape=tuple(pltpu.VMEM(shape, F32) for shape in outs),
        in_specs=[anyspace] * 18,
        out_specs=(near,) * 3,
        scratch_shapes=scratch,
        compiler_params=pltpu.CompilerParams(
            collective_id=0, has_side_effects=True, vmem_limit_bytes=48 * 1024 * 1024
        ),
    )(*operands)
    velocity, force_local, force_cross = pl.pallas_call(
        hand_out,
        out_shape=tuple(jax.ShapeDtypeStruct(shape, F32) for shape in outs),
        in_specs=[near] * 3,
        out_specs=(anyspace,) * 3,
        scratch_shapes=[dma((3,))],
        compiler_params=pltpu.CompilerParams(vmem_limit_bytes=1024 * 1024),
    )(*[pltpu.with_memory_space_constraint(v, pltpu.VMEM) for v in solved])
    return velocity, force_local.reshape(2560), force_cross.reshape(1, 4, 256)


def solution(mesh):
    both = ("gx", "gy")
    flat = P(both)
    wide = P(None, both)
    cube = P(both, None, None)
    return jax.shard_map(
        functools.partial(on_device, mesh.shape["gx"], mesh.shape["gy"]),
        mesh=mesh,
        in_specs=(wide, *[flat] * 6, wide, *[flat] * 4, *[cube] * 4, P(both, None), cube),
        out_specs=(wide, flat, cube),
        check_vma=False,
    )
```
